32 devices in a mesh: rep: 4 (over x, core), shard: 8 (over z, y).
Axes of the slice: x: 2, y: 2, z: 4, core: 2. Of those that a mesh axis runs over, the one named last changes fastest.
Arguments:
- layer_input: bfloat16 [32, 1024, 768], P(('rep', 'shard')), may hold values from -6 to 6
- in_weight: bfloat16 [768, 2304], P('shard'), may hold values from -0.21875 to 0.21875
- query_bias: bfloat16 [768], P('shard'), may hold values from -4 to 4
- value_bias: bfloat16 [768], P('shard'), may hold values from -1.5 to 1.5
- out_weight: bfloat16 [768, 768], P('shard'), may hold values from -0.875 to 0.875
- out_bias: bfloat16 [768], P('shard'), may hold values from -3 to 3
- first_gain: bfloat16 [768], P('shard'), may hold values from 0.5 to 1.5
- first_shift: bfloat16 [768], P('shard'), may hold values from -3 to 3
- inner_weight: bfloat16 [768, 3072], P('shard'), may hold values from -0.21875 to 0.21875
- inner_bias: bfloat16 [3072], P('shard'), may hold values from -4 to 4
- outer_weight: bfloat16 [3072, 768], P('shard'), may hold values from -0.15625 to 0.15625
- outer_bias: bfloat16 [768], P('shard'), may hold values from -3 to 3
- second_gain: bfloat16 [768], P('shard'), may hold values from 0.5 to 1.5
- second_shift: bfloat16 [768], P('shard'), may hold values from -3 to 3
- segment_ids: int32 [32, 1024], P(('rep', 'shard')), may hold values from 0 to 3, never falling along the last dimension, each value on 1 to 512 neighbouring positions
- token_valid: int32 [32, 1024], P(('rep', 'shard')), may hold values from 0 to 1, as said below
- query_perm: int32 [32, 12, 1024], P(('rep', 'shard')), may hold values from 0 to 1023, each once within a row
- key_perm: int32 [32, 12, 1024], P(('rep', 'shard')), may hold values from 0 to 1023, each once within a row
- out_cotangent: bfloat16 [32, 1024, 768], P(('rep', 'shard')), may hold values from -6 to 6
Outputs:
- hidden_out: bfloat16 [32, 1024, 768], P(('rep', 'shard'))
- input_grad: bfloat16 [32, 1024, 768], P(('rep', 'shard'))
- grad_in_weight: float32 [768, 2304], P('shard')
- grad_query_bias: float32 [768], P('shard')
- grad_value_bias: float32 [768], P('shard')
- grad_out_weight: float32 [768, 768], P('shard')
- grad_out_bias: float32 [768], P('shard')
- grad_first_gain: float32 [768], P('shard')
- grad_first_shift: float32 [768], P('shard')
- grad_inner_weight: float32 [768, 3072], P('shard')
- grad_inner_bias: float32 [3072], P('shard')
- grad_outer_weight: float32 [3072, 768], P('shard')
- grad_outer_bias: float32 [768], P('shard')
- grad_second_gain: float32 [768], P('shard')
- grad_second_shift: float32 [768], P('shard')
The draws below stay inside these ranges and needn't reach their ends.
Inputs may be any that keep to these rules, and one draw needn't show every extreme that they name: `token_valid`: in each sequence the real tokens come first and at least one last position is padding (0), at most 128 positions. `segment_ids`: numbers never fall along a sequence. `query_perm`: for each sequence and head, a permutation of the positions. `key_perm`: for each sequence and head, a permutation of the positions.
All inputs are finite; a program needn't handle non-finite values.
Results may differ from the reference program's by a relative error of at most 0.015.
Values may be sent and summed in bfloat16 or wider, within the bound.
A program may use at most 256 MiB of HBM per device.

```python
import math
import jax
import jax.numpy as jnp
import numpy as np
from jax import lax

D = 768
HEADS = 12
HD = 64
FF = 3072
CL = 128
LEN = 1024
SEQS = 32


def draw_token_valid(key, part):
    pad_count = jax.random.randint(key, (SEQS, 1), 1, LEN // 8 + 1)
    places = jnp.arange(LEN, dtype=jnp.int32)[None, :]
    return (places < LEN - pad_count).astype(jnp.int32)


def with_spikes(values, own_key, source, target, parts, factor):
    owner, partner = [(jnp.arange(values.shape[dim]) // (values.shape[dim] // parts)).reshape([-1 if axis == dim else 1 for axis in range(values.ndim)]) for dim in (source, target)]
    chosen = jax.random.permutation(own_key, parts)[partner]
    strong = (owner == chosen) | (owner == (partner + parts // 2) % parts)
    return jnp.where(strong, factor * values, values)


def steps_of(stream_key, shape, shards, low, top_value):
    factor_of = 1.0
    for dim, parts in shards:
        steps = jax.random.uniform(jax.random.fold_in(jax.random.fold_in(stream_key, 6), dim), (parts,), jnp.float32, low / len(shards), top_value / len(shards))
        factor_of = factor_of * jnp.repeat(jnp.exp(steps), shape[dim] // parts).reshape((-1,) + (1,) * (len(shape) - 1 - dim))
    return factor_of


def split_up(count, total, most, skew):
    loads = [(1 << 20) // math.isqrt(rank ** skew) + 1 for rank in range(2, count + 1)]
    surplus, holding = total - most - (count - 1), [1] * (count - 1)
    while surplus > 0:
        free = [i for i in range(count - 1) if holding[i] < most]
        pool, budget = sum([loads[i] for i in free]), surplus
        for i in free:
            extra = min(most - holding[i], max(1, budget * loads[i] // pool), surplus)
            holding[i] = holding[i] + extra
            surplus = surplus - extra
    return np.array([most] + holding)


def ragged(rng, number_of, total, limit, slope):
    if number_of == 2:
        one = jax.random.randint(rng, (), max(1, total - limit), min(limit, total - 1) + 1)
        return jnp.stack([one, total - one])
    tallies = jnp.asarray(split_up(number_of, total, limit, slope), jnp.int32)
    couples = (number_of - 1) // 2
    donor, sink = tallies[1:1 + 2 * couples:2], tallies[2:2 + 2 * couples:2]
    slack = jnp.minimum(donor - 1, limit - sink)
    moved = jax.random.randint(jax.random.fold_in(rng, 1), (couples,), 0, 1 << 20) % (slack + 1)
    tallies = tallies.at[1:1 + 2 * couples:2].set(donor - moved).at[2:2 + 2 * couples:2].set(sink + moved)
    return tallies[jax.random.permutation(jax.random.fold_in(rng, 2), number_of)]


def gaussian(key, shape, deviation, most, cuts=(), held_as=jnp.bfloat16):
    values = deviation * jax.random.normal(key, shape, jnp.float32)
    if cuts:
        values = values * steps_of(key, shape, cuts, -0.22, 0.18)
    return jnp.clip(values, -most, most).astype(held_as)


def bell_draw_with(stream_key, extent, spread, reach, shards, heavy, held_as=jnp.bfloat16):
    values = spread * jax.random.normal(stream_key, extent, jnp.float32)
    if shards:
        values = values * steps_of(stream_key, extent, shards, -0.22, 0.18)
    return jnp.clip(with_spikes(values, jax.random.fold_in(stream_key, 3), *heavy), -reach, reach).astype(held_as)


def setup_inputs(seed: int = 0) -> dict:
    key_of = jax.random.split(jax.random.key(seed), 20)
    layer_input = gaussian(key_of[0], (SEQS, LEN, D), 1.0, 6.0, ((0, 32),))
    in_weight = gaussian(key_of[1], (D, 3 * D), D ** -0.5, 0.21875, ((0, 8),))
    query_bias = gaussian(key_of[2], (D,), 0.3, 4.0, ((0, 8),))
    value_bias = gaussian(key_of[3], (D,), 0.1, 1.5, ((0, 8),))
    out_weight = gaussian(key_of[4], (D, D), (D // 16) ** -0.5, 0.875, ((0, 8),))
    out_bias = gaussian(key_of[5], (D,), 0.2, 3.0, ((0, 8),))
    first_gain = jnp.clip(1.0 + 0.1 * jax.random.normal(key_of[6], (D,), jnp.float32), 0.5, 1.5).astype(jnp.bfloat16)
    first_shift = gaussian(key_of[7], (D,), 0.2, 3.0, ((0, 8),))
    inner_weight = gaussian(key_of[8], (D, FF), D ** -0.5, 0.21875, ((0, 8),))
    inner_bias = gaussian(key_of[9], (FF,), 0.3, 4.0, ((0, 8),))
    outer_weight = gaussian(key_of[10], (FF, D), (FF // 2) ** -0.5, 0.15625, ((0, 8),))
    outer_bias = gaussian(key_of[11], (D,), 0.2, 3.0, ((0, 8),))
    second_gain = jnp.clip(1.0 + 0.1 * jax.random.normal(key_of[12], (D,), jnp.float32), 0.5, 1.5).astype(jnp.bfloat16)
    second_shift = gaussian(key_of[13], (D,), 0.2, 3.0, ((0, 8),))
    segment_ids = jax.vmap(lambda own: jnp.searchsorted(jnp.cumsum(ragged(own, max(3, LEN // 256), LEN, LEN // 2, 0)), jnp.arange(LEN), side="right"))(jax.random.split(key_of[14], SEQS)).reshape((SEQS, LEN)).astype(jnp.int32)
    token_valid = draw_token_valid(jax.random.fold_in(key_of[19], 71), 0)
    query_perm = jax.vmap(lambda own: jax.random.permutation(own, LEN))(jax.random.split(key_of[16], SEQS * HEADS)).reshape((SEQS, HEADS, LEN)).astype(jnp.int32)
    key_perm = jax.vmap(lambda own: jax.random.permutation(own, LEN))(jax.random.split(key_of[17], SEQS * HEADS)).reshape((SEQS, HEADS, LEN)).astype(jnp.int32)
    out_cotangent = bell_draw_with(key_of[18], (SEQS, LEN, D), 1.0, 6.0, ((0, 32),), (0, 2, 32, 2.75))
    return dict(layer_input=layer_input, in_weight=in_weight, query_bias=query_bias, value_bias=value_bias, out_weight=out_weight, out_bias=out_bias, first_gain=first_gain, first_shift=first_shift, inner_weight=inner_weight, inner_bias=inner_bias, outer_weight=outer_weight, outer_bias=outer_bias, second_gain=second_gain, second_shift=second_shift, segment_ids=segment_ids, token_valid=token_valid, query_perm=query_perm, key_perm=key_perm, out_cotangent=out_cotangent)


EPS = 1e-06
HIGH = lax.Precision.HIGHEST

@jax.custom_vjp
def low(v):
    return lax.optimization_barrier(v.astype(jnp.bfloat16)).astype(jnp.float32)

@jax.custom_vjp
def low_back(v):
    return v

def low_keep(v):
    return (low(v), None)

def low_pass(kept, grad):
    return (grad,)

def back_keep(v):
    return (v, None)

def back_low(kept, grad):
    return (low(grad),)
low.defvjp(low_keep, low_pass)
low_back.defvjp(back_keep, back_low)

def norm_rows(resid, gain, shift):
    average = lax.optimization_barrier(jnp.mean(resid, axis=-1, keepdims=True))
    centred = resid - average
    variance = lax.optimization_barrier(jnp.mean(centred * centred, axis=-1, keepdims=True))
    return centred * lax.rsqrt(variance + EPS) * gain + shift

def invert_order(order):

    def single(row_order):
        return jnp.zeros_like(row_order).at[row_order].set(jnp.arange(row_order.shape[0], dtype=jnp.int32))
    return jax.vmap(jax.vmap(single))(order)

def to_heads(tensor):
    return jnp.transpose(tensor.reshape(tensor.shape[0], LEN, HEADS, HD), (0, 2, 1, 3))

def arrange(tensor, order):
    return jnp.take_along_axis(tensor, order[..., None], axis=2)

def in_clusters(tensor):
    return tensor.reshape(tensor.shape[0], HEADS, LEN // CL, CL, tensor.shape[-1])

def attend(query, keys, values, seg_block, ok_block, qp_block, kp_block):
    q_cl = in_clusters(arrange(to_heads(query), qp_block))
    k_cl = in_clusters(arrange(to_heads(keys), kp_block))
    v_cl = in_clusters(arrange(to_heads(values), kp_block))
    seg_heads = jnp.broadcast_to(seg_block[:, None, :], qp_block.shape)
    ok_heads = jnp.broadcast_to(ok_block[:, None, :], qp_block.shape)
    cshape = (qp_block.shape[0], HEADS, LEN // CL, CL)
    seg_query = jnp.take_along_axis(seg_heads, qp_block, axis=2).reshape(cshape)
    seg_key = jnp.take_along_axis(seg_heads, kp_block, axis=2).reshape(cshape)
    ok_query = jnp.take_along_axis(ok_heads, qp_block, axis=2).reshape(cshape)
    ok_key = jnp.take_along_axis(ok_heads, kp_block, axis=2).reshape(cshape)
    visible = (seg_query[..., :, None] == seg_key[..., None, :]) & (ok_query[..., :, None] > 0) & (ok_key[..., None, :] > 0)
    scores = low_back(jnp.einsum('bhcie,bhcje->bhcij', q_cl, k_cl, precision=HIGH) * HD ** (-0.5))
    maxima = lax.optimization_barrier(jnp.max(jnp.where(visible, scores, -1e+30), axis=-1, keepdims=True))
    raised = jnp.where(visible, jnp.exp(jnp.where(visible, scores - maxima, 0.0)), 0.0)
    divisor = jnp.maximum(lax.optimization_barrier(jnp.sum(raised, axis=-1, keepdims=True)), 1.0)
    weights = low(raised / divisor)
    combined = jnp.einsum('bhcij,bhcje->bhcie', weights, v_cl, precision=HIGH)
    combined = combined.reshape(combined.shape[0], HEADS, LEN, HD)
    restored = arrange(combined, invert_order(qp_block))
    return jnp.transpose(restored, (0, 2, 1, 3)).reshape(restored.shape[0], LEN, D)

def layer(x_in, weights, seg_block, ok_block, qp_block, kp_block):
    w_in, b_query, b_value, w_out, b_out, g_first, s_first, w_inner, b_inner, w_outer, b_outer, g_second, s_second = weights
    projected = jnp.einsum('bld,de->ble', x_in, w_in, precision=HIGH)
    query = low(low_back(projected[..., :D] + b_query))
    keys = low(low_back(projected[..., D:2 * D]))
    values = low(low_back(projected[..., 2 * D:] + b_value))
    attended = low(low_back(attend(query, keys, values, seg_block, ok_block, qp_block, kp_block)))
    branch = low_back(jnp.einsum('bld,de->ble', attended, w_out, precision=HIGH) + b_out)
    first_out = norm_rows(x_in + branch, g_first, s_first)
    inner = low_back(jnp.einsum('bld,df->blf', low(first_out), w_inner, precision=HIGH) + b_inner)
    activated = low(jax.nn.gelu(inner, approximate=False))
    outer = low_back(jnp.einsum('blf,fd->bld', activated, w_outer, precision=HIGH) + b_outer)
    return norm_rows(first_out + outer, g_second, s_second)

def reference(layer_input, in_weight, query_bias, value_bias, out_weight, out_bias, first_gain, first_shift, inner_weight, inner_bias, outer_weight, outer_bias, second_gain, second_shift, segment_ids, token_valid, query_perm, key_perm, out_cotangent):
    params = tuple((p.astype(jnp.float32) for p in (in_weight, query_bias, value_bias, out_weight, out_bias, first_gain, first_shift, inner_weight, inner_bias, outer_weight, outer_bias, second_gain, second_shift)))
    per_block = math.gcd(SEQS, 4)
    blocks = SEQS // per_block

    def into_blocks(tensor):
        return tensor.reshape((blocks, per_block) + tensor.shape[1:])
    inputs = (into_blocks(layer_input.astype(jnp.float32)), into_blocks(segment_ids), into_blocks(token_valid), into_blocks(query_perm), into_blocks(key_perm), into_blocks(out_cotangent.astype(jnp.float32)))

    def one_block(totals, pieces):
        x_block, seg_block, ok_block, qp_block, kp_block, cot_block = pieces

        def forward(x_in, *weights):
            return layer(x_in, weights, seg_block, ok_block, qp_block, kp_block)
        output, pullback = jax.vjp(forward, x_block, *params)
        gradients = pullback(cot_block)
        totals = tuple((a + b for a, b in zip(totals, gradients[1:])))
        return (totals, (output.astype(jnp.bfloat16), gradients[0].astype(jnp.bfloat16)))
    initial = tuple((jnp.zeros(p.shape, jnp.float32) for p in params))
    totals, (outputs, in_grads) = lax.scan(one_block, initial, inputs)
    hidden_out = outputs.reshape(SEQS, LEN, D)
    input_grad = in_grads.reshape(SEQS, LEN, D)
    return (hidden_out, input_grad, totals[0], totals[1], totals[2], totals[3], totals[4], totals[5], totals[6], totals[7], totals[8], totals[9], totals[10], totals[11], totals[12])
```

```python
from functools import partial

import jax
import jax.numpy as jnp
from jax import lax
from jax.experimental import pallas as pl
from jax.experimental.pallas import tpu as pltpu
from jax.sharding import PartitionSpec as P

CL = 128
EPS = 1e-06
BIG = 2.0**100
F32 = jnp.float32
BF16 = jnp.bfloat16
NN = (((1,), (0,)), ((), ()))
NT = (((1,), (1,)), ((), ()))
TN = (((0,), (0,)), ((), ()))
TT = (((0,), (1,)), ((), ()))


def mm(a, b, dims):
    return lax.dot_general(a, b, dims, preferred_element_type=F32)


def rows2(value):
    return value.reshape(value.shape[0] * value.shape[1] * value.shape[2], value.shape[3])


def norm_parts(resid):
    average = jnp.mean(resid, axis=-1, keepdims=True)
    centred = resid - average
    variance = jnp.mean(centred * centred, axis=-1, keepdims=True)
    inv_std = lax.rsqrt(variance + EPS)
    return centred * inv_std, inv_std


def norm_back(grad_out, normed, inv_std, gain):
    scaled = grad_out * gain
    first_term = jnp.mean(scaled, axis=-1, keepdims=True)
    second_term = jnp.mean(scaled * normed, axis=-1, keepdims=True)
    return inv_std * (scaled - first_term - normed * second_term)


def gelu_both(z):
    gauss = jnp.exp(-0.5 * (z * z))
    t = 1.0 / (1.0 + (0.3275911 * 0.7071067811865476) * jnp.abs(z))
    poly = t * (0.127414796 + t * (-0.142248368 + t * (0.7107068705 + t * (-0.7265760135 + t * 0.5307027145))))
    tail = poly * gauss
    phi = jnp.where(z >= 0.0, 1.0 - tail, tail)
    return z * phi, phi + z * gauss * 0.3989422804014327


def one_hot(perm_ref, h, pt_ref):
    length = pt_ref.shape[0]
    row = perm_ref[pl.ds(h, 1), :].astype(jnp.int16)
    places = lax.broadcasted_iota(jnp.int16, (length, length), 0)
    pt_ref[...] = jnp.where(places == row, jnp.ones((), BF16), jnp.zeros((), BF16))


def fwd_kernel(
    heads,
    x_hbm, w_in_hbm, w_out_hbm, w_inner_hbm, w_outer_hbm, vec_ref, seg_ref, ok_ref, qperm_ref, kperm_ref, cot_hbm,
    hid_hbm, act_hbm, din_hbm, flow_hbm, dou_hbm, dfi_hbm, dbr_hbm, att_hbm, head_hbm, xt_hbm, vgrad_ref,
    xv, cot, w_in, w_out, w_inner, w_outer, qkv, qcode, kcode, ptq, ptk, att, head, xt,
    act, din, flow, dou, dfi, dbr, hid, gp, fo, nf, ds,
    in_sem, out_sem, head_sem,
):
    length, width = xv.shape
    hd = width // heads
    ff = act.shape[-1]
    tm = act.shape[1]
    fc = width
    n_in = 3 * width

    loads = [
        pltpu.make_async_copy(s, d, in_sem.at[i])
        for i, (s, d) in enumerate(
            ((x_hbm, xv), (w_in_hbm, w_in), (w_out_hbm, w_out), (w_inner_hbm, w_inner), (w_outer_hbm, w_outer), (cot_hbm, cot))
        )
    ]
    for load in loads:
        load.start()
    vec = vec_ref[...].astype(F32)
    vec_t = vec.T

    code_rows = lax.broadcasted_iota(jnp.int32, (16, length), 0)
    seg = seg_ref[...]
    ok = ok_ref[...] > 0
    qcode[...] = jnp.where(code_rows == jnp.where(ok, seg, 4), 1.0, 0.0).astype(BF16)
    kcode[...] = jnp.where((code_rows < 5) & (code_rows != jnp.where(ok, seg, 5)), -BIG, 0.0).astype(BF16)

    loads[0].wait()
    xt[...] = xv[...].T
    loads[1].wait()
    nt = 256
    for i in range(n_in // nt):
        n0 = i * nt
        acc = mm(rows2(w_in[:, :, :, n0 : n0 + nt]), xv[...], TT)
        if n0 < width:
            acc = (acc + vec_t[n0 : n0 + nt, 0:1]).astype(BF16) * 0.125
        elif n0 >= 2 * width:
            acc = acc + vec_t[n0 - 2 * width : n0 - 2 * width + nt, 1:2]
        qkv[n0 : n0 + nt, :] = acc.astype(BF16)

    def attend(h):
        r0 = pl.multiple_of(h * hd, hd)
        rows = pl.ds(r0, hd)
        one_hot(qperm_ref, h, ptq)
        one_hot(kperm_ref, h, ptk)
        q_side = jnp.concatenate([qkv[rows, :], qcode[...]], axis=0)
        k_side = jnp.concatenate(
            [qkv[pl.ds(pl.multiple_of(width + r0, hd), hd), :], kcode[...], qkv[pl.ds(pl.multiple_of(2 * width + r0, hd), hd), :]],
            axis=0,
        )
        q_arr = mm(q_side, ptq[...], NN).astype(BF16)
        k_arr = mm(k_side, ptk[...], NN).astype(BF16)
        v_arr = k_arr[hd + 16 :, :]
        head[h, :hd, :] = q_arr[:hd, :]
        head[h, hd : 2 * hd, :] = k_arr[:hd, :]
        head[h, 2 * hd : 3 * hd, :] = v_arr
        cols = [slice(c * CL, (c + 1) * CL) for c in range(length // CL)]
        scores = jnp.concatenate([mm(k_arr[: hd + 16, c], q_arr[:, c], TN) for c in cols], axis=1)
        top = jnp.maximum(jnp.max(scores, axis=0, keepdims=True), -1e29)
        raised = jnp.exp(scores - top)
        total = jnp.maximum(jnp.sum(raised, axis=0, keepdims=True), 1.0)
        probs = (raised * (1.0 / total)).astype(BF16)
        head[h, 3 * hd :, :] = probs
        combined = jnp.concatenate([mm(v_arr[:, c], probs[:, c], NN) for c in cols], axis=1)
        att[rows, :] = mm(combined.astype(BF16), ptq[...], NT).astype(BF16)

    @pl.loop(0, heads)
    def _(h):
        attend(h)

    heads_out = [
        pltpu.make_async_copy(s, d, head_sem.at[i])
        for i, (s, d) in enumerate(((att, att_hbm), (head, head_hbm), (xt, xt_hbm)))
    ]
    for copy in heads_out:
        copy.start()
    for load in loads[2:]:
        load.wait()

    b_out, g_first, s_first = vec[2:3, :], vec[3:4, :], vec[4:5, :]
    b_outer, g_second, s_second = vec[5:6, :], vec[6:7, :], vec[7:8, :]
    vgrad_ref[...] = jnp.zeros_like(vgrad_ref)

    def add_row(row, value):
        vgrad_ref[row : row + 1, :] += jnp.sum(value, axis=0, keepdims=True)

    def outs(i, slot):
        rows = pl.ds(pl.multiple_of(i * tm, tm), tm)
        return [
            pltpu.make_async_copy(s.at[slot], d.at[rows, :], out_sem.at[slot, n])
            for n, (s, d) in enumerate(
                ((act, act_hbm), (din, din_hbm), (flow, flow_hbm), (dou, dou_hbm), (dfi, dfi_hbm), (dbr, dbr_hbm), (hid, hid_hbm))
            )
        ]

    n_tiles = length // tm

    @pl.loop(0, n_tiles)
    def _(i):
        slot = lax.rem(i, 2)
        t0 = pl.multiple_of(i * tm, tm)
        rows = pl.ds(t0, tm)

        @pl.when(i >= 2)
        def _():
            for copy in outs(i - 2, slot):
                copy.wait()

        branch = mm(att[:, rows], rows2(w_out[...]), TN)
        first_sum = xv[rows, :].astype(F32) + branch + b_out
        normed, inv_first = norm_parts(first_sum)
        nf[...] = normed
        first_out = normed * g_first + s_first
        fo[...] = first_out
        flow[slot] = first_out.astype(BF16)
        outer = None
        for j in range(ff // fc):
            cols = slice(j * fc, (j + 1) * fc)
            inner = mm(flow[slot], rows2(w_inner[:, :, :, cols]), NN) + vec[8 + j : 9 + j, :]
            high, slope = gelu_both(inner)
            act[slot, :, cols] = high.astype(BF16)
            gp[:, cols] = slope
            per = w_outer.shape[0] * fc // ff
            term = mm(act[slot, :, cols], rows2(w_outer[j * per : (j + 1) * per]), NN)
            outer = term if outer is None else outer + term
        normed_second, inv_second = norm_parts(fo[...] + outer + b_outer)
        hid[slot] = (normed_second * g_second + s_second).astype(BF16)
        grad = cot[rows, :].astype(F32)
        d_second = norm_back(grad, normed_second, inv_second, g_second)
        add_row(6, grad * normed_second)
        add_row(7, grad)
        ds[...] = d_second
        low = d_second.astype(BF16)
        dou[slot] = low
        add_row(5, low.astype(F32))
        back = None
        for j in range(ff // fc):
            cols = slice(j * fc, (j + 1) * fc)
            per = w_outer.shape[0] * fc // ff
            d_act = mm(dou[slot], rows2(w_outer[j * per : (j + 1) * per]), NT)
            d_inner = (d_act * gp[:, cols]).astype(BF16)
            din[slot, :, cols] = d_inner
            add_row(8 + j, d_inner.astype(F32))
            term = mm(d_inner, rows2(w_inner[:, :, :, cols]), NT)
            back = term if back is None else back + term
        d_first_out = ds[...] + back
        normed = nf[...]
        add_row(3, d_first_out * normed)
        add_row(4, d_first_out)
        d_first = norm_back(d_first_out, normed, inv_first, g_first)
        dfi[slot] = d_first
        low = d_first.astype(BF16)
        dbr[slot] = low
        add_row(2, low.astype(F32))
        for copy in outs(i, slot):
            copy.start()

    for i in range(max(0, n_tiles - 2), n_tiles):
        for copy in outs(i, i % 2):
            copy.wait()
    for copy in heads_out:
        copy.wait()


def fwd_call(x, w_in, w_out, w_inner, w_outer, vec, seg, ok, qperm, kperm, cot):
    length, width = x.shape
    heads = qperm.shape[0]
    hd = width // heads
    ff = w_inner.shape[-1]
    tm = 256
    hbm = pl.BlockSpec(memory_space=pl.ANY)
    vmem = pl.BlockSpec(memory_space=pltpu.VMEM)
    outs = [
        ((length, width), BF16), ((length, ff), BF16), ((length, ff), BF16), ((length, width), BF16), ((length, width), BF16),
        ((length, width), F32), ((length, width), BF16), ((width, length), BF16), ((heads, 3 * hd + CL, length), BF16),
        ((width, length), BF16), ((16, width), F32),
    ]
    scratch = [
        ((length, width), BF16), ((length, width), BF16), (w_in.shape, BF16), (w_out.shape, BF16), (w_inner.shape, BF16), (w_outer.shape, BF16),
        ((3 * width, length), BF16), ((16, length), BF16), ((16, length), BF16), ((length, length), BF16), ((length, length), BF16),
        ((width, length), BF16), ((heads, 3 * hd + CL, length), BF16), ((width, length), BF16),
        ((2, tm, ff), BF16), ((2, tm, ff), BF16), ((2, tm, width), BF16), ((2, tm, width), BF16), ((2, tm, width), F32), ((2, tm, width), BF16),
        ((2, tm, width), BF16), ((tm, ff), F32), ((tm, width), F32), ((tm, width), F32), ((tm, width), F32),
    ]
    return pl.pallas_call(
        partial(fwd_kernel, heads),
        out_shape=[jax.ShapeDtypeStruct(s, d) for s, d in outs],
        in_specs=[hbm] * 5 + [vmem] * 5 + [hbm],
        out_specs=[hbm] * 10 + [vmem],
        scratch_shapes=[pltpu.VMEM(s, d) for s, d in scratch]
        + [pltpu.SemaphoreType.DMA((6,)), pltpu.SemaphoreType.DMA((2, 7)), pltpu.SemaphoreType.DMA((3,))],
        compiler_params=pltpu.CompilerParams(vmem_limit_bytes=60 << 20),
        name="layer_forward",
    )(x, w_in, w_out, w_inner, w_outer, vec, seg, ok, qperm, kperm, cot)


HG = 4


def bwd_kernel(
    heads,
    act_hbm, din_hbm, flow_hbm, dou_hbm, dfi_hbm, dbr_hbm, att_hbm, head_hbm, xt_hbm, w_in_hbm, w_out_hbm, qperm_ref, kperm_ref, vg_ref,
    ig_hbm, g_in_hbm, g_out_hbm, g_inner_hbm, g_outer_hbm, vgrad_ref,
    act, din, flow, dou, dfi, dbr, att, head, xt, w_in, w_out, ptq, ptk, mixed, dproj, g_in, g_out, g_inner, g_outer, ig,
    in_sem, act_sem, din_sem, head_sem, dfi_sem, out_sem,
):
    length, width = flow.shape
    hd = width // heads
    tm = ig.shape[1]
    fc = act.shape[2]
    ic = din.shape[2]
    copy = pltpu.make_async_copy
    n_act = act_hbm.shape[1] // fc
    n_din = din_hbm.shape[1] // ic
    n_tiles = length // tm
    acts = [copy(act_hbm.at[:, j * fc : (j + 1) * fc], act.at[j % 2], act_sem.at[j % 2]) for j in range(n_act)]
    dins = [copy(din_hbm.at[:, j * ic : (j + 1) * ic], din.at[j % 2], din_sem.at[j % 2]) for j in range(n_din)]
    dfis = [copy(dfi_hbm.at[i * tm : (i + 1) * tm, :], dfi.at[i % 2], dfi_sem.at[i % 2]) for i in range(n_tiles)]
    loads = {
        name: copy(s, d, in_sem.at[i])
        for i, (name, s, d) in enumerate(
            (
                ("dou", dou_hbm, dou), ("flow", flow_hbm, flow), ("dbr", dbr_hbm, dbr), ("w_out", w_out_hbm, w_out),
                ("att", att_hbm, att), ("xt", xt_hbm, xt.at[:width, :]), ("w_in", w_in_hbm, w_in),
            )
        )
    }

    def head_copy(h, slot):
        return copy(head_hbm.at[h], head.at[slot], head_sem.at[slot])

    loads["dou"].start()
    acts[0].start()
    acts[1].start()
    loads["flow"].start()
    dins[0].start()
    dins[1].start()
    for name in ("dbr", "w_out", "att", "xt", "w_in"):
        loads[name].start()
    head_copy(0, 0).start()
    dfis[0].start()
    dfis[1].start()

    loads["dou"].wait()
    for j in range(n_act):
        acts[j].wait()
        part = mm(act[j % 2], dou[...], TN)
        g_outer[j] = part.astype(BF16).reshape(g_outer.shape[1:])
        if j + 2 < n_act:
            acts[j + 2].start()

    loads["flow"].wait()
    mixed[...] = flow[...].T
    for j in range(n_din):
        dins[j].wait()
        part = mm(mixed[...], din[j % 2], NN)
        g_inner[:, :, :, j * ic : (j + 1) * ic] = part.astype(BF16).reshape(g_inner.shape[:3] + (ic,))
        if j + 2 < n_din:
            dins[j + 2].start()

    for name in ("dbr", "w_out", "att"):
        loads[name].wait()
    mixed[...] = mm(rows2(w_out[...]), dbr[...], NT).astype(BF16)
    g_out[...] = mm(att[...], dbr[...], NN).astype(BF16).reshape(g_out.shape)

    cols = [slice(c * CL, (c + 1) * CL) for c in range(length // CL)]

    def attend(h):
        slot = lax.rem(h, 2)
        one_hot(qperm_ref, h, ptq)
        one_hot(kperm_ref, h, ptk)
        r0 = pl.multiple_of(h * hd, hd)
        d_arr = mm(mixed[pl.ds(r0, hd), :], ptq[...], NN).astype(BF16)
        head_copy(h, slot).wait()

        @pl.when(h + 1 < heads)
        def _():
            head_copy(h + 1, 1 - slot).start()

        q_arr = head[slot, :hd, :]
        k_arr = head[slot, hd : 2 * hd, :]
        v_arr = head[slot, 2 * hd : 3 * hd, :]
        probs = head[slot, 3 * hd :, :]
        d_probs = jnp.concatenate([mm(v_arr[:, c], d_arr[:, c], TN) for c in cols], axis=1)
        wide = probs.astype(F32)
        terms = jnp.sum(wide * d_probs, axis=0, keepdims=True)
        d_scores = (wide * (d_probs - terms)).astype(BF16)
        dq = jnp.concatenate([mm(k_arr[:, c], d_scores[:, c], NN) for c in cols], axis=1) * 0.125
        dk = jnp.concatenate([mm(q_arr[:, c], d_scores[:, c], NT) for c in cols], axis=1)
        dv = jnp.concatenate([mm(d_arr[:, c], probs[:, c], NT) for c in cols], axis=1)
        dproj[pl.ds(r0, hd), :] = mm(dq.astype(BF16), ptq[...], NT).astype(BF16)
        dkv = mm(jnp.concatenate([dk, dv], axis=0).astype(BF16), ptk[...], NT).astype(BF16)
        dproj[pl.ds(pl.multiple_of(width + r0, hd), hd), :] = dkv[:hd, :]
        dproj[pl.ds(pl.multiple_of(2 * width + r0, hd), hd), :] = dkv[hd:, :]

    loads["xt"].wait()
    xt[width:, :] = jnp.where(lax.broadcasted_iota(jnp.int32, (16, length), 0) == 0, 1.0, 0.0).astype(BF16)
    vgrad_ref[...] = vg_ref[...]
    gw = HG * hd
    for g in range(heads // HG):
        @pl.loop(g * HG, (g + 1) * HG)
        def _(h):
            attend(h)

        for part in range(3):
            c0 = part * width + g * gw
            prod = mm(xt[...], dproj[c0 : c0 + gw, :], NT)
            g_in[g, :, :, :, part * gw : (part + 1) * gw] = prod[:width].astype(BF16).reshape(g_in.shape[1:4] + (gw,))
            if part != 1:
                vgrad_ref[part // 2 : part // 2 + 1, g * gw : (g + 1) * gw] = prod[width : width + 1]

    outs = [
        copy(s, d, out_sem.at[i])
        for i, (s, d) in enumerate(((g_in, g_in_hbm), (g_out, g_out_hbm), (g_inner, g_inner_hbm), (g_outer, g_outer_hbm)))
    ]
    for out in outs:
        out.start()
    loads["w_in"].wait()
    stores = [copy(ig.at[i % 2], ig_hbm.at[i * tm : (i + 1) * tm, :], out_sem.at[4 + i % 2]) for i in range(n_tiles)]
    for i in range(n_tiles):
        prod = mm(rows2(w_in[...]), dproj[:, i * tm : (i + 1) * tm], NN)
        dfis[i].wait()
        if i >= 2:
            stores[i - 2].wait()
        ig[i % 2] = (dfi[i % 2] + prod.T).astype(BF16)
        stores[i].start()
        if i + 2 < n_tiles:
            dfis[i + 2].start()
    for i in range(max(0, n_tiles - 2), n_tiles):
        stores[i].wait()
    for out in outs:
        out.wait()


def bwd_call(act, din, flow, dou, dfi, dbr, att, head, xt, w_in, w_out, qperm, kperm, vgrad):
    length, width = flow.shape
    heads = qperm.shape[0]
    hd = width // heads
    ff = act.shape[1]
    tm = 256
    hbm = pl.BlockSpec(memory_space=pl.ANY)
    vmem = pl.BlockSpec(memory_space=pltpu.VMEM)
    blocks = w_in.shape[:3]
    gshapes = [(heads // HG,) + blocks + (3 * HG * hd,), blocks + (width,), blocks + (ff,), (8, 2, ff // 16, width)]
    fc = ff // 8
    outs = [((length, width), BF16)] + [(s, BF16) for s in gshapes] + [((16, width), F32)]
    scratch = [
        ((2, length, fc), BF16), ((2, length, width), BF16), ((length, width), BF16), ((length, width), BF16), ((2, tm, width), F32),
        ((length, width), BF16), ((width, length), BF16), ((2,) + head.shape[1:], BF16), ((width + 16, length), BF16), (w_in.shape, BF16), (w_out.shape, BF16),
        ((length, length), BF16), ((length, length), BF16), ((width, length), BF16), ((3 * width, length), BF16),
    ] + [(s, BF16) for s in gshapes] + [((2, tm, width), BF16)]
    return pl.pallas_call(
        partial(bwd_kernel, heads),
        out_shape=[jax.ShapeDtypeStruct(s, d) for s, d in outs],
        in_specs=[hbm] * 11 + [vmem] * 3,
        out_specs=[hbm] * 5 + [vmem],
        scratch_shapes=[pltpu.VMEM(s, d) for s, d in scratch]
        + [pltpu.SemaphoreType.DMA((n,)) for n in (7, 2, 2, 2, 2, 6)],
        compiler_params=pltpu.CompilerParams(vmem_limit_bytes=60 << 20),
        name="layer_backward",
    )(act, din, flow, dou, dfi, dbr, att, head, xt, w_in, w_out, qperm, kperm, vgrad)


def shards(
    layer_input, in_weight, query_bias, value_bias, out_weight, out_bias, first_gain, first_shift, inner_weight, inner_bias,
    outer_weight, outer_bias, second_gain, second_shift, segment_ids, token_valid, query_perm, key_perm, out_cotangent,
):
    _, length, width = layer_input.shape
    heads = query_perm.shape[1]
    ff = inner_weight.shape[1]
    n_shard = lax.axis_size("shard")
    shard = lax.axis_index("shard")

    def whole(rows):
        return lax.all_gather(rows, "shard", axis=0, tiled=True)

    def blocked(rows):
        return rows.reshape(8, 2, rows.shape[0] // 16, rows.shape[1])

    w_in, w_out, w_inner, w_outer = [blocked(whole(w)) for w in (in_weight, out_weight, inner_weight, outer_weight)]
    short = jnp.stack([query_bias, value_bias, out_bias, first_gain, first_shift, outer_bias, second_gain, second_shift])
    vectors = lax.all_gather(jnp.concatenate([short.reshape(-1), inner_bias]), "shard", axis=0)
    piece = width // n_shard
    vec = jnp.concatenate(
        [
            jnp.transpose(vectors[:, : 8 * piece].reshape(n_shard, 8, piece), (1, 0, 2)).reshape(8, width),
            vectors[:, 8 * piece :].reshape(ff // width, width),
            jnp.zeros((8 - ff // width, width), BF16),
        ]
    )
    hidden, act, din, flow, dou, dfi, dbr, att, head, xt, vg = fwd_call(
        layer_input[0], w_in, w_out, w_inner, w_outer, vec, segment_ids, token_valid, query_perm[0], key_perm[0], out_cotangent[0]
    )
    grad_x, g_in, g_out, g_inner, g_outer, vg = bwd_call(
        act, din, flow, dou, dfi, dbr, att, head, xt, w_in, w_out, query_perm[0], key_perm[0], vg
    )
    groups = heads // HG
    g_in = jnp.transpose(g_in.reshape(groups, width, 3, width // groups), (1, 2, 0, 3)).reshape(width, 3 * width)
    grads = [g_in, g_out.reshape(width, width), g_inner.reshape(width, ff), g_outer.reshape(ff, width)]

    def summed(grad):
        rows = lax.psum_scatter(grad.astype(F32), "shard", scatter_dimension=0, tiled=True)
        return lax.psum(rows.astype(BF16), "rep").astype(F32)

    d_in, d_out, d_inner, d_outer = [summed(g) for g in grads]
    vg = lax.psum(vg, ("rep", "shard"))
    mine = lax.dynamic_slice(vg, (0, shard * piece), (8, piece))
    inner_piece = ff // n_shard
    inner_mine = lax.dynamic_slice(vg[8 : 8 + ff // width].reshape(ff), (shard * inner_piece,), (inner_piece,))
    return (
        hidden[None], grad_x[None], d_in, mine[0], mine[1], d_out, mine[2], mine[3], mine[4], d_inner, inner_mine, d_outer,
        mine[5], mine[6], mine[7],
    )


def solution(mesh):
    rows, vector = P("shard", None), P("shard")
    seq2, seq3 = P(("rep", "shard"), None), P(("rep", "shard"), None, None)
    return jax.shard_map(
        shards,
        mesh=mesh,
        in_specs=(
            seq3, rows, vector, vector, rows, vector, vector, vector, rows, vector, rows, vector, vector, vector, seq2, seq2, seq3, seq3, seq3,
        ),
        out_specs=(seq3, seq3, rows, vector, vector, rows, vector, vector, vector, rows, vector, rows, vector, vector, vector),
        check_vma=False,
    )
```

```python
from functools import partial

import jax
import jax.numpy as jnp
from jax import lax
from jax.experimental import pallas as pl
from jax.experimental.pallas import tpu as pltpu
from jax.sharding import PartitionSpec as P

CL = 128
EPS = 1e-06
BIG = 2.0**100
F32 = jnp.float32
BF16 = jnp.bfloat16
NN = (((1,), (0,)), ((), ()))
NT = (((1,), (1,)), ((), ()))
TN = (((0,), (0,)), ((), ()))
TT = (((0,), (1,)), ((), ()))


def mm(a, b, dims):
    return lax.dot_general(a, b, dims, preferred_element_type=F32)


def rows2(value):
    return value.reshape(value.shape[0] * value.shape[1] * value.shape[2], value.shape[3])


def norm_parts(resid):
    average = jnp.mean(resid, axis=-1, keepdims=True)
    centred = resid - average
    variance = jnp.mean(centred * centred, axis=-1, keepdims=True)
    inv_std = lax.rsqrt(variance + EPS)
    return centred * inv_std, inv_std


def norm_back(grad_out, normed, inv_std, gain):
    scaled = grad_out * gain
    first_term = jnp.mean(scaled, axis=-1, keepdims=True)
    second_term = jnp.mean(scaled * normed, axis=-1, keepdims=True)
    return inv_std * (scaled - first_term - normed * second_term)


def gelu_both(z):
    gauss = jnp.exp(-0.5 * (z * z))
    t = 1.0 / (1.0 + (0.3275911 * 0.7071067811865476) * jnp.abs(z))
    poly = t * (0.127414796 + t * (-0.142248368 + t * (0.7107068705 + t * (-0.7265760135 + t * 0.5307027145))))
    tail = poly * gauss
    phi = jnp.where(z >= 0.0, 1.0 - tail, tail)
    return z * phi, phi + z * gauss * 0.3989422804014327


def rcopy(src, dst, send, recv, axis, index):
    return pltpu.make_async_remote_copy(
        src_ref=src, dst_ref=dst, send_sem=send, recv_sem=recv, device_id={axis: index}, device_id_type=pl.DeviceIdType.MESH
    )


class Place:
    def __init__(self):
        rep, shard = lax.axis_index("rep"), lax.axis_index("shard")
        self.x, self.c = rep // 2, rep % 2
        self.z, self.y = shard // 2, shard % 2
        self.rep, self.shard = rep, shard
        self.sibling = self.x * 2 + (1 - self.c)
        self.across = (1 - self.x) * 2 + self.c
        self.beside = self.z * 2 + (1 - self.y)

    def plane(self, dz):
        return (self.z + dz) % 4

    def block(self, dz, dy):
        return self.plane(dz) * 2 + (self.y + dy) % 2


XZ, XY, XX, YZ, YX, YY, CC, OWN, GATHER_SEMS = 0, 4, 8, 16, 20, 24, 28, 36, 37


class Gather:
    def __init__(self, place, source, whole, split, send, recv):
        self.p, self.source, self.whole, self.send, self.recv = place, source, whole, send, recv
        self.half = whole.shape[3] // 2
        start = place.c * self.half
        self.left = pl.ds(pl.multiple_of(start, 128), split)
        self.right = pl.ds(pl.multiple_of(start + split, 128), self.half - split)
        self.mine = pl.ds(pl.multiple_of(start, 128), self.half)
        self.theirs = pl.ds(pl.multiple_of((1 - place.c) * self.half, 128), self.half)
        self.started = []

    def go(self, src, dst, sem, axis, index):
        rcopy(src, dst, self.send.at[sem], self.recv.at[sem], axis, index).start()
        self.started.append((dst.shape, sem))

    def came(self, dst, sem):
        rcopy(dst, dst, self.send.at[sem], self.recv.at[sem], "rep", self.p.sibling).wait_recv()

    def own(self):
        self.own_copy = pltpu.make_async_copy(self.source, self.whole.at[self.p.shard], self.recv.at[OWN])
        self.own_copy.start()

    def stage_z(self):
        p = self.p
        for cols, base in ((self.left, XZ), (self.right, YZ)):
            for dz in (1, 2, 3):
                self.go(
                    self.source.at[p.x, :, cols], self.whole.at[p.shard, p.x, :, cols], base + 4 - dz, "shard", p.plane(dz) * 2 + p.y
                )

    def stage_second(self):
        p = self.p
        own = self.source.at[p.x, :, self.left]
        self.go(own, self.whole.at[p.shard, p.x, :, self.left], XY, "shard", p.beside)
        own = self.source.at[:, :, self.right]
        self.go(own, self.whole.at[p.shard, :, :, self.right], YY, "shard", p.beside)
        for dz in (1, 2, 3):
            spot = self.whole.at[p.block(dz, 0), p.x, :, self.left]
            self.came(spot, XZ + dz)
            self.go(spot, spot, XY + dz, "shard", p.beside)
            self.go(spot, spot, XX + dz, "rep", p.across)
            spot = self.whole.at[p.block(dz, 0), p.x, :, self.right]
            self.came(spot, YZ + dz)
            self.go(spot, spot, YX + dz, "rep", p.across)

    def stage_third(self):
        p = self.p
        for dz in range(4):
            spot = self.whole.at[p.block(dz, 1), p.x, :, self.left]
            self.came(spot, XY + dz)
            self.go(spot, spot, XX + 4 + dz, "rep", p.across)
            if dz:
                self.came(self.whole.at[p.block(dz, 0), 1 - p.x, :, self.right], YX + dz)
                spot = self.whole.at[p.block(dz, 0), :, :, self.right]
                self.go(spot, spot, YY + dz, "shard", p.beside)

    def stage_core(self):
        p = self.p
        for dy in (0, 1):
            for dz in range(4):
                if dy or dz:
                    self.came(self.whole.at[p.block(dz, dy), 1 - p.x, :, self.left], XX + 4 * dy + dz)
                    if dy:
                        self.came(self.whole.at[p.block(dz, 1), :, :, self.right], YY + dz)
                    spot = self.whole.at[p.block(dz, dy), :, :, self.mine]
                    self.go(spot, spot, CC + 4 * dy + dz, "rep", p.sibling)

    def finish(self):
        p = self.p
        self.own_copy.wait()
        for dy in (0, 1):
            for dz in range(4):
                if dy or dz:
                    self.came(self.whole.at[p.block(dz, dy), :, :, self.theirs], CC + 4 * dy + dz)

    def drain(self):
        for shape, sem in self.started:
            spot = self.whole.at[0, 0] if len(shape) == 2 else self.whole.at[0]
            spot = spot.at[..., : shape[-1]]
            rcopy(spot, spot, self.send.at[sem], self.recv.at[sem], "rep", self.p.sibling).wait_send()


def one_hot(perm_ref, h, pt_ref):
    length = pt_ref.shape[0]
    row = perm_ref[pl.ds(h, 1), :].astype(jnp.int16)
    places = lax.broadcasted_iota(jnp.int16, (length, length), 0)
    pt_ref[...] = jnp.where(places == row, jnp.ones((), BF16), jnp.zeros((), BF16))


def fwd_kernel(heads, remote, *refs):
    (x_hbm, w_in_hbm, w_out_hbm, w_inner_hbm, w_outer_hbm, vec_ref, seg_ref, ok_ref, qperm_ref, kperm_ref, cot_hbm), refs = refs[:11], refs[11:]
    (hid_hbm, act_hbm, din_hbm, flow_hbm, dou_hbm, dfi_hbm, dbr_hbm, att_hbm, head_hbm, xt_hbm, vgrad_ref), refs = refs[:11], refs[11:]
    if remote:
        (w_in_whole, w_out_whole), refs = refs[:2], refs[2:]
    (xv, cot, w_in, w_out, w_inner, w_outer, qkv, qcode, kcode, ptq, ptk, att, head, xt), refs = refs[:14], refs[14:]
    (act, din, flow, dou, dfi, dbr, hid, gp, fo, nf, ds, in_sem, out_sem, head_sem), refs = refs[:14], refs[14:]
    length, width = xv.shape
    hd = width // heads
    ff = act.shape[-1]
    tm = act.shape[1]
    fc = width
    n_in = 3 * width

    if remote:
        vslots, send, recv, vsend, vrecv, whole_sem = refs
        p = Place()
        barrier = pltpu.get_barrier_semaphore()
        n_shard = lax.axis_size("shard")
        for d in range(1, n_shard):
            pl.semaphore_signal(barrier, inc=1, device_id={"shard": (p.shard + d) % n_shard}, device_id_type=pl.DeviceIdType.MESH)
        for other in (p.sibling, p.across):
            pl.semaphore_signal(barrier, inc=1, device_id={"rep": other}, device_id_type=pl.DeviceIdType.MESH)
        weights = [
            Gather(p, source, whole, split, send.at[a], recv.at[a])
            for a, (source, whole, split) in enumerate(
                ((w_in_hbm, w_in, 640), (w_out_hbm, w_out, 256), (w_inner_hbm, w_inner, 768), (w_outer_hbm, w_outer, 128))
            )
        ]
        g_in, g_out, g_inner, g_outer = weights
        pl.semaphore_wait(barrier, n_shard + 1)
        g_in.stage_z()
        shorts = [
            rcopy(vec_ref, vslots.at[n_shard - d], vsend.at[n_shard - d], vrecv.at[n_shard - d], "shard", (p.shard + d) % n_shard)
            for d in range(1, n_shard)
        ]
        for copy in shorts:
            copy.start()
        g_out.stage_z()
        loads = [pltpu.make_async_copy(s, d, in_sem.at[i]) for i, (s, d) in enumerate(((x_hbm, xv), (cot_hbm, cot)))]
        loads[0].start()
        for weight in weights:
            weight.own()
        loads[1].start()
    else:
        loads = [
            pltpu.make_async_copy(s, d, in_sem.at[i])
            for i, (s, d) in enumerate(
                ((x_hbm, xv), (w_in_hbm, w_in), (w_out_hbm, w_out), (w_inner_hbm, w_inner), (w_outer_hbm, w_outer), (cot_hbm, cot))
            )
        ]
        for load in loads:
            load.start()

    code_rows = lax.broadcasted_iota(jnp.int32, (16, length), 0)
    seg = seg_ref[...]
    ok = ok_ref[...] > 0
    qcode[...] = jnp.where(code_rows == jnp.where(ok, seg, 4), 1.0, 0.0).astype(BF16)
    kcode[...] = jnp.where((code_rows < 5) & (code_rows != jnp.where(ok, seg, 5)), -BIG, 0.0).astype(BF16)

    loads[0].wait()
    xt[...] = xv[...].T
    if remote:
        g_in.stage_second()
        g_out.stage_second()
        g_in.stage_third()
        g_inner.stage_z()
        g_in.stage_core()
        g_out.stage_third()
        for copy in shorts:
            copy.wait_recv()
        vec = vec_ref[...].astype(F32)
        for d in range(1, n_shard):
            vec = vec + vslots[d].astype(F32)
        g_in.finish()
        whole_in = pltpu.make_async_copy(w_in, w_in_whole, whole_sem.at[0])
        whole_in.start()
    else:
        vec = vec_ref[...].astype(F32)
        loads[1].wait()
    vec_t = vec.T
    nt = 256
    for i in range(n_in // nt):
        n0 = i * nt
        acc = mm(rows2(w_in[:, :, :, n0 : n0 + nt]), xv[...], TT)
        if n0 < width:
            acc = (acc + vec_t[n0 : n0 + nt, 0:1]).astype(BF16) * 0.125
        elif n0 >= 2 * width:
            acc = acc + vec_t[n0 - 2 * width : n0 - 2 * width + nt, 1:2]
        qkv[n0 : n0 + nt, :] = acc.astype(BF16)

    def attend(h):
        r0 = pl.multiple_of(h * hd, hd)
        rows = pl.ds(r0, hd)
        one_hot(qperm_ref, h, ptq)
        one_hot(kperm_ref, h, ptk)
        q_side = jnp.concatenate([qkv[rows, :], qcode[...]], axis=0)
        k_side = jnp.concatenate(
            [qkv[pl.ds(pl.multiple_of(width + r0, hd), hd), :], kcode[...], qkv[pl.ds(pl.multiple_of(2 * width + r0, hd), hd), :]],
            axis=0,
        )
        q_arr = mm(q_side, ptq[...], NN).astype(BF16)
        k_arr = mm(k_side, ptk[...], NN).astype(BF16)
        v_arr = k_arr[hd + 16 :, :]
        head[h, :hd, :] = q_arr[:hd, :]
        head[h, hd : 2 * hd, :] = k_arr[:hd, :]
        head[h, 2 * hd : 3 * hd, :] = v_arr
        cols = [slice(c * CL, (c + 1) * CL) for c in range(length // CL)]
        scores = jnp.concatenate([mm(k_arr[: hd + 16, c], q_arr[:, c], TN) for c in cols], axis=1)
        top = jnp.maximum(jnp.max(scores, axis=0, keepdims=True), -1e29)
        raised = jnp.exp(scores - top)
        total = jnp.maximum(jnp.sum(raised, axis=0, keepdims=True), 1.0)
        probs = (raised * (1.0 / total)).astype(BF16)
        head[h, 3 * hd :, :] = probs
        combined = jnp.concatenate([mm(v_arr[:, c], probs[:, c], NN) for c in cols], axis=1)
        att[rows, :] = mm(combined.astype(BF16), ptq[...], NT).astype(BF16)

    if remote:
        g_out.stage_core()
        g_outer.stage_z()
        g_inner.stage_second()

    @pl.loop(0, heads)
    def _(h):
        attend(h)
        if remote:
            @pl.when(h == heads // 3)
            def _():
                g_inner.stage_third()
                g_outer.stage_second()

            @pl.when(h == 2 * heads // 3)
            def _():
                g_inner.stage_core()
                g_outer.stage_third()

    heads_out = [
        pltpu.make_async_copy(s, d, head_sem.at[i])
        for i, (s, d) in enumerate(((att, att_hbm), (head, head_hbm), (xt, xt_hbm)))
    ]
    for copy in heads_out:
        copy.start()
    if remote:
        g_outer.stage_core()
        loads[1].wait()
        g_out.finish()
        whole_out = pltpu.make_async_copy(w_out, w_out_whole, whole_sem.at[1])
        whole_out.start()
        g_inner.finish()
        g_outer.finish()
    else:
        for load in loads[2:]:
            load.wait()

    b_out, g_first, s_first = vec[2:3, :], vec[3:4, :], vec[4:5, :]
    b_outer, g_second, s_second = vec[5:6, :], vec[6:7, :], vec[7:8, :]
    vgrad_ref[...] = jnp.zeros_like(vgrad_ref)

    def add_row(row, value):
        vgrad_ref[row : row + 1, :] += jnp.sum(value, axis=0, keepdims=True)

    def outs(i, slot):
        rows = pl.ds(pl.multiple_of(i * tm, tm), tm)
        return [
            pltpu.make_async_copy(s.at[slot], d.at[rows, :], out_sem.at[slot, n])
            for n, (s, d) in enumerate(
                ((act, act_hbm), (din, din_hbm), (flow, flow_hbm), (dou, dou_hbm), (dfi, dfi_hbm), (dbr, dbr_hbm), (hid, hid_hbm))
            )
        ]

    n_tiles = length // tm

    @pl.loop(0, n_tiles)
    def _(i):
        slot = lax.rem(i, 2)
        t0 = pl.multiple_of(i * tm, tm)
        rows = pl.ds(t0, tm)

        @pl.when(i >= 2)
        def _():
            for copy in outs(i - 2, slot):
                copy.wait()

        branch = mm(att[:, rows], rows2(w_out[...]), TN)
        first_sum = xv[rows, :].astype(F32) + branch + b_out
        normed, inv_first = norm_parts(first_sum)
        nf[...] = normed
        first_out = normed * g_first + s_first
        fo[...] = first_out
        flow[slot] = first_out.astype(BF16)
        outer = None
        for j in range(ff // fc):
            cols = slice(j * fc, (j + 1) * fc)
            inner = mm(flow[slot], rows2(w_inner[:, :, :, cols]), NN) + vec[8 + j : 9 + j, :]
            high, slope = gelu_both(inner)
            act[slot, :, cols] = high.astype(BF16)
            gp[:, cols] = slope
            per = w_outer.shape[0] * fc // ff
            term = mm(act[slot, :, cols], rows2(w_outer[j * per : (j + 1) * per]), NN)
            outer = term if outer is None else outer + term
        normed_second, inv_second = norm_parts(fo[...] + outer + b_outer)
        hid[slot] = (normed_second * g_second + s_second).astype(BF16)
        grad = cot[rows, :].astype(F32)
        d_second = norm_back(grad, normed_second, inv_second, g_second)
        add_row(6, grad * normed_second)
        add_row(7, grad)
        ds[...] = d_second
        low = d_second.astype(BF16)
        dou[slot] = low
        add_row(5, low.astype(F32))
        back = None
        for j in range(ff // fc):
            cols = slice(j * fc, (j + 1) * fc)
            per = w_outer.shape[0] * fc // ff
            d_act = mm(dou[slot], rows2(w_outer[j * per : (j + 1) * per]), NT)
            d_inner = (d_act * gp[:, cols]).astype(BF16)
            din[slot, :, cols] = d_inner
            add_row(8 + j, d_inner.astype(F32))
            term = mm(d_inner, rows2(w_inner[:, :, :, cols]), NT)
            back = term if back is None else back + term
        d_first_out = ds[...] + back
        normed = nf[...]
        add_row(3, d_first_out * normed)
        add_row(4, d_first_out)
        d_first = norm_back(d_first_out, normed, inv_first, g_first)
        dfi[slot] = d_first
        low = d_first.astype(BF16)
        dbr[slot] = low
        add_row(2, low.astype(F32))
        for copy in outs(i, slot):
            copy.start()

    for i in range(max(0, n_tiles - 2), n_tiles):
        for copy in outs(i, i % 2):
            copy.wait()
    for copy in heads_out:
        copy.wait()
    if remote:
        for weight in weights:
            weight.drain()
        for copy in shorts:
            copy.wait_send()
        whole_in.wait()
        whole_out.wait()


def fwd_call(remote, x, w_in, w_out, w_inner, w_outer, vec, seg, ok, qperm, kperm, cot):
    length, width = x.shape
    heads = qperm.shape[0]
    hd = width // heads
    ff = w_inner.shape[-1]
    wholes = [(8, 2, w.shape[-2], w.shape[-1]) for w in (w_in, w_out, w_inner, w_outer)]
    tm = 256
    hbm = pl.BlockSpec(memory_space=pl.ANY)
    vmem = pl.BlockSpec(memory_space=pltpu.VMEM)
    outs = [
        ((length, width), BF16), ((length, ff), BF16), ((length, ff), BF16), ((length, width), BF16), ((length, width), BF16),
        ((length, width), F32), ((length, width), BF16), ((width, length), BF16), ((heads, 3 * hd + CL, length), BF16),
        ((width, length), BF16), ((16, width), F32),
    ]
    if remote:
        outs += [(wholes[0], BF16), (wholes[1], BF16)]
    scratch = [
        ((length, width), BF16), ((length, width), BF16), *[(whole, BF16) for whole in wholes],
        ((3 * width, length), BF16), ((16, length), BF16), ((16, length), BF16), ((length, length), BF16), ((length, length), BF16),
        ((width, length), BF16), ((heads, 3 * hd + CL, length), BF16), ((width, length), BF16),
        ((2, tm, ff), BF16), ((2, tm, ff), BF16), ((2, tm, width), BF16), ((2, tm, width), BF16), ((2, tm, width), F32), ((2, tm, width), BF16),
        ((2, tm, width), BF16), ((tm, ff), F32), ((tm, width), F32), ((tm, width), F32), ((tm, width), F32),
    ]
    sems = [(6,), (2, 7), (3,)]
    if remote:
        n_shard = lax.axis_size("shard")
        extra = [pltpu.VMEM((n_shard, 16, width), BF16)]
        extra += [pltpu.SemaphoreType.DMA(n) for n in ((4, GATHER_SEMS), (4, GATHER_SEMS), (n_shard,), (n_shard,), (2,))]
    else:
        extra = []
    return pl.pallas_call(
        partial(fwd_kernel, heads, remote),
        out_shape=[jax.ShapeDtypeStruct(s, d) for s, d in outs],
        in_specs=[hbm] * 5 + [vmem] * 5 + [hbm],
        out_specs=[hbm] * 10 + [vmem] + [hbm] * (len(outs) - 11),
        scratch_shapes=[pltpu.VMEM(s, d) for s, d in scratch]
        + [pltpu.SemaphoreType.DMA(n) for n in sems]
        + extra,
        compiler_params=pltpu.CompilerParams(vmem_limit_bytes=60 << 20, collective_id=0 if remote else None, has_side_effects=remote),
        name="layer_forward",
    )(x, w_in, w_out, w_inner, w_outer, vec, seg, ok, qperm, kperm, cot)


HG = 4


def bwd_kernel(
    heads,
    act_hbm, din_hbm, flow_hbm, dou_hbm, dfi_hbm, dbr_hbm, att_hbm, head_hbm, xt_hbm, w_in_hbm, w_out_hbm, qperm_ref, kperm_ref, vg_ref,
    ig_hbm, g_in_hbm, g_out_hbm, g_inner_hbm, g_outer_hbm, vgrad_ref,
    act, din, flow, dou, dfi, dbr, att, head, xt, w_in, w_out, ptq, ptk, mixed, dproj, g_in, g_out, g_inner, g_outer, ig,
    in_sem, act_sem, din_sem, head_sem, dfi_sem, out_sem,
):
    length, width = flow.shape
    hd = width // heads
    tm = ig.shape[1]
    fc = act.shape[2]
    ic = din.shape[2]
    copy = pltpu.make_async_copy
    n_act = act_hbm.shape[1] // fc
    n_din = din_hbm.shape[1] // ic
    n_tiles = length // tm
    acts = [copy(act_hbm.at[:, j * fc : (j + 1) * fc], act.at[j % 2], act_sem.at[j % 2]) for j in range(n_act)]
    dins = [copy(din_hbm.at[:, j * ic : (j + 1) * ic], din.at[j % 2], din_sem.at[j % 2]) for j in range(n_din)]
    dfis = [copy(dfi_hbm.at[i * tm : (i + 1) * tm, :], dfi.at[i % 2], dfi_sem.at[i % 2]) for i in range(n_tiles)]
    loads = {
        name: copy(s, d, in_sem.at[i])
        for i, (name, s, d) in enumerate(
            (
                ("dou", dou_hbm, dou), ("flow", flow_hbm, flow), ("dbr", dbr_hbm, dbr), ("w_out", w_out_hbm, w_out),
                ("att", att_hbm, att), ("xt", xt_hbm, xt.at[:width, :]), ("w_in", w_in_hbm, w_in),
            )
        )
    }

    def head_copy(h, slot):
        return copy(head_hbm.at[h], head.at[slot], head_sem.at[slot])

    loads["dou"].start()
    acts[0].start()
    acts[1].start()
    loads["flow"].start()
    dins[0].start()
    dins[1].start()
    for name in ("dbr", "w_out", "att", "xt", "w_in"):
        loads[name].start()
    head_copy(0, 0).start()
    dfis[0].start()
    dfis[1].start()

    loads["dou"].wait()
    for j in range(n_act):
        acts[j].wait()
        part = mm(act[j % 2], dou[...], TN)
        g_outer[j] = part.astype(BF16).reshape(g_outer.shape[1:])
        if j + 2 < n_act:
            acts[j + 2].start()

    loads["flow"].wait()
    mixed[...] = flow[...].T
    for j in range(n_din):
        dins[j].wait()
        part = mm(mixed[...], din[j % 2], NN)
        g_inner[:, :, :, j * ic : (j + 1) * ic] = part.astype(BF16).reshape(g_inner.shape[:3] + (ic,))
        if j + 2 < n_din:
            dins[j + 2].start()

    for name in ("dbr", "w_out", "att"):
        loads[name].wait()
    mixed[...] = mm(rows2(w_out[...]), dbr[...], NT).astype(BF16)
    g_out[...] = mm(att[...], dbr[...], NN).astype(BF16).reshape(g_out.shape)

    cols = [slice(c * CL, (c + 1) * CL) for c in range(length // CL)]

    def attend(h):
        slot = lax.rem(h, 2)
        one_hot(qperm_ref, h, ptq)
        one_hot(kperm_ref, h, ptk)
        r0 = pl.multiple_of(h * hd, hd)
        d_arr = mm(mixed[pl.ds(r0, hd), :], ptq[...], NN).astype(BF16)
        head_copy(h, slot).wait()

        @pl.when(h + 1 < heads)
        def _():
            head_copy(h + 1, 1 - slot).start()

        q_arr = head[slot, :hd, :]
        k_arr = head[slot, hd : 2 * hd, :]
        v_arr = head[slot, 2 * hd : 3 * hd, :]
        probs = head[slot, 3 * hd :, :]
        d_probs = jnp.concatenate([mm(v_arr[:, c], d_arr[:, c], TN) for c in cols], axis=1)
        wide = probs.astype(F32)
        terms = jnp.sum(wide * d_probs, axis=0, keepdims=True)
        d_scores = (wide * (d_probs - terms)).astype(BF16)
        dq = jnp.concatenate([mm(k_arr[:, c], d_scores[:, c], NN) for c in cols], axis=1) * 0.125
        dk = jnp.concatenate([mm(q_arr[:, c], d_scores[:, c], NT) for c in cols], axis=1)
        dv = jnp.concatenate([mm(d_arr[:, c], probs[:, c], NT) for c in cols], axis=1)
        dproj[pl.ds(r0, hd), :] = mm(dq.astype(BF16), ptq[...], NT).astype(BF16)
        dkv = mm(jnp.concatenate([dk, dv], axis=0).astype(BF16), ptk[...], NT).astype(BF16)
        dproj[pl.ds(pl.multiple_of(width + r0, hd), hd), :] = dkv[:hd, :]
        dproj[pl.ds(pl.multiple_of(2 * width + r0, hd), hd), :] = dkv[hd:, :]

    loads["xt"].wait()
    xt[width:, :] = jnp.where(lax.broadcasted_iota(jnp.int32, (16, length), 0) == 0, 1.0, 0.0).astype(BF16)
    vgrad_ref[...] = vg_ref[...]
    gw = HG * hd
    for g in range(heads // HG):
        @pl.loop(g * HG, (g + 1) * HG)
        def _(h):
            attend(h)

        for part in range(3):
            c0 = part * width + g * gw
            prod = mm(xt[...], dproj[c0 : c0 + gw, :], NT)
            g_in[g, :, :, :, part * gw : (part + 1) * gw] = prod[:width].astype(BF16).reshape(g_in.shape[1:4] + (gw,))
            if part != 1:
                vgrad_ref[part // 2 : part // 2 + 1, g * gw : (g + 1) * gw] = prod[width : width + 1]

    outs = [
        copy(s, d, out_sem.at[i])
        for i, (s, d) in enumerate(((g_in, g_in_hbm), (g_out, g_out_hbm), (g_inner, g_inner_hbm), (g_outer, g_outer_hbm)))
    ]
    for out in outs:
        out.start()
    loads["w_in"].wait()
    stores = [copy(ig.at[i % 2], ig_hbm.at[i * tm : (i + 1) * tm, :], out_sem.at[4 + i % 2]) for i in range(n_tiles)]
    for i in range(n_tiles):
        prod = mm(rows2(w_in[...]), dproj[:, i * tm : (i + 1) * tm], NN)
        dfis[i].wait()
        if i >= 2:
            stores[i - 2].wait()
        ig[i % 2] = (dfi[i % 2] + prod.T).astype(BF16)
        stores[i].start()
        if i + 2 < n_tiles:
            dfis[i + 2].start()
    for i in range(max(0, n_tiles - 2), n_tiles):
        stores[i].wait()
    for out in outs:
        out.wait()


def bwd_call(act, din, flow, dou, dfi, dbr, att, head, xt, w_in, w_out, qperm, kperm, vgrad):
    length, width = flow.shape
    heads = qperm.shape[0]
    hd = width // heads
    ff = act.shape[1]
    tm = 256
    hbm = pl.BlockSpec(memory_space=pl.ANY)
    vmem = pl.BlockSpec(memory_space=pltpu.VMEM)
    blocks = w_in.shape[:3]
    gshapes = [(heads // HG,) + blocks + (3 * HG * hd,), blocks + (width,), blocks + (ff,), (8, 2, ff // 16, width)]
    fc = ff // 8
    outs = [((length, width), BF16)] + [(s, BF16) for s in gshapes] + [((16, width), F32)]
    scratch = [
        ((2, length, fc), BF16), ((2, length, width), BF16), ((length, width), BF16), ((length, width), BF16), ((2, tm, width), F32),
        ((length, width), BF16), ((width, length), BF16), ((2,) + head.shape[1:], BF16), ((width + 16, length), BF16), (w_in.shape, BF16), (w_out.shape, BF16),
        ((length, length), BF16), ((length, length), BF16), ((width, length), BF16), ((3 * width, length), BF16),
    ] + [(s, BF16) for s in gshapes] + [((2, tm, width), BF16)]
    return pl.pallas_call(
        partial(bwd_kernel, heads),
        out_shape=[jax.ShapeDtypeStruct(s, d) for s, d in outs],
        in_specs=[hbm] * 11 + [vmem] * 3,
        out_specs=[hbm] * 5 + [vmem],
        scratch_shapes=[pltpu.VMEM(s, d) for s, d in scratch]
        + [pltpu.SemaphoreType.DMA((n,)) for n in (7, 2, 2, 2, 2, 6)],
        compiler_params=pltpu.CompilerParams(vmem_limit_bytes=60 << 20),
        name="layer_backward",
    )(act, din, flow, dou, dfi, dbr, att, head, xt, w_in, w_out, qperm, kperm, vgrad)


def shards(
    layer_input, in_weight, query_bias, value_bias, out_weight, out_bias, first_gain, first_shift, inner_weight, inner_bias,
    outer_weight, outer_bias, second_gain, second_shift, segment_ids, token_valid, query_perm, key_perm, out_cotangent,
):
    _, length, width = layer_input.shape
    heads = query_perm.shape[1]
    ff = inner_weight.shape[1]
    n_shard = lax.axis_size("shard")
    shard = lax.axis_index("shard")

    piece = width // n_shard
    remote = n_shard == 8 and lax.axis_size("rep") == 4

    def whole(rows):
        return lax.all_gather(rows, "shard", axis=0, tiled=True)

    def blocked(rows):
        return rows.reshape(8, 2, rows.shape[0] // 16, rows.shape[1])

    def halved(rows):
        return rows.reshape(2, rows.shape[0] // 2, rows.shape[1])

    weights = (in_weight, out_weight, inner_weight, outer_weight)
    short = jnp.stack([query_bias, value_bias, out_bias, first_gain, first_shift, outer_bias, second_gain, second_shift])
    inner_piece = ff // n_shard
    if remote:
        w_in, w_out, w_inner, w_outer = [halved(w) for w in weights]
        vec = lax.dynamic_update_slice(jnp.zeros((16, width), BF16), short, (0, shard * piece))
        first = shard * inner_piece
        vec = lax.dynamic_update_slice(vec, inner_bias[None], (8 + first // width, first % width))
    else:
        w_in, w_out, w_inner, w_outer = [blocked(whole(w)) for w in weights]
        vectors = lax.all_gather(jnp.concatenate([short.reshape(-1), inner_bias]), "shard", axis=0)
        vec = jnp.concatenate(
            [
                jnp.transpose(vectors[:, : 8 * piece].reshape(n_shard, 8, piece), (1, 0, 2)).reshape(8, width),
                vectors[:, 8 * piece :].reshape(ff // width, width),
                jnp.zeros((8 - ff // width, width), BF16),
            ]
        )
    hidden, act, din, flow, dou, dfi, dbr, att, head, xt, vg, *wholes = fwd_call(
        remote, layer_input[0], w_in, w_out, w_inner, w_outer, vec, segment_ids, token_valid, query_perm[0], key_perm[0], out_cotangent[0]
    )
    if remote:
        w_in, w_out = wholes
    grad_x, g_in, g_out, g_inner, g_outer, vg = bwd_call(
        act, din, flow, dou, dfi, dbr, att, head, xt, w_in, w_out, query_perm[0], key_perm[0], vg
    )
    groups = heads // HG
    g_in = jnp.transpose(g_in.reshape(groups, width, 3, width // groups), (1, 2, 0, 3)).reshape(width, 3 * width)
    grads = [g_in, g_out.reshape(width, width), g_inner.reshape(width, ff), g_outer.reshape(ff, width)]

    def summed(grad):
        rows = lax.psum_scatter(grad.astype(F32), "shard", scatter_dimension=0, tiled=True)
        return lax.psum(rows.astype(BF16), "rep").astype(F32)

    d_in, d_out, d_inner, d_outer = [summed(g) for g in grads]
    vg = lax.psum(vg, ("rep", "shard"))
    mine = lax.dynamic_slice(vg, (0, shard * piece), (8, piece))
    inner_mine = lax.dynamic_slice(vg[8 : 8 + ff // width].reshape(ff), (shard * inner_piece,), (inner_piece,))
    return (
        hidden[None], grad_x[None], d_in, mine[0], mine[1], d_out, mine[2], mine[3], mine[4], d_inner, inner_mine, d_outer,
        mine[5], mine[6], mine[7],
    )


def solution(mesh):
    rows, vector = P("shard", None), P("shard")
    seq2, seq3 = P(("rep", "shard"), None), P(("rep", "shard"), None, None)
    return jax.shard_map(
        shards,
        mesh=mesh,
        in_specs=(
            seq3, rows, vector, vector, rows, vector, vector, vector, rows, vector, rows, vector, vector, vector, seq2, seq2, seq3, seq3, seq3,
        ),
        out_specs=(seq3, seq3, rows, vector, vector, rows, vector, vector, vector, rows, vector, rows, vector, vector, vector),
        check_vma=False,
    )
```

```python
from functools import partial

import jax
import jax.numpy as jnp
from jax import lax
from jax.experimental import pallas as pl
from jax.experimental.pallas import tpu as pltpu
from jax.sharding import PartitionSpec as P

CL = 128
EPS = 1e-06
BIG = 2.0**100
F32 = jnp.float32
BF16 = jnp.bfloat16
NN = (((1,), (0,)), ((), ()))
NT = (((1,), (1,)), ((), ()))
TN = (((0,), (0,)), ((), ()))
TT = (((0,), (1,)), ((), ()))


def mm(a, b, dims):
    return lax.dot_general(a, b, dims, preferred_element_type=F32)


def rows2(value):
    return value.reshape(value.shape[0] * value.shape[1] * value.shape[2], value.shape[3])


def norm_parts(resid):
    average = jnp.mean(resid, axis=-1, keepdims=True)
    centred = resid - average
    variance = jnp.mean(centred * centred, axis=-1, keepdims=True)
    inv_std = lax.rsqrt(variance + EPS)
    return centred * inv_std, inv_std


def norm_back(grad_out, normed, inv_std, gain):
    scaled = grad_out * gain
    first_term = jnp.mean(scaled, axis=-1, keepdims=True)
    second_term = jnp.mean(scaled * normed, axis=-1, keepdims=True)
    return inv_std * (scaled - first_term - normed * second_term)


def gelu_both(z):
    gauss = jnp.exp(-0.5 * (z * z))
    t = 1.0 / (1.0 + (0.3275911 * 0.7071067811865476) * jnp.abs(z))
    poly = t * (0.127414796 + t * (-0.142248368 + t * (0.7107068705 + t * (-0.7265760135 + t * 0.5307027145))))
    tail = poly * gauss
    phi = jnp.where(z >= 0.0, 1.0 - tail, tail)
    return z * phi, phi + z * gauss * 0.3989422804014327


def rcopy(src, dst, send, recv, axis, index):
    return pltpu.make_async_remote_copy(
        src_ref=src, dst_ref=dst, send_sem=send, recv_sem=recv, device_id={axis: index}, device_id_type=pl.DeviceIdType.MESH
    )


class Place:
    def __init__(self):
        rep, shard = lax.axis_index("rep"), lax.axis_index("shard")
        self.x, self.c = rep // 2, rep % 2
        self.z, self.y = shard // 2, shard % 2
        self.rep, self.shard = rep, shard
        self.sibling = self.x * 2 + (1 - self.c)
        self.across = (1 - self.x) * 2 + self.c
        self.beside = self.z * 2 + (1 - self.y)

    def plane(self, dz):
        return (self.z + dz) % 4

    def block(self, dz, dy):
        return self.plane(dz) * 2 + (self.y + dy) % 2


XZ, XY, XX, YZ, YX, YY, CC, OWN, GATHER_SEMS = 0, 4, 8, 16, 20, 24, 28, 36, 37


class Gather:
    def __init__(self, place, source, whole, split, send, recv):
        self.p, self.source, self.whole, self.send, self.recv = place, source, whole, send, recv
        self.half = whole.shape[3] // 2
        start = place.c * self.half
        self.left = pl.ds(pl.multiple_of(start, 128), split)
        self.right = pl.ds(pl.multiple_of(start + split, 128), self.half - split)
        self.mine = pl.ds(pl.multiple_of(start, 128), self.half)
        self.theirs = pl.ds(pl.multiple_of((1 - place.c) * self.half, 128), self.half)
        self.started = []

    def go(self, src, dst, sem, axis, index):
        rcopy(src, dst, self.send.at[sem], self.recv.at[sem], axis, index).start()
        self.started.append((dst.shape, sem))

    def came(self, dst, sem):
        rcopy(dst, dst, self.send.at[sem], self.recv.at[sem], "rep", self.p.sibling).wait_recv()

    def own(self):
        self.own_copy = pltpu.make_async_copy(self.source, self.whole.at[self.p.shard], self.recv.at[OWN])
        self.own_copy.start()

    def stage_z(self):
        p = self.p
        for cols, base in ((self.left, XZ), (self.right, YZ)):
            for dz in (1, 2, 3):
                self.go(
                    self.source.at[p.x, :, cols], self.whole.at[p.shard, p.x, :, cols], base + 4 - dz, "shard", p.plane(dz) * 2 + p.y
                )

    def stage_second(self):
        p = self.p
        own = self.source.at[p.x, :, self.left]
        self.go(own, self.whole.at[p.shard, p.x, :, self.left], XY, "shard", p.beside)
        own = self.source.at[:, :, self.right]
        self.go(own, self.whole.at[p.shard, :, :, self.right], YY, "shard", p.beside)
        for dz in (1, 2, 3):
            spot = self.whole.at[p.block(dz, 0), p.x, :, self.left]
            self.came(spot, XZ + dz)
            self.go(spot, spot, XY + dz, "shard", p.beside)
            self.go(spot, spot, XX + dz, "rep", p.across)
            spot = self.whole.at[p.block(dz, 0), p.x, :, self.right]
            self.came(spot, YZ + dz)
            self.go(spot, spot, YX + dz, "rep", p.across)

    def stage_third(self):
        p = self.p
        for dz in range(4):
            spot = self.whole.at[p.block(dz, 1), p.x, :, self.left]
            self.came(spot, XY + dz)
            self.go(spot, spot, XX + 4 + dz, "rep", p.across)
            if dz:
                self.came(self.whole.at[p.block(dz, 0), 1 - p.x, :, self.right], YX + dz)
                spot = self.whole.at[p.block(dz, 0), :, :, self.right]
                self.go(spot, spot, YY + dz, "shard", p.beside)

    def stage_core(self):
        p = self.p
        for dy in (0, 1):
            for dz in range(4):
                if dy or dz:
                    self.came(self.whole.at[p.block(dz, dy), 1 - p.x, :, self.left], XX + 4 * dy + dz)
                    if dy:
                        self.came(self.whole.at[p.block(dz, 1), :, :, self.right], YY + dz)
                    spot = self.whole.at[p.block(dz, dy), :, :, self.mine]
                    self.go(spot, spot, CC + 4 * dy + dz, "rep", p.sibling)

    def finish(self):
        p = self.p
        self.own_copy.wait()
        for dy in (0, 1):
            for dz in range(4):
                if dy or dz:
                    self.came(self.whole.at[p.block(dz, dy), :, :, self.theirs], CC + 4 * dy + dz)

    def drain(self):
        for shape, sem in self.started:
            spot = self.whole.at[0, 0] if len(shape) == 2 else self.whole.at[0]
            spot = spot.at[..., : shape[-1]]
            rcopy(spot, spot, self.send.at[sem], self.recv.at[sem], "rep", self.p.sibling).wait_send()


SC, LX, LY, LZ, RY, RX, RZ, AX, AC, SCATTER_SEMS = 0, 1, 2, 3, 7, 8, 9, 13, 14, 15


def scatter_buffers(shape, split):
    _, _, rows, columns = shape
    half = columns // 2
    left, right = split, half - split
    return [
        (8, 2, rows, half), (4, 2, rows, left), (4, rows, left), (3, rows, left), (4, 2, rows, right), (4, rows, right), (3, rows, right),
        (2, rows, columns),
    ]


class Scatter:
    def __init__(self, place, part, split, buffers, send, recv):
        self.p, self.part, self.send, self.recv, self.split = place, part, send, recv, split
        self.core, self.left2, self.left3, self.left4, self.right2, self.right3, self.right4, self.out = buffers
        self.half = self.core.shape[3]
        self.mine = pl.ds(pl.multiple_of(place.c * self.half, 128), self.half)
        self.theirs = pl.ds(pl.multiple_of((1 - place.c) * self.half, 128), self.half)
        self.left, self.right = slice(0, split), slice(split, self.half)

    def go(self, src, dst, sem, axis, index):
        rcopy(src, dst, self.send.at[sem], self.recv.at[sem], axis, index).start()

    def came(self, dst, sem):
        rcopy(dst, dst, self.send.at[sem], self.recv.at[sem], "rep", self.p.sibling).wait_recv()

    def stage_core(self):
        self.go(self.part.at[:, :, :, self.theirs], self.core, SC, "rep", self.p.sibling)

    def stage_second(self):
        p = self.p
        self.came(self.core, SC)

        @pl.loop(0, 8)
        def _(s):
            self.core[s] = self.core[s] + self.part[s, :, :, self.mine]

        halves = self.core.reshape(4, 2, 2, *self.core.shape[2:])
        self.go(halves.at[:, :, 1 - p.x, :, self.left], self.left2, LX, "rep", p.across)
        self.go(halves.at[:, 1 - p.y, :, :, self.right], self.right2, RY, "shard", p.beside)

    def stage_third(self):
        p = self.p
        halves = self.core.reshape(4, 2, 2, *self.core.shape[2:])
        self.came(self.left2, LX)

        @pl.loop(0, 4)
        def _(z):
            self.left2[z] = self.left2[z] + halves[z, :, p.x, :, self.left]

        self.go(self.left2.at[:, 1 - p.y], self.left3, LY, "shard", p.beside)
        self.came(self.right2, RY)

        @pl.loop(0, 4)
        def _(z):
            self.right2[z] = self.right2[z] + halves[z, p.y, :, :, self.right]

        self.go(self.right2.at[:, 1 - p.x], self.right3, RX, "rep", p.across)

    def stage_z(self):
        p = self.p
        for third, second, mine, sem, fourth, base in (
            (self.left3, self.left2, p.y, LY, self.left4, LZ), (self.right3, self.right2, p.x, RX, self.right4, RZ)
        ):
            self.came(third, sem)
            third[...] = third[...] + second[:, mine]
            for dz in (1, 2, 3):
                self.go(third.at[p.plane(dz)], fourth.at[3 - dz], base + 3 - dz, "shard", p.plane(dz) * 2 + p.y)

    def stage_share(self):
        p = self.p
        start = p.c * self.half
        for third, fourth, base, offset, size in (
            (self.left3, self.left4, LZ, 0, self.split), (self.right3, self.right4, RZ, self.split, self.half - self.split)
        ):
            total = third[p.z].astype(F32)
            for dz in range(3):
                self.came(fourth.at[dz], base + dz)
                total = total + fourth[dz].astype(F32)
            self.out[p.x, :, pl.ds(pl.multiple_of(start + offset, 128), size)] = total.astype(BF16)
        spot = self.out.at[p.x, :, self.mine]
        self.go(spot, spot, AX, "rep", p.across)

    def stage_last(self):
        p = self.p
        self.came(self.out.at[1 - p.x, :, self.mine], AX)
        spot = self.out.at[:, :, self.mine]
        self.go(spot, spot, AC, "rep", p.sibling)

    def finish(self):
        self.came(self.out.at[:, :, self.theirs], AC)

    def drain(self):
        p = self.p
        spots = [(self.core, SC), (self.left2, LX), (self.right2, RY), (self.left3, LY), (self.right3, RX)]
        spots += [(self.left4.at[dz], LZ + dz) for dz in range(3)] + [(self.right4.at[dz], RZ + dz) for dz in range(3)]
        spots += [(self.out.at[0, :, : self.half], AX), (self.out.at[:, :, : self.half], AC)]
        for spot, sem in spots:
            rcopy(spot, spot, self.send.at[sem], self.recv.at[sem], "rep", p.sibling).wait_send()


def one_hot(perm_ref, h, pt_ref):
    length = pt_ref.shape[0]
    row = perm_ref[pl.ds(h, 1), :].astype(jnp.int16)
    places = lax.broadcasted_iota(jnp.int16, (length, length), 0)
    pt_ref[...] = jnp.where(places == row, jnp.ones((), BF16), jnp.zeros((), BF16))


def fwd_kernel(heads, remote, *refs):
    (x_hbm, w_in_hbm, w_out_hbm, w_inner_hbm, w_outer_hbm, vec_ref, seg_ref, ok_ref, qperm_ref, kperm_ref, cot_hbm), refs = refs[:11], refs[11:]
    (hid_hbm, act_hbm, din_hbm, flow_hbm, dou_hbm, dfi_hbm, dbr_hbm, att_hbm, head_hbm, xt_hbm, vgrad_ref), refs = refs[:11], refs[11:]
    if remote:
        (w_in_whole, w_out_whole), refs = refs[:2], refs[2:]
    (xv, cot, w_in, w_out, w_inner, w_outer, qkv, qcode, kcode, ptq, ptk, att, head, xt), refs = refs[:14], refs[14:]
    (act, din, flow, dou, dfi, dbr, hid, gp, fo, nf, ds, in_sem, out_sem, head_sem), refs = refs[:14], refs[14:]
    length, width = xv.shape
    hd = width // heads
    ff = act.shape[-1]
    tm = act.shape[1]
    fc = width
    n_in = 3 * width

    if remote:
        vslots, send, recv, vsend, vrecv, whole_sem = refs
        p = Place()
        barrier = pltpu.get_barrier_semaphore()
        n_shard = lax.axis_size("shard")
        for d in range(1, n_shard):
            pl.semaphore_signal(barrier, inc=1, device_id={"shard": (p.shard + d) % n_shard}, device_id_type=pl.DeviceIdType.MESH)
        for other in (p.sibling, p.across):
            pl.semaphore_signal(barrier, inc=1, device_id={"rep": other}, device_id_type=pl.DeviceIdType.MESH)
        weights = [
            Gather(p, source, whole, split, send.at[a], recv.at[a])
            for a, (source, whole, split) in enumerate(
                ((w_in_hbm, w_in, 640), (w_out_hbm, w_out, 256), (w_inner_hbm, w_inner, 768), (w_outer_hbm, w_outer, 128))
            )
        ]
        g_in, g_out, g_inner, g_outer = weights
        pl.semaphore_wait(barrier, n_shard + 1)
        g_in.stage_z()
        shorts = [
            rcopy(vec_ref, vslots.at[n_shard - d], vsend.at[n_shard - d], vrecv.at[n_shard - d], "shard", (p.shard + d) % n_shard)
            for d in range(1, n_shard)
        ]
        for copy in shorts:
            copy.start()
        g_out.stage_z()
        loads = [pltpu.make_async_copy(s, d, in_sem.at[i]) for i, (s, d) in enumerate(((x_hbm, xv), (cot_hbm, cot)))]
        loads[0].start()
        for weight in weights:
            weight.own()
        loads[1].start()
    else:
        loads = [
            pltpu.make_async_copy(s, d, in_sem.at[i])
            for i, (s, d) in enumerate(
                ((x_hbm, xv), (w_in_hbm, w_in), (w_out_hbm, w_out), (w_inner_hbm, w_inner), (w_outer_hbm, w_outer), (cot_hbm, cot))
            )
        ]
        for load in loads:
            load.start()

    code_rows = lax.broadcasted_iota(jnp.int32, (16, length), 0)
    seg = seg_ref[...]
    ok = ok_ref[...] > 0
    qcode[...] = jnp.where(code_rows == jnp.where(ok, seg, 4), 1.0, 0.0).astype(BF16)
    kcode[...] = jnp.where((code_rows < 5) & (code_rows != jnp.where(ok, seg, 5)), -BIG, 0.0).astype(BF16)

    loads[0].wait()
    xt[...] = xv[...].T
    if remote:
        g_in.stage_second()
        g_out.stage_second()
        g_in.stage_third()
        g_inner.stage_z()
        g_in.stage_core()
        g_out.stage_third()
        for copy in shorts:
            copy.wait_recv()
        vec = vec_ref[...].astype(F32)
        for d in range(1, n_shard):
            vec = vec + vslots[d].astype(F32)
        g_in.finish()
        whole_in = pltpu.make_async_copy(w_in, w_in_whole, whole_sem.at[0])
        whole_in.start()
    else:
        vec = vec_ref[...].astype(F32)
        loads[1].wait()
    vec_t = vec.T
    nt = 256
    for i in range(n_in // nt):
        n0 = i * nt
        acc = mm(rows2(w_in[:, :, :, n0 : n0 + nt]), xv[...], TT)
        if n0 < width:
            acc = (acc + vec_t[n0 : n0 + nt, 0:1]).astype(BF16) * 0.125
        elif n0 >= 2 * width:
            acc = acc + vec_t[n0 - 2 * width : n0 - 2 * width + nt, 1:2]
        qkv[n0 : n0 + nt, :] = acc.astype(BF16)

    def attend(h):
        r0 = pl.multiple_of(h * hd, hd)
        rows = pl.ds(r0, hd)
        one_hot(qperm_ref, h, ptq)
        one_hot(kperm_ref, h, ptk)
        q_side = jnp.concatenate([qkv[rows, :], qcode[...]], axis=0)
        k_side = jnp.concatenate(
            [qkv[pl.ds(pl.multiple_of(width + r0, hd), hd), :], kcode[...], qkv[pl.ds(pl.multiple_of(2 * width + r0, hd), hd), :]],
            axis=0,
        )
        q_arr = mm(q_side, ptq[...], NN).astype(BF16)
        k_arr = mm(k_side, ptk[...], NN).astype(BF16)
        v_arr = k_arr[hd + 16 :, :]
        head[h, :hd, :] = q_arr[:hd, :]
        head[h, hd : 2 * hd, :] = k_arr[:hd, :]
        head[h, 2 * hd : 3 * hd, :] = v_arr
        cols = [slice(c * CL, (c + 1) * CL) for c in range(length // CL)]
        scores = jnp.concatenate([mm(k_arr[: hd + 16, c], q_arr[:, c], TN) for c in cols], axis=1)
        top = jnp.maximum(jnp.max(scores, axis=0, keepdims=True), -1e29)
        raised = jnp.exp(scores - top)
        total = jnp.maximum(jnp.sum(raised, axis=0, keepdims=True), 1.0)
        probs = (raised * (1.0 / total)).astype(BF16)
        head[h, 3 * hd :, :] = probs
        combined = jnp.concatenate([mm(v_arr[:, c], probs[:, c], NN) for c in cols], axis=1)
        att[rows, :] = mm(combined.astype(BF16), ptq[...], NT).astype(BF16)

    if remote:
        g_out.stage_core()
        g_outer.stage_z()
        g_inner.stage_second()

    @pl.loop(0, heads)
    def _(h):
        attend(h)
        if remote:
            @pl.when(h == heads // 3)
            def _():
                g_inner.stage_third()
                g_outer.stage_second()

            @pl.when(h == 2 * heads // 3)
            def _():
                g_inner.stage_core()
                g_outer.stage_third()

    heads_out = [
        pltpu.make_async_copy(s, d, head_sem.at[i])
        for i, (s, d) in enumerate(((att, att_hbm), (head, head_hbm), (xt, xt_hbm)))
    ]
    for copy in heads_out:
        copy.start()
    if remote:
        g_outer.stage_core()
        loads[1].wait()
        g_out.finish()
        whole_out = pltpu.make_async_copy(w_out, w_out_whole, whole_sem.at[1])
        whole_out.start()
        g_inner.finish()
        g_outer.finish()
    else:
        for load in loads[2:]:
            load.wait()

    b_out, g_first, s_first = vec[2:3, :], vec[3:4, :], vec[4:5, :]
    b_outer, g_second, s_second = vec[5:6, :], vec[6:7, :], vec[7:8, :]
    vgrad_ref[...] = jnp.zeros_like(vgrad_ref)

    def add_row(row, value):
        vgrad_ref[row : row + 1, :] += jnp.sum(value, axis=0, keepdims=True)

    def outs(i, slot):
        rows = pl.ds(pl.multiple_of(i * tm, tm), tm)
        return [
            pltpu.make_async_copy(s.at[slot], d.at[rows, :], out_sem.at[slot, n])
            for n, (s, d) in enumerate(
                ((act, act_hbm), (din, din_hbm), (flow, flow_hbm), (dou, dou_hbm), (dfi, dfi_hbm), (dbr, dbr_hbm), (hid, hid_hbm))
            )
        ]

    n_tiles = length // tm

    @pl.loop(0, n_tiles)
    def _(i):
        slot = lax.rem(i, 2)
        t0 = pl.multiple_of(i * tm, tm)
        rows = pl.ds(t0, tm)

        @pl.when(i >= 2)
        def _():
            for copy in outs(i - 2, slot):
                copy.wait()

        branch = mm(att[:, rows], rows2(w_out[...]), TN)
        first_sum = xv[rows, :].astype(F32) + branch + b_out
        normed, inv_first = norm_parts(first_sum)
        nf[...] = normed
        first_out = normed * g_first + s_first
        fo[...] = first_out
        flow[slot] = first_out.astype(BF16)
        outer = None
        for j in range(ff // fc):
            cols = slice(j * fc, (j + 1) * fc)
            inner = mm(flow[slot], rows2(w_inner[:, :, :, cols]), NN) + vec[8 + j : 9 + j, :]
            high, slope = gelu_both(inner)
            act[slot, :, cols] = high.astype(BF16)
            gp[:, cols] = slope
            per = w_outer.shape[0] * fc // ff
            term = mm(act[slot, :, cols], rows2(w_outer[j * per : (j + 1) * per]), NN)
            outer = term if outer is None else outer + term
        normed_second, inv_second = norm_parts(fo[...] + outer + b_outer)
        hid[slot] = (normed_second * g_second + s_second).astype(BF16)
        grad = cot[rows, :].astype(F32)
        d_second = norm_back(grad, normed_second, inv_second, g_second)
        add_row(6, grad * normed_second)
        add_row(7, grad)
        ds[...] = d_second
        low = d_second.astype(BF16)
        dou[slot] = low
        add_row(5, low.astype(F32))
        back = None
        for j in range(ff // fc):
            cols = slice(j * fc, (j + 1) * fc)
            per = w_outer.shape[0] * fc // ff
            d_act = mm(dou[slot], rows2(w_outer[j * per : (j + 1) * per]), NT)
            d_inner = (d_act * gp[:, cols]).astype(BF16)
            din[slot, :, cols] = d_inner
            add_row(8 + j, d_inner.astype(F32))
            term = mm(d_inner, rows2(w_inner[:, :, :, cols]), NT)
            back = term if back is None else back + term
        d_first_out = ds[...] + back
        normed = nf[...]
        add_row(3, d_first_out * normed)
        add_row(4, d_first_out)
        d_first = norm_back(d_first_out, normed, inv_first, g_first)
        dfi[slot] = d_first
        low = d_first.astype(BF16)
        dbr[slot] = low
        add_row(2, low.astype(F32))
        for copy in outs(i, slot):
            copy.start()

    for i in range(max(0, n_tiles - 2), n_tiles):
        for copy in outs(i, i % 2):
            copy.wait()
    for copy in heads_out:
        copy.wait()
    if remote:
        for weight in weights:
            weight.drain()
        for copy in shorts:
            copy.wait_send()
        whole_in.wait()
        whole_out.wait()


def fwd_call(remote, x, w_in, w_out, w_inner, w_outer, vec, seg, ok, qperm, kperm, cot):
    length, width = x.shape
    heads = qperm.shape[0]
    hd = width // heads
    ff = w_inner.shape[-1]
    wholes = [(8, 2, w.shape[-2], w.shape[-1]) for w in (w_in, w_out, w_inner, w_outer)]
    tm = 256
    hbm = pl.BlockSpec(memory_space=pl.ANY)
    vmem = pl.BlockSpec(memory_space=pltpu.VMEM)
    outs = [
        ((length, width), BF16), ((length, ff), BF16), ((length, ff), BF16), ((length, width), BF16), ((length, width), BF16),
        ((length, width), F32), ((length, width), BF16), ((width, length), BF16), ((heads, 3 * hd + CL, length), BF16),
        ((width, length), BF16), ((16, width), F32),
    ]
    if remote:
        outs += [(wholes[0], BF16), (wholes[1], BF16)]
    scratch = [
        ((length, width), BF16), ((length, width), BF16), *[(whole, BF16) for whole in wholes],
        ((3 * width, length), BF16), ((16, length), BF16), ((16, length), BF16), ((length, length), BF16), ((length, length), BF16),
        ((width, length), BF16), ((heads, 3 * hd + CL, length), BF16), ((width, length), BF16),
        ((2, tm, ff), BF16), ((2, tm, ff), BF16), ((2, tm, width), BF16), ((2, tm, width), BF16), ((2, tm, width), F32), ((2, tm, width), BF16),
        ((2, tm, width), BF16), ((tm, ff), F32), ((tm, width), F32), ((tm, width), F32), ((tm, width), F32),
    ]
    sems = [(6,), (2, 7), (3,)]
    if remote:
        n_shard = lax.axis_size("shard")
        extra = [pltpu.VMEM((n_shard, 16, width), BF16)]
        extra += [pltpu.SemaphoreType.DMA(n) for n in ((4, GATHER_SEMS), (4, GATHER_SEMS), (n_shard,), (n_shard,), (2,))]
    else:
        extra = []
    return pl.pallas_call(
        partial(fwd_kernel, heads, remote),
        out_shape=[jax.ShapeDtypeStruct(s, d) for s, d in outs],
        in_specs=[hbm] * 5 + [vmem] * 5 + [hbm],
        out_specs=[hbm] * 10 + [vmem] + [hbm] * (len(outs) - 11),
        scratch_shapes=[pltpu.VMEM(s, d) for s, d in scratch]
        + [pltpu.SemaphoreType.DMA(n) for n in sems]
        + extra,
        compiler_params=pltpu.CompilerParams(vmem_limit_bytes=60 << 20, collective_id=0 if remote else None, has_side_effects=remote),
        name="layer_forward",
    )(x, w_in, w_out, w_inner, w_outer, vec, seg, ok, qperm, kperm, cot)


HG = 4


def bwd_kernel(heads, remote, splits, *refs):
    (act_hbm, din_hbm, flow_hbm, dou_hbm, dfi_hbm, dbr_hbm, att_hbm, head_hbm, xt_hbm, w_in_hbm, w_out_hbm, qperm_ref, kperm_ref, vg_ref), refs = (
        refs[:14], refs[14:]
    )
    groups = heads // HG
    n_grads = groups + 3
    (ig_hbm, vgrad_ref), grad_outs, refs = refs[:2], refs[2 : 2 + n_grads], refs[2 + n_grads :]
    (act, din, flow, dou, dfi, att, head, xt, w_in, w_out, ptq, ptk, mixed, dproj), refs = refs[:14], refs[14:]
    dbr = flow
    grads, refs = refs[:n_grads], refs[n_grads:]
    (ig, in_sem, act_sem, din_sem, head_sem, dfi_sem, ig_sem, out_sem), refs = refs[:8], refs[8:]
    g_outer, g_inner, g_out, *g_in = grads
    length, width = flow.shape
    hd = width // heads
    tm = ig.shape[1]
    fc = act.shape[2]
    ic = din.shape[2]
    copy = pltpu.make_async_copy
    n_act = act_hbm.shape[1] // fc
    n_din = din_hbm.shape[1] // ic
    n_tiles = length // tm
    acts = [copy(act_hbm.at[:, j * fc : (j + 1) * fc], act.at[j % 2], act_sem.at[j % 2]) for j in range(n_act)]
    dins = [copy(din_hbm.at[:, j * ic : (j + 1) * ic], din.at[j % 2], din_sem.at[j % 2]) for j in range(n_din)]
    dfis = [copy(dfi_hbm.at[i * tm : (i + 1) * tm, :], dfi.at[i % 2], dfi_sem.at[i % 2]) for i in range(n_tiles)]
    loads = {
        name: copy(s, d, in_sem.at[i])
        for i, (name, s, d) in enumerate(
            (
                ("dou", dou_hbm, dou), ("flow", flow_hbm, flow), ("dbr", dbr_hbm, dbr), ("w_out", w_out_hbm, w_out),
                ("att", att_hbm, att), ("xt", xt_hbm, xt.at[:width, :]), ("w_in", w_in_hbm, w_in),
            )
        )
    }

    def head_copy(h, slot):
        return copy(head_hbm.at[h], head.at[slot], head_sem.at[slot])

    if remote:
        buffers, (vslots, vsum, vsend, vrecv, send, recv) = refs[: 8 * n_grads], refs[8 * n_grads :]
        p = Place()
        sums = [
            Scatter(p, grads[a], splits[a], buffers[8 * a : 8 * a + 8], send.at[a], recv.at[a]) for a in range(n_grads)
        ]
        s_outer, s_inner, s_out, *s_in = sums
        barrier = pltpu.get_barrier_semaphore()
        for other in (p.sibling, p.across):
            pl.semaphore_signal(barrier, inc=1, device_id={"rep": other}, device_id_type=pl.DeviceIdType.MESH)
        for other in [p.beside] + [p.plane(dz) * 2 + p.y for dz in (1, 2, 3)]:
            pl.semaphore_signal(barrier, inc=1, device_id={"shard": other}, device_id_type=pl.DeviceIdType.MESH)

    loads["dou"].start()
    acts[0].start()
    acts[1].start()
    loads["flow"].start()
    dins[0].start()
    dins[1].start()
    for name in ("w_out", "att", "xt", "w_in"):
        loads[name].start()
    head_copy(0, 0).start()
    dfis[0].start()
    dfis[1].start()

    loads["dou"].wait()
    for j in range(n_act):
        acts[j].wait()
        part = mm(act[j % 2], dou[...], TN)
        g_outer[j] = part.astype(BF16).reshape(g_outer.shape[1:])
        if j + 2 < n_act:
            acts[j + 2].start()
    if remote:
        pl.semaphore_wait(barrier, 6)
        s_outer.stage_core()

    loads["flow"].wait()
    mixed[...] = flow[...].T
    loads["dbr"].start()
    for j in range(n_din):
        dins[j].wait()
        part = mm(mixed[...], din[j % 2], NN)
        g_inner[:, :, :, j * ic : (j + 1) * ic] = part.astype(BF16).reshape(g_inner.shape[:3] + (ic,))
        if j + 2 < n_din:
            dins[j + 2].start()
    if remote:
        s_inner.stage_core()
        s_outer.stage_second()

    for name in ("dbr", "w_out", "att"):
        loads[name].wait()
    mixed[...] = mm(rows2(w_out[...]), dbr[...], NT).astype(BF16)
    g_out[...] = mm(att[...], dbr[...], NN).astype(BF16).reshape(g_out.shape)
    if remote:
        s_out.stage_core()
        s_inner.stage_second()

    cols = [slice(c * CL, (c + 1) * CL) for c in range(length // CL)]

    def attend(h):
        slot = lax.rem(h, 2)
        one_hot(qperm_ref, h, ptq)
        one_hot(kperm_ref, h, ptk)
        r0 = pl.multiple_of(h * hd, hd)
        d_arr = mm(mixed[pl.ds(r0, hd), :], ptq[...], NN).astype(BF16)
        head_copy(h, slot).wait()

        @pl.when(h + 1 < heads)
        def _():
            head_copy(h + 1, 1 - slot).start()

        q_arr = head[slot, :hd, :]
        k_arr = head[slot, hd : 2 * hd, :]
        v_arr = head[slot, 2 * hd : 3 * hd, :]
        probs = head[slot, 3 * hd :, :]
        d_probs = jnp.concatenate([mm(v_arr[:, c], d_arr[:, c], TN) for c in cols], axis=1)
        wide = probs.astype(F32)
        terms = jnp.sum(wide * d_probs, axis=0, keepdims=True)
        d_scores = (wide * (d_probs - terms)).astype(BF16)
        dq = jnp.concatenate([mm(k_arr[:, c], d_scores[:, c], NN) for c in cols], axis=1) * 0.125
        dk = jnp.concatenate([mm(q_arr[:, c], d_scores[:, c], NT) for c in cols], axis=1)
        dv = jnp.concatenate([mm(d_arr[:, c], probs[:, c], NT) for c in cols], axis=1)
        dproj[pl.ds(r0, hd), :] = mm(dq.astype(BF16), ptq[...], NT).astype(BF16)
        dkv = mm(jnp.concatenate([dk, dv], axis=0).astype(BF16), ptk[...], NT).astype(BF16)
        dproj[pl.ds(pl.multiple_of(width + r0, hd), hd), :] = dkv[:hd, :]
        dproj[pl.ds(pl.multiple_of(2 * width + r0, hd), hd), :] = dkv[hd:, :]

    loads["xt"].wait()
    xt[width:, :] = jnp.where(lax.broadcasted_iota(jnp.int32, (16, length), 0) == 0, 1.0, 0.0).astype(BF16)
    vgrad_ref[...] = vg_ref[...]
    gw = HG * hd
    pumps = {}
    if remote:
        pumps = {
            2: [s_out.stage_second],
            5: [s_outer.stage_third, s_in[0].stage_second],
            7: [s_out.stage_third],
            8: [s_outer.stage_z],
            9: [s_inner.stage_third, s_in[1].stage_second],
            10: [s_out.stage_z, s_in[0].stage_third],
            11: [s_outer.stage_share, s_inner.stage_z],
        }
    for g in range(groups):
        @pl.loop(g * HG, (g + 1) * HG)
        def _(h):
            attend(h)
            for at in range(g * HG, (g + 1) * HG):
                if at in pumps:
                    @pl.when(h == at)
                    def _():
                        for pump in pumps[at]:
                            pump()

        for part in range(3):
            c0 = part * width + g * gw
            prod = mm(xt[...], dproj[c0 : c0 + gw, :], NT)
            g_in[g][:, :, :, part * gw : (part + 1) * gw] = prod[:width].astype(BF16).reshape(g_in[g].shape[:3] + (gw,))
            if part != 1:
                vgrad_ref[part // 2 : part // 2 + 1, g * gw : (g + 1) * gw] = prod[width : width + 1]
        if remote:
            s_in[g].stage_core()

    def vector_stage(n, axis, others):
        copies = [rcopy(vsum, vslots.at[n + i], vsend.at[n + i], vrecv.at[n + i], axis, other) for i, other in enumerate(others)]
        for one in copies:
            one.start()

        def wait():
            for one in copies:
                one.wait()
            total = vsum[...]
            for i in range(len(others)):
                total = total + vslots[n + i]
            vsum[...] = total

        return wait

    if remote:
        vsum[...] = vgrad_ref[...]
        vector_wait = vector_stage(0, "rep", [p.sibling])
        s_in[1].stage_third()
        s_out.stage_share()
        s_in[2].stage_second()
        s_outer.stage_last()
        s_in[0].stage_z()
        vector_wait()
        vector_wait = vector_stage(1, "rep", [p.across])
    else:
        outs = [copy(s, d, out_sem.at[i]) for i, (s, d) in enumerate(zip(grads, grad_outs))]
        for out in outs:
            out.start()
    loads["w_in"].wait()
    stores = [copy(ig.at[i % 2], ig_hbm.at[i * tm : (i + 1) * tm, :], ig_sem.at[i % 2]) for i in range(n_tiles)]
    for i in range(n_tiles):
        prod = mm(rows2(w_in[...]), dproj[:, i * tm : (i + 1) * tm], NN)
        dfis[i].wait()
        if i >= 2:
            stores[i - 2].wait()
        ig[i % 2] = (dfi[i % 2] + prod.T).astype(BF16)
        stores[i].start()
        if i + 2 < n_tiles:
            dfis[i + 2].start()
        if remote and i == 0:
            s_in[1].stage_z()
            s_inner.stage_share()
            s_out.stage_last()
            vector_wait()
            vector_wait = vector_stage(2, "shard", [p.beside])
        if remote and i == 2:
            s_in[2].stage_third()
            s_in[0].stage_share()
            vector_wait()
            vector_wait = vector_stage(3, "shard", [p.plane(dz) * 2 + p.y for dz in (3, 2, 1)])
    if remote:
        s_inner.stage_last()
        s_in[2].stage_z()
        s_in[1].stage_share()
        s_in[0].stage_last()
        vector_wait()
        vgrad_ref[...] = vsum[...]
        s_in[2].stage_share()
        s_in[1].stage_last()
        s_in[2].stage_last()
        for one in sums:
            one.finish()
        outs = [copy(one.out, d, out_sem.at[i]) for i, (one, d) in enumerate(zip(sums, grad_outs))]
        for out in outs:
            out.start()
        for one in sums:
            one.drain()
    for i in range(max(0, n_tiles - 2), n_tiles):
        stores[i].wait()
    for out in outs:
        out.wait()


def bwd_call(remote, act, din, flow, dou, dfi, dbr, att, head, xt, w_in, w_out, qperm, kperm, vgrad):
    length, width = flow.shape
    heads = qperm.shape[0]
    hd = width // heads
    ff = act.shape[1]
    groups = heads // HG
    tm = 256
    hbm = pl.BlockSpec(memory_space=pl.ANY)
    vmem = pl.BlockSpec(memory_space=pltpu.VMEM)
    blocks = w_in.shape[:3]
    gshapes = [(8, 2, ff // 16, width), blocks + (ff,), blocks + (width,)] + [blocks + (3 * HG * hd,)] * groups
    splits = [256, 768, 128] + [128, 256, 128][:groups]
    n_grads = len(gshapes)
    fc = ff // 8
    outs = [((length, width), BF16), ((16, width), F32)]
    outs += [((shape[1:] if remote else shape), BF16) for shape in gshapes]
    scratch = [
        ((2, length, fc), BF16), ((2, length, fc), BF16), ((length, width), BF16), ((length, width), BF16), ((2, tm, width), F32),
        ((width, length), BF16), ((2,) + head.shape[1:], BF16), ((width + 16, length), BF16), (w_in.shape, BF16), (w_out.shape, BF16),
        ((length, length), BF16), ((length, length), BF16), ((width, length), BF16), ((3 * width, length), BF16),
    ] + [(s, BF16) for s in gshapes] + [((2, tm, width), BF16)]
    extra = []
    if remote:
        for shape, split in zip(gshapes, splits):
            extra += [pltpu.VMEM(s, BF16) for s in scatter_buffers(shape, split)]
        extra += [pltpu.VMEM((6, 16, width), F32), pltpu.VMEM((16, width), F32)]
        extra += [pltpu.SemaphoreType.DMA(n) for n in ((6,), (6,), (n_grads, SCATTER_SEMS), (n_grads, SCATTER_SEMS))]
    return pl.pallas_call(
        partial(bwd_kernel, heads, remote, splits),
        out_shape=[jax.ShapeDtypeStruct(s, d) for s, d in outs],
        in_specs=[hbm] * 11 + [vmem] * 3,
        out_specs=[hbm, vmem] + [hbm] * n_grads,
        scratch_shapes=[pltpu.VMEM(s, d) for s, d in scratch]
        + [pltpu.SemaphoreType.DMA((n,)) for n in (7, 2, 2, 2, 2, 2, n_grads)]
        + extra,
        compiler_params=pltpu.CompilerParams(vmem_limit_bytes=60 << 20, collective_id=1 if remote else None, has_side_effects=remote),
        name="layer_backward",
    )(act, din, flow, dou, dfi, dbr, att, head, xt, w_in, w_out, qperm, kperm, vgrad)


def shards(
    layer_input, in_weight, query_bias, value_bias, out_weight, out_bias, first_gain, first_shift, inner_weight, inner_bias,
    outer_weight, outer_bias, second_gain, second_shift, segment_ids, token_valid, query_perm, key_perm, out_cotangent,
):
    _, length, width = layer_input.shape
    heads = query_perm.shape[1]
    ff = inner_weight.shape[1]
    n_shard = lax.axis_size("shard")
    shard = lax.axis_index("shard")

    piece = width // n_shard
    remote = n_shard == 8 and lax.axis_size("rep") == 4

    def whole(rows):
        return lax.all_gather(rows, "shard", axis=0, tiled=True)

    def blocked(rows):
        return rows.reshape(8, 2, rows.shape[0] // 16, rows.shape[1])

    def halved(rows):
        return rows.reshape(2, rows.shape[0] // 2, rows.shape[1])

    weights = (in_weight, out_weight, inner_weight, outer_weight)
    short = jnp.stack([query_bias, value_bias, out_bias, first_gain, first_shift, outer_bias, second_gain, second_shift])
    inner_piece = ff // n_shard
    if remote:
        w_in, w_out, w_inner, w_outer = [halved(w) for w in weights]
        vec = lax.dynamic_update_slice(jnp.zeros((16, width), BF16), short, (0, shard * piece))
        first = shard * inner_piece
        vec = lax.dynamic_update_slice(vec, inner_bias[None], (8 + first // width, first % width))
    else:
        w_in, w_out, w_inner, w_outer = [blocked(whole(w)) for w in weights]
        vectors = lax.all_gather(jnp.concatenate([short.reshape(-1), inner_bias]), "shard", axis=0)
        vec = jnp.concatenate(
            [
                jnp.transpose(vectors[:, : 8 * piece].reshape(n_shard, 8, piece), (1, 0, 2)).reshape(8, width),
                vectors[:, 8 * piece :].reshape(ff // width, width),
                jnp.zeros((8 - ff // width, width), BF16),
            ]
        )
    hidden, act, din, flow, dou, dfi, dbr, att, head, xt, vg, *wholes = fwd_call(
        remote, layer_input[0], w_in, w_out, w_inner, w_outer, vec, segment_ids, token_valid, query_perm[0], key_perm[0], out_cotangent[0]
    )
    if remote:
        w_in, w_out = wholes
    grad_x, vg, g_outer, g_inner, g_out, *g_in = bwd_call(
        remote, act, din, flow, dou, dfi, dbr, att, head, xt, w_in, w_out, query_perm[0], key_perm[0], vg
    )
    groups = heads // HG
    g_in = jnp.stack([g.reshape(-1, 3, width // groups) for g in g_in], axis=2).reshape(-1, 3 * width)
    grads = [g_in, g_out.reshape(-1, width), g_inner.reshape(-1, ff), g_outer.reshape(-1, width)]

    def summed(grad):
        rows = lax.psum_scatter(grad.astype(F32), "shard", scatter_dimension=0, tiled=True)
        return lax.psum(rows.astype(BF16), "rep").astype(F32)

    if remote:
        d_in, d_out, d_inner, d_outer = [g.astype(F32) for g in grads]
    else:
        d_in, d_out, d_inner, d_outer = [summed(g) for g in grads]
        vg = lax.psum(vg, ("rep", "shard"))
    mine = lax.dynamic_slice(vg, (0, shard * piece), (8, piece))
    inner_mine = lax.dynamic_slice(vg[8 : 8 + ff // width].reshape(ff), (shard * inner_piece,), (inner_piece,))
    return (
        hidden[None], grad_x[None], d_in, mine[0], mine[1], d_out, mine[2], mine[3], mine[4], d_inner, inner_mine, d_outer,
        mine[5], mine[6], mine[7],
    )


def solution(mesh):
    rows, vector = P("shard", None), P("shard")
    seq2, seq3 = P(("rep", "shard"), None), P(("rep", "shard"), None, None)
    return jax.shard_map(
        shards,
        mesh=mesh,
        in_specs=(
            seq3, rows, vector, vector, rows, vector, vector, vector, rows, vector, rows, vector, vector, vector, seq2, seq2, seq3, seq3, seq3,
        ),
        out_specs=(seq3, seq3, rows, vector, vector, rows, vector, vector, vector, rows, vector, rows, vector, vector, vector),
        check_vma=False,
    )
```

```python
from functools import partial

import jax
import jax.numpy as jnp
from jax import lax
from jax.experimental import pallas as pl
from jax.experimental.pallas import tpu as pltpu
from jax.sharding import PartitionSpec as P

CL = 128
EPS = 1e-06
BIG = 2.0**100
F32 = jnp.float32
BF16 = jnp.bfloat16
NN = (((1,), (0,)), ((), ()))
NT = (((1,), (1,)), ((), ()))
TN = (((0,), (0,)), ((), ()))
TT = (((0,), (1,)), ((), ()))


def mm(a, b, dims):
    return lax.dot_general(a, b, dims, preferred_element_type=F32)


def rows2(value):
    return value.reshape(value.shape[0] * value.shape[1] * value.shape[2], value.shape[3])


def norm_parts(resid):
    average = jnp.mean(resid, axis=-1, keepdims=True)
    centred = resid - average
    variance = jnp.mean(centred * centred, axis=-1, keepdims=True)
    inv_std = lax.rsqrt(variance + EPS)
    return centred * inv_std, inv_std


def norm_back(grad_out, normed, inv_std, gain):
    scaled = grad_out * gain
    first_term = jnp.mean(scaled, axis=-1, keepdims=True)
    second_term = jnp.mean(scaled * normed, axis=-1, keepdims=True)
    return inv_std * (scaled - first_term - normed * second_term)


def gelu_both(z):
    gauss = jnp.exp(-0.5 * (z * z))
    t = 1.0 / (1.0 + (0.3275911 * 0.7071067811865476) * jnp.abs(z))
    poly = t * (0.127414796 + t * (-0.142248368 + t * (0.7107068705 + t * (-0.7265760135 + t * 0.5307027145))))
    tail = poly * gauss
    phi = jnp.where(z >= 0.0, 1.0 - tail, tail)
    return z * phi, phi + z * gauss * 0.3989422804014327


def rcopy(src, dst, send, recv, axis, index):
    return pltpu.make_async_remote_copy(
        src_ref=src, dst_ref=dst, send_sem=send, recv_sem=recv, device_id={axis: index}, device_id_type=pl.DeviceIdType.MESH
    )


class Place:
    def __init__(self):
        rep, shard = lax.axis_index("rep"), lax.axis_index("shard")
        self.x, self.c = rep // 2, rep % 2
        self.z, self.y = shard // 2, shard % 2
        self.rep, self.shard = rep, shard
        self.sibling = self.x * 2 + (1 - self.c)
        self.across = (1 - self.x) * 2 + self.c
        self.beside = self.z * 2 + (1 - self.y)

    def plane(self, dz):
        return (self.z + dz) % 4

    def block(self, dz, dy):
        return self.plane(dz) * 2 + (self.y + dy) % 2


GZ, GX, GA, GB, GC, GD, GATHER_SEMS = 0, 3, 6, 7, 8, 11, 12


class Gather:
    def __init__(self, place, whole, rows, start, size, kind, send, recv):
        half = whole.shape[-1] // 2
        self.p, self.rows, self.size, self.kind, self.send, self.recv = place, rows, size, kind, send, recv
        self.whole = whole.reshape(4, 2, 2, *whole.shape[2:])
        self.mine = pl.ds(pl.multiple_of(place.c * half + start, 128), size)
        self.theirs = pl.ds(pl.multiple_of((1 - place.c) * half + start, 128), size)

    def spot(self, z, y, x, columns=None):
        return self.whole.at[z, y, x, self.rows, self.mine if columns is None else columns]

    def go(self, spot, sem, axis, index):
        rcopy(spot, spot, self.send.at[sem], self.recv.at[sem], axis, index).start()

    def came(self, spot, sem):
        rcopy(spot, spot, self.send.at[sem], self.recv.at[sem], "rep", self.p.sibling).wait_recv()

    def first(self):
        p = self.p
        for dz in (1, 2, 3):
            self.go(self.spot(p.z, p.y, p.x), GZ + 3 - dz, "shard", p.plane(dz) * 2 + p.y)

    def second(self):
        p = self.p
        for dz in (1, 2, 3):
            spot = self.spot(p.plane(dz), p.y, p.x)
            self.came(spot, GZ + dz - 1)
            self.go(spot, GX + dz - 1, "rep", p.across)
        if self.kind == "x":
            self.go(self.spot(slice(None), p.y, p.x), GA, "shard", p.beside)

    def third(self):
        p = self.p
        if self.kind == "x":
            spot = self.spot(slice(None), 1 - p.y, p.x)
            self.came(spot, GA)
            self.go(spot, GB, "rep", p.across)
        for dz in (1, 2, 3):
            self.came(self.spot(p.plane(dz), p.y, 1 - p.x), GX + dz - 1)
        if self.kind == "y":
            self.go(self.spot(slice(None), p.y, slice(None)), GA, "shard", p.beside)
        for dz in (1, 2, 3):
            self.go(self.spot(p.plane(dz), p.y, slice(None)), GC + dz - 1, "rep", p.sibling)

    def fourth(self):
        p = self.p
        if self.kind == "x":
            self.came(self.spot(slice(None), 1 - p.y, 1 - p.x), GB)
        else:
            self.came(self.spot(slice(None), 1 - p.y, slice(None)), GA)
        self.go(self.spot(slice(None), 1 - p.y, slice(None)), GD, "rep", p.sibling)

    def last(self):
        p = self.p
        for dz in (1, 2, 3):
            self.came(self.spot(p.plane(dz), p.y, slice(None), self.theirs), GC + dz - 1)
        self.came(self.spot(slice(None), 1 - p.y, slice(None), self.theirs), GD)

    def drain(self):
        every = slice(None)
        columns = slice(0, self.size)
        one, four, pair, eight = (0, 0, 0), (every, 0, 0), (0, 0, every), (every, 0, every)
        sizes = {GA: four if self.kind == "x" else eight, GB: four, GD: eight}
        for dz in range(3):
            sizes.update({GZ + dz: one, GX + dz: one, GC + dz: pair})
        if self.kind == "y":
            del sizes[GB]
        for sem, (z, y, x) in sizes.items():
            spot = self.spot(z, y, x, columns)
            rcopy(spot, spot, self.send.at[sem], self.recv.at[sem], "rep", self.p.sibling).wait_send()


SC, S1, S2, SZ, SX, SL, SCATTER_SEMS = 0, 1, 2, 3, 6, 7, 8


def scatter_buffers(rows, size):
    return [(4, 2, 2, rows, size), (4, 2, rows, size), (4, rows, size), (3, rows, size)]


class Scatter:
    def __init__(self, place, part, out, rows, start, size, kind, buffers, send, recv):
        half = part.shape[-1] // 2
        self.p, self.kind, self.send, self.recv, self.out, self.rows, self.size = place, kind, send, recv, out, rows, size
        self.part = part.reshape(4, 2, 2, *part.shape[2:])
        self.one, self.two, self.three, self.four = buffers
        self.mine = pl.ds(pl.multiple_of(place.c * half + start, 128), size)
        self.theirs = pl.ds(pl.multiple_of((1 - place.c) * half + start, 128), size)

    def go(self, src, dst, sem, axis, index):
        rcopy(src, dst, self.send.at[sem], self.recv.at[sem], axis, index).start()

    def came(self, dst, sem):
        rcopy(dst, dst, self.send.at[sem], self.recv.at[sem], "rep", self.p.sibling).wait_recv()

    def core(self):
        self.go(self.part.at[:, :, :, self.rows, self.theirs], self.one, SC, "rep", self.p.sibling)

    def first(self):
        p = self.p
        self.came(self.one, SC)

        @pl.loop(0, 4)
        def _(z):
            self.one[z] = self.one[z] + self.part[z, :, :, self.rows, self.mine]

        if self.kind == "x":
            self.go(self.one.at[:, :, 1 - p.x], self.two, S1, "rep", p.across)
        else:
            self.go(self.one.at[:, 1 - p.y], self.two, S1, "shard", p.beside)

    def second(self):
        p = self.p
        self.came(self.two, S1)
        if self.kind == "x":
            self.two[...] = self.two[...] + self.one[:, :, p.x]
            self.go(self.two.at[:, 1 - p.y], self.three, S2, "shard", p.beside)
        else:
            self.two[...] = self.two[...] + self.one[:, p.y]
            self.go(self.two.at[:, 1 - p.x], self.three, S2, "rep", p.across)

    def third(self):
        p = self.p
        self.came(self.three, S2)
        self.three[...] = self.three[...] + self.two[:, p.y if self.kind == "x" else p.x]
        for dz in (1, 2, 3):
            self.go(self.three.at[p.plane(dz)], self.four.at[3 - dz], SZ + 3 - dz, "shard", p.plane(dz) * 2 + p.y)

    def fourth(self):
        p = self.p
        total = self.three[p.z].astype(F32)
        for dz in range(3):
            self.came(self.four.at[dz], SZ + dz)
            total = total + self.four[dz].astype(F32)
        self.out[p.x, self.rows, self.mine] = total.astype(BF16)
        spot = self.out.at[p.x, self.rows, self.mine]
        self.go(spot, spot, SX, "rep", p.across)

    def fifth(self):
        p = self.p
        self.came(self.out.at[1 - p.x, self.rows, self.mine], SX)
        spot = self.out.at[:, self.rows, self.mine]
        self.go(spot, spot, SL, "rep", p.sibling)

    def last(self):
        self.came(self.out.at[:, self.rows, self.theirs], SL)

    def drain(self):
        columns = slice(0, self.size)
        spots = [(self.one, SC), (self.two, S1), (self.three, S2)] + [(self.four.at[dz], SZ + dz) for dz in range(3)]
        spots += [(self.out.at[0, self.rows, columns], SX), (self.out.at[:, self.rows, columns], SL)]
        for spot, sem in spots:
            rcopy(spot, spot, self.send.at[sem], self.recv.at[sem], "rep", self.p.sibling).wait_send()


def one_hot(perm_ref, h, pt_ref):
    length = pt_ref.shape[0]
    row = perm_ref[pl.ds(h, 1), :].astype(jnp.int16)
    places = lax.broadcasted_iota(jnp.int16, (length, length), 0)
    pt_ref[...] = jnp.where(places == row, jnp.ones((), BF16), jnp.zeros((), BF16))


HG = 4

GATHERED = [("in0", 0, 0, 256, "x"), ("in0", 0, 256, 128, "y"), ("in1", 0, 0, 384, "x"), ("in2", 0, 0, 384, "y"), ("out", 0, 0, 384, "x")]
GATHERED += [("inner", 0, n * 384, 384, "yx"[n % 2]) for n in range(4)]
GATHERED += [("outer", n * 48, 0, 384, "xxyx"[n]) for n in range(4)]
IN0, IN1, IN2, OUT, INNER, OUTER = [0, 1], [2], [3], [4], [5, 6, 7, 8], [9, 10, 11, 12]
AT_START = [(1, 0), (1, 1)]
AHEAD = [(2, 0), (1, 2), (2, 1), (1, 3), (3, 0), (3, 1), (2, 2), (1, 4), (4, 0), (4, 1), (2, 3), (1, 5), (5, 0), (5, 1)]
AT_HEAD = {1: [(3, 2), (3, 3), (2, 4), (2, 5), (1, 6), (1, 7)], 3: [(4, 2), (2, 6), (1, 8)], 4: [(4, 3), (5, 2)], 5: [(3, 4), (3, 5), (2, 7), (2, 8), (1, 9), (1, 10)], 6: [(3, 6)], 7: [(4, 4), (2, 9), (1, 11)], 8: [(4, 5), (3, 7), (2, 10), (1, 12), (5, 3)], 9: [(4, 6), (3, 8), (2, 11)], 10: [(3, 9), (2, 12)]}
AT_FFN = [(5, 4), (5, 5), (5, 6), (4, 7), (5, 7), (4, 8), (5, 8)]
AT_TILE = {0: [(3, 10), (3, 11), (4, 9)], 1: [(4, 10), (3, 12)], 2: [(4, 11), (4, 12)]}
AT_BACK = [(5, 9), (5, 10), (5, 11), (5, 12)]
STAGES = ("", "first", "second", "third", "fourth", "last")


def fwd_kernel(heads, remote, *refs):
    (x_hbm, w_in_hbm, w_out_hbm, w_inner_hbm, w_outer_hbm, vec_ref, seg_ref, ok_ref, qperm_ref, kperm_ref, cot_hbm), refs = refs[:11], refs[11:]
    (hid_hbm, act_hbm, din_hbm, flow_hbm, dou_hbm, dfi_hbm, dbr_hbm, att_hbm, head_hbm, xt_hbm, vgrad_ref), refs = refs[:11], refs[11:]
    if remote:
        (w_in_whole, w_out_whole), refs = refs[:2], refs[2:]
    (xv, cot, w_in, w_out, w_inner, w_outer, qkv, vcol, qcode, kcode, ptq, ptk, att, head, xt), refs = refs[:15], refs[15:]
    (act, gp, flow, fo, nf, inv, dou, dfi, dbr, hid, ds, in_sem, act_sem, out_sem, head_sem, once_sem), refs = refs[:16], refs[16:]
    length, width = xv.shape
    hd = width // heads
    tm, ff = act.shape[1:]
    fc = width
    groups = heads // HG
    gw = HG * hd
    n_tiles = length // tm
    copy = pltpu.make_async_copy

    loads = {"x": copy(x_hbm, xv, in_sem.at[0]), "cot": copy(cot_hbm, cot, in_sem.at[1])}
    pairs = ((w_out_hbm, w_out), (w_inner_hbm, w_inner), (w_outer_hbm, w_outer))
    if remote:
        vslots, send, recv, vsend, vrecv, whole_sem = refs
        p = Place()
        n_shard = lax.axis_size("shard")
        owns = [
            copy(w_in_hbm.at[:, :, pl.ds(q * width + g * gw, gw)], w_in.at[g, p.shard, :, :, pl.ds(q * gw, gw)], in_sem.at[5 + 3 * g + q])
            for g in range(groups)
            for q in range(3)
        ]
        owns += [copy(source, whole.at[p.shard], in_sem.at[2 + n]) for n, (source, whole) in enumerate(pairs)]
        for own in owns:
            own.start()
        for name in ("x", "cot"):
            loads[name].start()
        barrier = pltpu.get_barrier_semaphore()
        for d in range(1, n_shard):
            pl.semaphore_signal(barrier, inc=1, device_id={"shard": (p.shard + d) % n_shard}, device_id_type=pl.DeviceIdType.MESH)
        for other in (p.sibling, p.across):
            pl.semaphore_signal(barrier, inc=1, device_id={"rep": other}, device_id_type=pl.DeviceIdType.MESH)
        wholes = {"in0": w_in.at[0], "in1": w_in.at[1], "in2": w_in.at[2], "out": w_out, "inner": w_inner, "outer": w_outer}
        units = [
            Gather(p, wholes[name], slice(row, row + 48), start, size, kind, send.at[u], recv.at[u])
            for u, (name, row, start, size, kind) in enumerate(GATHERED)
        ]
        shorts = [
            rcopy(vec_ref, vslots.at[n_shard - d], vsend.at[n_shard - d], vrecv.at[n_shard - d], "shard", (p.shard + d) % n_shard)
            for d in range(1, n_shard)
        ]

        def pump(steps):
            for stage, u in steps:
                getattr(units[u], STAGES[stage])()

        for own in owns:
            own.wait()
        pl.semaphore_wait(barrier, n_shard + 1)
        pump(AT_START)
        for short in shorts:
            short.start()
    else:
        owns = [copy(w_in_hbm, w_in, in_sem.at[5])] + [copy(source, whole, in_sem.at[2 + n]) for n, (source, whole) in enumerate(pairs)]
        for own in owns:
            own.start()
        for name in ("x", "cot"):
            loads[name].start()

        def pump(steps):
            pass

    code_rows = lax.broadcasted_iota(jnp.int32, (16, length), 0)
    seg = seg_ref[...]
    ok = ok_ref[...] > 0
    qcode[...] = jnp.where(code_rows == jnp.where(ok, seg, 4), 1.0, 0.0).astype(BF16)
    kcode[...] = jnp.where((code_rows < 5) & (code_rows != jnp.where(ok, seg, 5)), -BIG, 0.0).astype(BF16)
    vgrad_ref[...] = jnp.zeros_like(vgrad_ref)
    loads["x"].wait()
    xt[...] = xv[...].T
    xt_copy = copy(xt, xt_hbm, once_sem.at[0])
    xt_copy.start()
    vec = vec_ref[...].astype(F32)
    if remote:
        for short in shorts:
            short.wait_recv()
        for d in range(1, n_shard):
            vec = vec + vslots[d].astype(F32)
        pump(AHEAD)
    else:
        for own in owns:
            own.wait()
    vcol[...] = vec.T

    def head_copy(h, slot):
        return copy(head.at[slot], head_hbm.at[h], head_sem.at[slot])

    def project(g):
        for q in range(3):
            weight = rows2(w_in[g, :, :, :, q * gw : (q + 1) * gw])
            acc = mm(weight, xt[...], TN)
            bias = vcol[pl.ds(pl.multiple_of(g * gw, gw), gw), :]
            if q == 0:
                acc = (acc + bias[:, 0:1]).astype(BF16) * 0.125
            elif q == 2:
                acc = acc + bias[:, 1:2]
            qkv[q * gw : (q + 1) * gw, :] = acc.astype(BF16)

    def attend(h):
        slot = lax.rem(h, 2)
        r0 = pl.multiple_of(lax.rem(h, HG) * hd, hd)
        rows = pl.ds(pl.multiple_of(h * hd, hd), hd)
        one_hot(qperm_ref, h, ptq)
        one_hot(kperm_ref, h, ptk)
        q_side = jnp.concatenate([qkv[pl.ds(r0, hd), :], qcode[...]], axis=0)
        k_side = jnp.concatenate(
            [qkv[pl.ds(pl.multiple_of(gw + r0, hd), hd), :], kcode[...], qkv[pl.ds(pl.multiple_of(2 * gw + r0, hd), hd), :]], axis=0
        )
        q_arr = mm(q_side, ptq[...], NN).astype(BF16)
        k_arr = mm(k_side, ptk[...], NN).astype(BF16)
        v_arr = k_arr[hd + 16 :, :]

        @pl.when(h >= 2)
        def _():
            head_copy(h - 2, slot).wait()

        head[slot, :hd, :] = q_arr[:hd, :]
        head[slot, hd : 2 * hd, :] = k_arr[:hd, :]
        head[slot, 2 * hd : 3 * hd, :] = v_arr
        cols = [slice(c * CL, (c + 1) * CL) for c in range(length // CL)]
        scores = jnp.concatenate([mm(k_arr[: hd + 16, c], q_arr[:, c], TN) for c in cols], axis=1)
        top = jnp.maximum(jnp.max(scores, axis=0, keepdims=True), -1e29)
        raised = jnp.exp(scores - top)
        total = jnp.maximum(jnp.sum(raised, axis=0, keepdims=True), 1.0)
        probs = (raised * (1.0 / total)).astype(BF16)
        head[slot, 3 * hd :, :] = probs
        head_copy(h, slot).start()
        combined = jnp.concatenate([mm(v_arr[:, c], probs[:, c], NN) for c in cols], axis=1)
        att[rows, :] = mm(combined.astype(BF16), ptq[...], NT).astype(BF16)

    @pl.loop(0, heads)
    def _(h):
        for at in AT_HEAD if remote else ():
            @pl.when(h == at)
            def _():
                pump(AT_HEAD[at])

        @pl.when(lax.rem(h, HG) == 0)
        def _():
            project(h // HG)

        attend(h)

    att_copy = copy(att, att_hbm, once_sem.at[1])
    att_copy.start()
    if remote:
        pump(AT_FFN)
        whole_copies = [copy(w_in, w_in_whole, whole_sem.at[0]), copy(w_out, w_out_whole, whole_sem.at[1])]
        for one in whole_copies:
            one.start()
    b_out, g_first, s_first = vec[2:3, :], vec[3:4, :], vec[4:5, :]
    b_outer, g_second, s_second = vec[5:6, :], vec[6:7, :], vec[7:8, :]

    def add_row(row, value):
        vgrad_ref[row : row + 1, :] += jnp.sum(value, axis=0, keepdims=True)

    def row_copies(i, which):
        rows = pl.ds(pl.multiple_of(i * tm, tm), tm)
        if which == 0:
            return [copy(act.at[i], act_hbm.at[rows, :], act_sem.at[i, 0]), copy(flow.at[i], flow_hbm.at[rows, :], act_sem.at[i, 1])]
        if which == 1:
            return [copy(gp.at[i], din_hbm.at[rows, :], act_sem.at[i, 2])]
        slot = lax.rem(i, 2)
        return [
            copy(s.at[slot], d.at[rows, :], out_sem.at[slot, n])
            for n, (s, d) in enumerate(((dou, dou_hbm), (dfi, dfi_hbm), (dbr, dbr_hbm), (hid, hid_hbm)))
        ]

    @pl.loop(0, n_tiles)
    def _(i):
        for at in AT_TILE if remote else ():
            @pl.when(i == at)
            def _():
                pump(AT_TILE[at])

        rows = pl.ds(pl.multiple_of(i * tm, tm), tm)
        branch = mm(att[:, rows], rows2(w_out[...]), TN)
        normed, inv_first = norm_parts(xv[rows, :].astype(F32) + branch + b_out)
        nf[i] = normed
        inv[i] = inv_first
        first_out = normed * g_first + s_first
        fo[i] = first_out
        flow[i] = first_out.astype(BF16)
        for j in range(ff // fc):
            cols = slice(j * fc, (j + 1) * fc)
            inner = mm(flow[i], rows2(w_inner[:, :, :, cols]), NN) + vec[8 + j : 9 + j, :]
            high, slope = gelu_both(inner)
            act[i, :, cols] = high.astype(BF16)
            gp[i, :, cols] = slope.astype(BF16)
        for one in row_copies(i, 0):
            one.start()

    if remote:
        pump(AT_BACK)
    loads["cot"].wait()
    per = w_outer.shape[0] * fc // ff

    @pl.loop(0, n_tiles)
    def _(i):
        slot = lax.rem(i, 2)
        rows = pl.ds(pl.multiple_of(i * tm, tm), tm)

        @pl.when(i >= 2)
        def _():
            for one in row_copies(i - 2, 2):
                one.wait()

        outer = None
        for j in range(ff // fc):
            term = mm(act[i, :, j * fc : (j + 1) * fc], rows2(w_outer[j * per : (j + 1) * per]), NN)
            outer = term if outer is None else outer + term
        normed_second, inv_second = norm_parts(fo[i] + outer + b_outer)
        hid[slot] = (normed_second * g_second + s_second).astype(BF16)
        grad = cot[rows, :].astype(F32)
        d_second = norm_back(grad, normed_second, inv_second, g_second)
        add_row(6, grad * normed_second)
        add_row(7, grad)
        ds[...] = d_second
        low = d_second.astype(BF16)
        dou[slot] = low
        add_row(5, low.astype(F32))
        back = None
        for j in range(ff // fc):
            cols = slice(j * fc, (j + 1) * fc)
            d_act = mm(dou[slot], rows2(w_outer[j * per : (j + 1) * per]), NT)
            d_inner = (d_act * gp[i, :, cols].astype(F32)).astype(BF16)
            gp[i, :, cols] = d_inner
            add_row(8 + j, d_inner.astype(F32))
            term = mm(d_inner, rows2(w_inner[:, :, :, cols]), NT)
            back = term if back is None else back + term
        for one in row_copies(i, 1):
            one.start()
        d_first_out = ds[...] + back
        normed = nf[i]
        add_row(3, d_first_out * normed)
        add_row(4, d_first_out)
        d_first = norm_back(d_first_out, normed, inv[i], g_first)
        dfi[slot] = d_first
        low = d_first.astype(BF16)
        dbr[slot] = low
        add_row(2, low.astype(F32))
        for one in row_copies(i, 2):
            one.start()

    if remote:
        for unit in units:
            unit.drain()
        for short in shorts:
            short.wait_send()
        for one in whole_copies:
            one.wait()
    for i in range(n_tiles):
        for which in (0, 1, 2) if i >= n_tiles - 2 else (0, 1):
            for one in row_copies(i, which):
                one.wait()
    for h in range(max(0, heads - 2), heads):
        head_copy(h, h % 2).wait()
    xt_copy.wait()
    att_copy.wait()


def fwd_call(remote, x, w_in, w_out, w_inner, w_outer, vec, seg, ok, qperm, kperm, cot):
    length, width = x.shape
    heads = qperm.shape[0]
    hd = width // heads
    ff = w_inner.shape[-1]
    groups = heads // HG
    wholes = [(groups, 8, 2, width // 16, 3 * HG * hd)] + [(8, 2, w.shape[-2], w.shape[-1]) for w in (w_out, w_inner, w_outer)]
    tm = 256
    n_tiles = length // tm
    hbm = pl.BlockSpec(memory_space=pl.ANY)
    vmem = pl.BlockSpec(memory_space=pltpu.VMEM)
    outs = [
        ((length, width), BF16), ((length, ff), BF16), ((length, ff), BF16), ((length, width), BF16), ((length, width), BF16),
        ((length, width), F32), ((length, width), BF16), ((width, length), BF16), ((heads, 3 * hd + CL, length), BF16),
        ((width, length), BF16), ((16, width), F32),
    ]
    if remote:
        outs += [(wholes[0], BF16), (wholes[1], BF16)]
    scratch = [
        ((length, width), BF16), ((length, width), BF16), *[(whole, BF16) for whole in wholes],
        ((3 * HG * hd, length), BF16), ((width, 16), F32), ((16, length), BF16), ((16, length), BF16), ((length, length), BF16), ((length, length), BF16),
        ((width, length), BF16), ((2, 3 * hd + CL, length), BF16), ((width, length), BF16),
        ((n_tiles, tm, ff), BF16), ((n_tiles, tm, ff), BF16), ((n_tiles, tm, width), BF16), ((n_tiles, tm, width), F32), ((n_tiles, tm, width), F32),
        ((n_tiles, tm, 1), F32), ((2, tm, width), BF16), ((2, tm, width), F32), ((2, tm, width), BF16), ((2, tm, width), BF16), ((tm, width), F32),
    ]
    sems = [(5 + 3 * groups,), (n_tiles, 3), (2, 4), (2,), (2,)]
    extra = []
    if remote:
        n_shard, units = lax.axis_size("shard"), len(GATHERED)
        extra = [pltpu.VMEM((n_shard, 16, width), BF16)]
        extra += [pltpu.SemaphoreType.DMA(n) for n in ((units, GATHER_SEMS), (units, GATHER_SEMS), (n_shard,), (n_shard,), (2,))]
    return pl.pallas_call(
        partial(fwd_kernel, heads, remote),
        out_shape=[jax.ShapeDtypeStruct(s, d) for s, d in outs],
        in_specs=[hbm] * 5 + [vmem] * 5 + [hbm],
        out_specs=[hbm] * 10 + [vmem] + [hbm] * (len(outs) - 11),
        scratch_shapes=[pltpu.VMEM(s, d) for s, d in scratch] + [pltpu.SemaphoreType.DMA(n) for n in sems] + extra,
        compiler_params=pltpu.CompilerParams(vmem_limit_bytes=63_400_000, collective_id=0 if remote else None, has_side_effects=remote),
        name="layer_forward",
    )(x, w_in, w_out, w_inner, w_outer, vec, seg, ok, qperm, kperm, cot)


SUMMED = [("outer", n * 48, 0, 384, "xy"[n % 2]) for n in range(4)]
SUMMED += [("inner", 0, n * 384, 384, "xy"[n % 2]) for n in range(4)]
SUMMED += [("out", 0, 0, 384, "x"), ("in0", 0, 0, 384, "y"), ("in1", 0, 0, 384, "x"), ("in2", 0, 0, 256, "x"), ("in2", 0, 256, 128, "y")]
SUM_STAGES = ("core", "first", "second", "third", "fourth", "fifth", "last")
AT_INNER = {0: [(0, 0), (0, 1), (0, 2), (0, 3)], 5: [(1, 0), (1, 1)]}
AT_ATTENDED = [(0, 4), (0, 5), (0, 6), (0, 7)]
AT_BACK_HEAD = {
    0: [(0, 8), (1, 2), (1, 3)],
    1: [(2, 0), (2, 1)],
    2: [(1, 4), (1, 5)],
    3: [(3, 0), (3, 1), (2, 2), (2, 3)],
    4: [(0, 9), (1, 6), (1, 7)],
    5: [(3, 2), (3, 3), (2, 4), (2, 5)],
    6: [(4, 0), (4, 1), (1, 8)],
    7: [(3, 4), (3, 5)],
    8: [(0, 10), (2, 6), (2, 7), (1, 9), (5, 0), (5, 1), (4, 2), (4, 3)],
    9: [(2, 8), (4, 4), (4, 5)],
    10: [(3, 6), (3, 7), (1, 10), (5, 2), (5, 3)],
    11: [(2, 9), (3, 8), (5, 4), (5, 5)],
}
AT_GRAD = {
    0: [(0, 11), (0, 12), (2, 10), (4, 6), (4, 7)],
    1: [(1, 11), (1, 12), (3, 9), (4, 8)],
    2: [(3, 10), (5, 6), (5, 7), (5, 8)],
    3: [(2, 11), (2, 12), (4, 9)],
}
AT_END = [
    (4, 10), (3, 11), (3, 12), (5, 9), (5, 10), (4, 11), (4, 12), (5, 11), (5, 12),
]


def bwd_kernel(heads, remote, *refs):
    (act_hbm, din_hbm, flow_hbm, dou_hbm, dfi_hbm, dbr_hbm, att_hbm, head_hbm, xt_hbm, w_in_hbm, w_out_hbm, qperm_ref, kperm_ref, vg_ref), refs = (
        refs[:14], refs[14:]
    )
    (ig_hbm, vgrad_ref, *grad_outs), refs = refs[:6], refs[6:]
    (act, din, flow, dou, dfi, att, head, xt, w_in, w_out, ptq, ptk, mixed, dproj), refs = refs[:14], refs[14:]
    (g_outer, g_inner, g_out, g_in), refs = refs[:4], refs[4:]
    (ig, in_sem, act_sem, din_sem, head_sem, dfi_sem, ig_sem, out_sem), refs = refs[:8], refs[8:]
    dbr = flow
    length, width = flow.shape
    hd = width // heads
    groups = heads // HG
    gw = HG * hd
    tm = ig.shape[1]
    fc = act.shape[2]
    ic = din.shape[2]
    copy = pltpu.make_async_copy
    n_act = act_hbm.shape[1] // fc
    n_din = din_hbm.shape[1] // ic
    n_tiles = length // tm
    acts = [copy(act_hbm.at[:, j * fc : (j + 1) * fc], act.at[j % 2], act_sem.at[j % 2]) for j in range(n_act)]
    dins = [copy(din_hbm.at[:, j * ic : (j + 1) * ic], din.at[j % 2], din_sem.at[j % 2]) for j in range(n_din)]
    dfis = [copy(dfi_hbm.at[i * tm : (i + 1) * tm, :], dfi.at[i % 2], dfi_sem.at[i % 2]) for i in range(n_tiles)]
    loads = {
        name: copy(s, d, in_sem.at[i])
        for i, (name, s, d) in enumerate(
            (
                ("dou", dou_hbm, dou), ("flow", flow_hbm, flow), ("dbr", dbr_hbm, dbr), ("w_out", w_out_hbm, w_out),
                ("att", att_hbm, att), ("xt", xt_hbm, xt.at[:width, :]), ("w_in", w_in_hbm, w_in),
            )
        )
    }

    def head_copy(h, slot):
        return copy(head_hbm.at[h], head.at[slot], head_sem.at[slot])

    loads["dou"].start()
    acts[0].start()
    acts[1].start()
    loads["flow"].start()
    dins[0].start()
    dins[1].start()
    for name in ("w_out", "att", "xt", "w_in"):
        loads[name].start()
    head_copy(0, 0).start()
    dfis[0].start()
    dfis[1].start()

    if remote:
        sum_outs, (vslots, vsum, vsend, vrecv, send, recv, *buffers) = refs[:4], refs[4:]
        p = Place()
        barrier = pltpu.get_barrier_semaphore()
        for other in (p.sibling, p.across):
            pl.semaphore_signal(barrier, inc=1, device_id={"rep": other}, device_id_type=pl.DeviceIdType.MESH)
        for other in [p.beside] + [p.plane(dz) * 2 + p.y for dz in (1, 2, 3)]:
            pl.semaphore_signal(barrier, inc=1, device_id={"shard": other}, device_id_type=pl.DeviceIdType.MESH)
        parts = {"outer": (g_outer, sum_outs[0]), "inner": (g_inner, sum_outs[1]), "out": (g_out, sum_outs[2])}
        parts.update({"in%d" % g: (g_in.at[g], sum_outs[3].at[g]) for g in range(groups)})
        units = [
            Scatter(p, *parts[name], slice(row, row + 48), start, size, kind, buffers[4 * u : 4 * u + 4], send.at[u], recv.at[u])
            for u, (name, row, start, size, kind) in enumerate(SUMMED)
        ]

        def pump(steps):
            for stage, u in steps:
                getattr(units[u], SUM_STAGES[stage])()
    else:
        def pump(steps):
            pass

    loads["dou"].wait()
    for j in range(n_act):
        acts[j].wait()
        part = mm(act[j % 2], dou[...], TN)
        g_outer[j] = part.astype(BF16).reshape(g_outer.shape[1:])
        if j + 2 < n_act:
            acts[j + 2].start()
    if remote:
        pl.semaphore_wait(barrier, 6)

    loads["flow"].wait()
    mixed[...] = flow[...].T
    loads["dbr"].start()
    for j in range(n_din):
        pump(AT_INNER.get(j, ()))
        dins[j].wait()
        part = mm(mixed[...], din[j % 2], NN)
        g_inner[:, :, :, j * ic : (j + 1) * ic] = part.astype(BF16).reshape(g_inner.shape[:3] + (ic,))
        if j + 2 < n_din:
            dins[j + 2].start()
    pump(AT_ATTENDED)

    for name in ("dbr", "w_out", "att"):
        loads[name].wait()
    mixed[...] = mm(rows2(w_out[...]), dbr[...], NT).astype(BF16)
    g_out[...] = mm(att[...], dbr[...], NN).astype(BF16).reshape(g_out.shape)

    cols = [slice(c * CL, (c + 1) * CL) for c in range(length // CL)]

    def attend(h):
        slot = lax.rem(h, 2)
        one_hot(qperm_ref, h, ptq)
        one_hot(kperm_ref, h, ptk)
        d_arr = mm(mixed[pl.ds(pl.multiple_of(h * hd, hd), hd), :], ptq[...], NN).astype(BF16)
        head_copy(h, slot).wait()

        @pl.when(h + 1 < heads)
        def _():
            head_copy(h + 1, 1 - slot).start()

        q_arr = head[slot, :hd, :]
        k_arr = head[slot, hd : 2 * hd, :]
        v_arr = head[slot, 2 * hd : 3 * hd, :]
        probs = head[slot, 3 * hd :, :]
        d_probs = jnp.concatenate([mm(v_arr[:, c], d_arr[:, c], TN) for c in cols], axis=1)
        wide = probs.astype(F32)
        terms = jnp.sum(wide * d_probs, axis=0, keepdims=True)
        d_scores = (wide * (d_probs - terms)).astype(BF16)
        dq = jnp.concatenate([mm(k_arr[:, c], d_scores[:, c], NN) for c in cols], axis=1) * 0.125
        dk = jnp.concatenate([mm(q_arr[:, c], d_scores[:, c], NT) for c in cols], axis=1)
        dv = jnp.concatenate([mm(d_arr[:, c], probs[:, c], NT) for c in cols], axis=1)
        base = (h // HG) * 3 * gw + lax.rem(h, HG) * hd
        dproj[pl.ds(pl.multiple_of(base, hd), hd), :] = mm(dq.astype(BF16), ptq[...], NT).astype(BF16)
        dkv = mm(jnp.concatenate([dk, dv], axis=0).astype(BF16), ptk[...], NT).astype(BF16)
        dproj[pl.ds(pl.multiple_of(base + gw, hd), hd), :] = dkv[:hd, :]
        dproj[pl.ds(pl.multiple_of(base + 2 * gw, hd), hd), :] = dkv[hd:, :]

    loads["xt"].wait()
    xt[width:, :] = jnp.where(lax.broadcasted_iota(jnp.int32, (16, length), 0) == 0, 1.0, 0.0).astype(BF16)
    vgrad_ref[...] = vg_ref[...]

    @pl.loop(0, heads)
    def _(h):
        for at in AT_BACK_HEAD if remote else ():
            @pl.when(h == at)
            def _():
                pump(AT_BACK_HEAD[at])

        attend(h)

        @pl.when(lax.rem(h, HG) == HG - 1)
        def _():
            g = h // HG
            prod = mm(xt[...], dproj[pl.ds(pl.multiple_of(g * 3 * gw, gw), 3 * gw), :], NT)
            g_in[g] = prod[:width].astype(BF16).reshape(g_in.shape[1:])
            where = pl.ds(pl.multiple_of(g * gw, gw), gw)
            vgrad_ref[0:1, where] = prod[width : width + 1, :gw]
            vgrad_ref[1:2, where] = prod[width : width + 1, 2 * gw :]

    def vector_stage(n, axis, others):
        copies = [rcopy(vsum, vslots.at[n + i], vsend.at[n + i], vrecv.at[n + i], axis, other) for i, other in enumerate(others)]
        for one in copies:
            one.start()

        def wait():
            for one in copies:
                one.wait()
            total = vsum[...]
            for i in range(len(others)):
                total = total + vslots[n + i]
            vsum[...] = total

        return wait

    if not remote:
        outs = [copy(s, d, out_sem.at[i]) for i, (s, d) in enumerate(zip((g_outer, g_inner, g_out, g_in), grad_outs))]
        for out in outs:
            out.start()
    loads["w_in"].wait()
    stores = [copy(ig.at[i % 2], ig_hbm.at[i * tm : (i + 1) * tm, :], ig_sem.at[i % 2]) for i in range(n_tiles)]
    if remote:
        planes = [p.plane(dz) * 2 + p.y for dz in (3, 2, 1)]
        vector_steps = [(0, "rep", [p.sibling]), (1, "rep", [p.across]), (2, "shard", [p.beside]), (3, "shard", planes)]
        vsum[...] = vgrad_ref[...]
    for i in range(n_tiles):
        if remote:
            if i:
                vector_wait()
            pump(AT_GRAD.get(i, ()))
            if i < len(vector_steps):
                vector_wait = vector_stage(*vector_steps[i])
        prod = mm(rows2(w_in[0]), dproj[: 3 * gw, i * tm : (i + 1) * tm], NN)
        for g in range(1, groups):
            prod = prod + mm(rows2(w_in[g]), dproj[g * 3 * gw : (g + 1) * 3 * gw, i * tm : (i + 1) * tm], NN)
        dfis[i].wait()
        if i >= 2:
            stores[i - 2].wait()
        ig[i % 2] = (dfi[i % 2] + prod.T).astype(BF16)
        stores[i].start()
        if i + 2 < n_tiles:
            dfis[i + 2].start()
    if remote:
        for i in range(n_tiles, len(vector_steps)):
            vector_wait()
            vector_wait = vector_stage(*vector_steps[i])
        pump(AT_END)
        vector_wait()
        vgrad_ref[...] = vsum[...]
        for unit in units:
            unit.last()
        outs = [copy(s, d, out_sem.at[i]) for i, (s, d) in enumerate(zip(sum_outs[:3], grad_outs))]
        outs += [
            copy(
                sum_outs[3].at[g, :, :, pl.ds(q * gw, gw)], grad_outs[3].at[:, :, pl.ds(q * width + g * gw, gw)], out_sem.at[3 + 3 * g + q]
            )
            for g in range(groups)
            for q in range(3)
        ]
        for out in outs:
            out.start()
        for unit in units:
            unit.drain()
    for i in range(max(0, n_tiles - 2), n_tiles):
        stores[i].wait()
    for out in outs:
        out.wait()


def bwd_call(remote, act, din, flow, dou, dfi, dbr, att, head, xt, w_in, w_out, qperm, kperm, vgrad):
    length, width = flow.shape
    heads = qperm.shape[0]
    hd = width // heads
    ff = act.shape[1]
    groups = heads // HG
    tm = 256
    hbm = pl.BlockSpec(memory_space=pl.ANY)
    vmem = pl.BlockSpec(memory_space=pltpu.VMEM)
    gshapes = [(8, 2, ff // 16, width), (8, 2, width // 16, ff), (8, 2, width // 16, width), (groups, 8, 2, width // 16, 3 * HG * hd)]
    fc = ff // 8
    if remote:
        finals = [shape[1:] for shape in gshapes[:3]] + [(2, width // 16, 3 * width)]
    else:
        finals = gshapes
    outs = [((length, width), BF16), ((16, width), F32)] + [(shape, BF16) for shape in finals]
    scratch = [
        ((2, length, fc), BF16), ((2, length, fc), BF16), ((length, width), BF16), ((length, width), BF16), ((2, tm, width), F32),
        ((width, length), BF16), ((2,) + head.shape[1:], BF16), ((width + 16, length), BF16), (w_in.shape, BF16), (w_out.shape, BF16),
        ((length, length), BF16), ((length, length), BF16), ((width, length), BF16), ((3 * width, length), BF16),
    ] + [(s, BF16) for s in gshapes] + [((2, tm, width), BF16)]
    sems = [(7,), (2,), (2,), (2,), (2,), (2,), (3 + 3 * groups,)]
    extra = []
    if remote:
        extra += [pltpu.VMEM(s, BF16) for s in [s[1:] for s in gshapes[:3]] + [(groups,) + gshapes[3][2:]]]
        extra += [pltpu.VMEM((6, 16, width), F32), pltpu.VMEM((16, width), F32)]
        extra += [pltpu.SemaphoreType.DMA(n) for n in ((6,), (6,), (len(SUMMED), SCATTER_SEMS), (len(SUMMED), SCATTER_SEMS))]
        for _, _, _, size, _ in SUMMED:
            extra += [pltpu.VMEM(s, BF16) for s in scatter_buffers(width // 16, size)]
    return pl.pallas_call(
        partial(bwd_kernel, heads, remote),
        out_shape=[jax.ShapeDtypeStruct(s, d) for s, d in outs],
        in_specs=[hbm] * 11 + [vmem] * 3,
        out_specs=[hbm, vmem] + [hbm] * 4,
        scratch_shapes=[pltpu.VMEM(s, d) for s, d in scratch] + [pltpu.SemaphoreType.DMA(n) for n in sems] + extra,
        compiler_params=pltpu.CompilerParams(vmem_limit_bytes=63_400_000, collective_id=1 if remote else None, has_side_effects=remote),
        name="layer_backward",
    )(act, din, flow, dou, dfi, dbr, att, head, xt, w_in, w_out, qperm, kperm, vgrad)


def shards(
    layer_input, in_weight, query_bias, value_bias, out_weight, out_bias, first_gain, first_shift, inner_weight, inner_bias,
    outer_weight, outer_bias, second_gain, second_shift, segment_ids, token_valid, query_perm, key_perm, out_cotangent,
):
    _, length, width = layer_input.shape
    heads = query_perm.shape[1]
    ff = inner_weight.shape[1]
    n_shard = lax.axis_size("shard")
    shard = lax.axis_index("shard")

    piece = width // n_shard
    groups = heads // HG
    remote = n_shard == 8 and lax.axis_size("rep") == 4

    def whole(rows):
        return lax.all_gather(rows, "shard", axis=0, tiled=True)

    def blocked(rows):
        return rows.reshape(8, 2, rows.shape[0] // 16, rows.shape[1])

    def halved(rows):
        return rows.reshape(2, rows.shape[0] // 2, rows.shape[1])

    weights = (in_weight, out_weight, inner_weight, outer_weight)
    short = jnp.stack([query_bias, value_bias, out_bias, first_gain, first_shift, outer_bias, second_gain, second_shift])
    inner_piece = ff // n_shard
    if remote:
        w_in, w_out, w_inner, w_outer = [halved(w) for w in weights]
        vec = lax.dynamic_update_slice(jnp.zeros((16, width), BF16), short, (0, shard * piece))
        first = shard * inner_piece
        vec = lax.dynamic_update_slice(vec, inner_bias[None], (8 + first // width, first % width))
    else:
        w_in, w_out, w_inner, w_outer = [whole(w) for w in weights]
        w_in = jnp.transpose(w_in.reshape(width, 3, groups, -1), (2, 0, 1, 3)).reshape(groups, 8, 2, width // 16, -1)
        w_out, w_inner, w_outer = [blocked(w) for w in (w_out, w_inner, w_outer)]
        vectors = lax.all_gather(jnp.concatenate([short.reshape(-1), inner_bias]), "shard", axis=0)
        vec = jnp.concatenate(
            [
                jnp.transpose(vectors[:, : 8 * piece].reshape(n_shard, 8, piece), (1, 0, 2)).reshape(8, width),
                vectors[:, 8 * piece :].reshape(ff // width, width),
                jnp.zeros((8 - ff // width, width), BF16),
            ]
        )
    hidden, act, din, flow, dou, dfi, dbr, att, head, xt, vg, *wholes = fwd_call(
        remote, layer_input[0], w_in, w_out, w_inner, w_outer, vec, segment_ids, token_valid, query_perm[0], key_perm[0], out_cotangent[0]
    )
    if remote:
        w_in, w_out = wholes
    grad_x, vg, g_outer, g_inner, g_out, g_in = bwd_call(
        remote, act, din, flow, dou, dfi, dbr, att, head, xt, w_in, w_out, query_perm[0], key_perm[0], vg
    )
    if not remote:
        g_in = jnp.transpose(g_in.reshape(groups, width, 3, -1), (1, 2, 0, 3))
    grads = [g_in.reshape(-1, 3 * width), g_out.reshape(-1, width), g_inner.reshape(-1, ff), g_outer.reshape(-1, width)]

    def summed(grad):
        rows = lax.psum_scatter(grad.astype(F32), "shard", scatter_dimension=0, tiled=True)
        return lax.psum(rows.astype(BF16), "rep").astype(F32)

    if remote:
        d_in, d_out, d_inner, d_outer = [g.astype(F32) for g in grads]
    else:
        d_in, d_out, d_inner, d_outer = [summed(g) for g in grads]
        vg = lax.psum(vg, ("rep", "shard"))
    mine = lax.dynamic_slice(vg, (0, shard * piece), (8, piece))
    inner_mine = lax.dynamic_slice(vg[8 : 8 + ff // width].reshape(ff), (shard * inner_piece,), (inner_piece,))
    return (
        hidden[None], grad_x[None], d_in, mine[0], mine[1], d_out, mine[2], mine[3], mine[4], d_inner, inner_mine, d_outer,
        mine[5], mine[6], mine[7],
    )


def solution(mesh):
    rows, vector = P("shard", None), P("shard")
    seq2, seq3 = P(("rep", "shard"), None), P(("rep", "shard"), None, None)
    return jax.shard_map(
        shards,
        mesh=mesh,
        in_specs=(
            seq3, rows, vector, vector, rows, vector, vector, vector, rows, vector, rows, vector, vector, vector, seq2, seq2, seq3, seq3, seq3,
        ),
        out_specs=(seq3, seq3, rows, vector, vector, rows, vector, vector, vector, rows, vector, rows, vector, vector, vector),
        check_vma=False,
    )
```

```python
from functools import partial

import jax
import jax.numpy as jnp
from jax import lax
from jax.experimental import pallas as pl
from jax.experimental.pallas import tpu as pltpu
from jax.sharding import PartitionSpec as P

CL = 128
EPS = 1e-06
BIG = 2.0**100
F32 = jnp.float32
BF16 = jnp.bfloat16
NN = (((1,), (0,)), ((), ()))
NT = (((1,), (1,)), ((), ()))
TN = (((0,), (0,)), ((), ()))
TT = (((0,), (1,)), ((), ()))


def mm(a, b, dims):
    return lax.dot_general(a, b, dims, preferred_element_type=F32)


def rows2(value):
    return value.reshape(value.shape[0] * value.shape[1] * value.shape[2], value.shape[3])


def norm_parts(resid):
    average = jnp.mean(resid, axis=-1, keepdims=True)
    centred = resid - average
    variance = jnp.mean(centred * centred, axis=-1, keepdims=True)
    inv_std = lax.rsqrt(variance + EPS)
    return centred * inv_std, inv_std


def norm_back(grad_out, normed, inv_std, gain):
    scaled = grad_out * gain
    first_term = jnp.mean(scaled, axis=-1, keepdims=True)
    second_term = jnp.mean(scaled * normed, axis=-1, keepdims=True)
    return inv_std * (scaled - first_term - normed * second_term)


def gelu_both(z):
    gauss = jnp.exp(-0.5 * (z * z))
    t = 1.0 / (1.0 + (0.3275911 * 0.7071067811865476) * jnp.abs(z))
    poly = t * (0.127414796 + t * (-0.142248368 + t * (0.7107068705 + t * (-0.7265760135 + t * 0.5307027145))))
    tail = poly * gauss
    phi = jnp.where(z >= 0.0, 1.0 - tail, tail)
    return z * phi, phi + z * gauss * 0.3989422804014327


def rcopy(src, dst, send, recv, axis, index):
    return pltpu.make_async_remote_copy(
        src_ref=src, dst_ref=dst, send_sem=send, recv_sem=recv, device_id={axis: index}, device_id_type=pl.DeviceIdType.MESH
    )


class Place:
    def __init__(self):
        rep, shard = lax.axis_index("rep"), lax.axis_index("shard")
        self.x, self.c = rep // 2, rep % 2
        self.z, self.y = shard // 2, shard % 2
        self.rep, self.shard = rep, shard
        self.sibling = self.x * 2 + (1 - self.c)
        self.across = (1 - self.x) * 2 + self.c
        self.beside = self.z * 2 + (1 - self.y)

    def plane(self, dz):
        return (self.z + dz) % 4

    def block(self, dz, dy):
        return self.plane(dz) * 2 + (self.y + dy) % 2


GZ, GX, GA, GB, GC, GD, GATHER_SEMS = 0, 3, 6, 7, 8, 11, 12


class Gather:
    def __init__(self, place, whole, rows, start, size, kind, send, recv):
        half = whole.shape[-1] // 2
        self.p, self.rows, self.size, self.kind, self.send, self.recv = place, rows, size, kind, send, recv
        self.whole = whole.reshape(4, 2, 2, *whole.shape[2:])
        self.mine = pl.ds(pl.multiple_of(place.c * half + start, 128), size)
        self.theirs = pl.ds(pl.multiple_of((1 - place.c) * half + start, 128), size)

    def spot(self, z, y, x, columns=None):
        return self.whole.at[z, y, x, self.rows, self.mine if columns is None else columns]

    def go(self, spot, sem, axis, index):
        rcopy(spot, spot, self.send.at[sem], self.recv.at[sem], axis, index).start()

    def came(self, spot, sem):
        rcopy(spot, spot, self.send.at[sem], self.recv.at[sem], "rep", self.p.sibling).wait_recv()

    def first(self):
        p = self.p
        for dz in (1, 2, 3):
            self.go(self.spot(p.z, p.y, p.x), GZ + 3 - dz, "shard", p.plane(dz) * 2 + p.y)

    def second(self):
        p = self.p
        for dz in (1, 2, 3):
            spot = self.spot(p.plane(dz), p.y, p.x)
            self.came(spot, GZ + dz - 1)
            self.go(spot, GX + dz - 1, "rep", p.across)
        if self.kind == "x":
            self.go(self.spot(slice(None), p.y, p.x), GA, "shard", p.beside)

    def third(self):
        p = self.p
        if self.kind == "x":
            spot = self.spot(slice(None), 1 - p.y, p.x)
            self.came(spot, GA)
            self.go(spot, GB, "rep", p.across)
        for dz in (1, 2, 3):
            self.came(self.spot(p.plane(dz), p.y, 1 - p.x), GX + dz - 1)
        if self.kind == "y":
            self.go(self.spot(slice(None), p.y, slice(None)), GA, "shard", p.beside)
        for dz in (1, 2, 3):
            self.go(self.spot(p.plane(dz), p.y, slice(None)), GC + dz - 1, "rep", p.sibling)

    def fourth(self):
        p = self.p
        if self.kind == "x":
            self.came(self.spot(slice(None), 1 - p.y, 1 - p.x), GB)
        else:
            self.came(self.spot(slice(None), 1 - p.y, slice(None)), GA)
        self.go(self.spot(slice(None), 1 - p.y, slice(None)), GD, "rep", p.sibling)

    def last(self):
        p = self.p
        for dz in (1, 2, 3):
            self.came(self.spot(p.plane(dz), p.y, slice(None), self.theirs), GC + dz - 1)
        self.came(self.spot(slice(None), 1 - p.y, slice(None), self.theirs), GD)

    def drain(self):
        every = slice(None)
        columns = slice(0, self.size)
        one, four, pair, eight = (0, 0, 0), (every, 0, 0), (0, 0, every), (every, 0, every)
        sizes = {GA: four if self.kind == "x" else eight, GB: four, GD: eight}
        for dz in range(3):
            sizes.update({GZ + dz: one, GX + dz: one, GC + dz: pair})
        if self.kind == "y":
            del sizes[GB]
        for sem, (z, y, x) in sizes.items():
            spot = self.spot(z, y, x, columns)
            rcopy(spot, spot, self.send.at[sem], self.recv.at[sem], "rep", self.p.sibling).wait_send()


SC, S1, S2, SZ, SX, SL, SCATTER_SEMS = 0, 1, 2, 3, 6, 7, 8


def scatter_buffers(rows, size):
    return [(4, 2, 2, rows, size), (4, 2, rows, size), (4, rows, size), (3, rows, size)]


class Scatter:
    def __init__(self, place, part, out, rows, start, size, kind, buffers, send, recv):
        half = part.shape[-1] // 2
        self.p, self.kind, self.send, self.recv, self.out, self.rows, self.size = place, kind, send, recv, out, rows, size
        self.part = part.reshape(4, 2, 2, *part.shape[2:])
        self.one, self.two, self.three, self.four = buffers
        self.mine = pl.ds(pl.multiple_of(place.c * half + start, 128), size)
        self.theirs = pl.ds(pl.multiple_of((1 - place.c) * half + start, 128), size)

    def go(self, src, dst, sem, axis, index):
        rcopy(src, dst, self.send.at[sem], self.recv.at[sem], axis, index).start()

    def came(self, dst, sem):
        rcopy(dst, dst, self.send.at[sem], self.recv.at[sem], "rep", self.p.sibling).wait_recv()

    def core(self):
        self.go(self.part.at[:, :, :, self.rows, self.theirs], self.one, SC, "rep", self.p.sibling)

    def first(self):
        p = self.p
        self.came(self.one, SC)

        @pl.loop(0, 4)
        def _(z):
            self.one[z] = self.one[z] + self.part[z, :, :, self.rows, self.mine]

        if self.kind == "x":
            self.go(self.one.at[:, :, 1 - p.x], self.two, S1, "rep", p.across)
        else:
            self.go(self.one.at[:, 1 - p.y], self.two, S1, "shard", p.beside)

    def second(self):
        p = self.p
        self.came(self.two, S1)
        if self.kind == "x":
            self.two[...] = self.two[...] + self.one[:, :, p.x]
            self.go(self.two.at[:, 1 - p.y], self.three, S2, "shard", p.beside)
        else:
            self.two[...] = self.two[...] + self.one[:, p.y]
            self.go(self.two.at[:, 1 - p.x], self.three, S2, "rep", p.across)

    def third(self):
        p = self.p
        self.came(self.three, S2)
        self.three[...] = self.three[...] + self.two[:, p.y if self.kind == "x" else p.x]
        for dz in (1, 2, 3):
            self.go(self.three.at[p.plane(dz)], self.four.at[3 - dz], SZ + 3 - dz, "shard", p.plane(dz) * 2 + p.y)

    def fourth(self):
        p = self.p
        total = self.three[p.z].astype(F32)
        for dz in range(3):
            self.came(self.four.at[dz], SZ + dz)
            total = total + self.four[dz].astype(F32)
        self.out[p.x, self.rows, self.mine] = total.astype(BF16)
        spot = self.out.at[p.x, self.rows, self.mine]
        self.go(spot, spot, SX, "rep", p.across)

    def fifth(self):
        p = self.p
        self.came(self.out.at[1 - p.x, self.rows, self.mine], SX)
        spot = self.out.at[:, self.rows, self.mine]
        self.go(spot, spot, SL, "rep", p.sibling)

    def last(self):
        self.came(self.out.at[:, self.rows, self.theirs], SL)

    def drain(self):
        columns = slice(0, self.size)
        spots = [(self.one, SC), (self.two, S1), (self.three, S2)] + [(self.four.at[dz], SZ + dz) for dz in range(3)]
        spots += [(self.out.at[0, self.rows, columns], SX), (self.out.at[:, self.rows, columns], SL)]
        for spot, sem in spots:
            rcopy(spot, spot, self.send.at[sem], self.recv.at[sem], "rep", self.p.sibling).wait_send()


def one_hot(perm_ref, h, pt_ref):
    length = pt_ref.shape[0]
    row = perm_ref[h].astype(jnp.int16)
    places = lax.broadcasted_iota(jnp.int16, (length, length), 0)
    pt_ref[...] = jnp.where(places == row, jnp.ones((), BF16), jnp.zeros((), BF16))


HG = 4

GATHERED = [("in0", 0, 0, 256, "x"), ("in0", 0, 256, 128, "y"), ("in1", 0, 0, 384, "x"), ("in2", 0, 0, 384, "y"), ("out", 0, 0, 384, "x")]
GATHERED += [("inner", 0, n * 384, 384, "yx"[n % 2]) for n in range(4)]
GATHERED += [("outer", n * 48, 0, 384, "xxyx"[n]) for n in range(4)]
IN0, IN1, IN2, OUT, INNER, OUTER = [0, 1], [2], [3], [4], [5, 6, 7, 8], [9, 10, 11, 12]
AT_START = [(1, 0), (1, 1), (1, 2)]
AHEAD_A = [(2, 0), (1, 3), (2, 1), (1, 4), (2, 2), (1, 5), (3, 0), (3, 1), (2, 3), (1, 6), (3, 2), (2, 4), (1, 7)]
AHEAD_B = [(4, 0), (4, 1), (5, 0), (5, 1)]
AT_HEAD = {0: [(3, 3), (2, 5), (1, 8)], 1: [(4, 2), (2, 6), (3, 4), (2, 7), (1, 9), (1, 10)], 2: [(3, 5)], 3: [(4, 3), (2, 8), (1, 11)], 4: [(4, 4), (3, 6), (2, 9), (1, 12), (5, 2)], 5: [(3, 7), (2, 10), (2, 11)], 6: [(4, 5)], 7: [(4, 6), (3, 8), (2, 12)], 8: [(3, 9), (5, 3)], 11: [(4, 7), (4, 8)]}
AT_FFN = [(3, 10), (3, 11), (5, 4), (5, 5), (5, 6), (5, 7), (5, 8)]
AT_TILE = {1: [(4, 9), (3, 12)], 2: [(4, 10), (4, 11)], 3: [(4, 12)]}
AT_BACK = [(5, 9), (5, 10), (5, 11), (5, 12)]
STAGES = ("", "first", "second", "third", "fourth", "last")


def placed(p, vslots, shorts, width, ff):
    n_shard = len(shorts) + 1
    piece = width // n_shard
    lanes = vslots.shape[2]
    per_row = width // piece
    for short in shorts:
        short.wait_recv()
    slots = [vslots[m] for m in range(n_shard)]
    joined = jnp.concatenate(slots, axis=1)
    shape = (n_shard * lanes, width)
    source = lax.broadcasted_iota(jnp.int32, shape, 0)
    offset = lax.broadcasted_iota(jnp.int32, shape, 1) - source % lanes
    owner = (source // lanes + p.shard) % n_shard
    offset = jnp.where(source % lanes < piece, offset, -1)
    spread = jnp.where(offset == owner * piece, 1.0, 0.0).astype(BF16)
    vec = mm(joined, spread, NN)
    rows = lax.broadcasted_iota(jnp.int32, (16, joined.shape[1]), 0)
    owners = (lax.broadcasted_iota(jnp.int32, (16, joined.shape[1]), 1) // lanes + p.shard) % n_shard
    repeats = ff // width
    result = jnp.where(lax.broadcasted_iota(jnp.int32, vec.shape, 0) < 8, vec, 0.0)
    for r in range(repeats):
        chunk = owners * repeats + r
        left = jnp.where(rows == 8 + chunk // per_row, joined[8 + r : 9 + r, :].astype(F32), 0.0).astype(BF16)
        spread = jnp.where(offset == (owner * repeats + r) % per_row * piece, 1.0, 0.0).astype(BF16)
        result = result + mm(left, spread, NN)
    return result


def fwd_kernel(heads, remote, *refs):
    (x_hbm, w_in_hbm, w_out_hbm, w_inner_hbm, w_outer_hbm, vec_ref, seg_ref, ok_ref, qperm_ref, kperm_ref, cot_hbm), refs = refs[:11], refs[11:]
    (hid_hbm, act_hbm, din_hbm, flow_hbm, dou_hbm, dfi_hbm, dbr_hbm, att_hbm, head_hbm, xt_hbm, vgrad_ref), refs = refs[:11], refs[11:]
    if remote:
        (w_in_whole, w_out_whole), refs = refs[:2], refs[2:]
    (xv, cot, w_in, w_out, w_inner, w_outer, qkv, vcol, qcode, kcode, ptq, ptk, att, head, xt), refs = refs[:15], refs[15:]
    (act, gp, flow, fo, nf, inv, dou, dfi, dbr, hid, ds, in_sem, act_sem, out_sem, head_sem, once_sem), refs = refs[:16], refs[16:]
    length, width = xv.shape
    hd = width // heads
    tm, ff = act.shape[1:]
    fc = width
    groups = heads // HG
    gw = HG * hd
    n_tiles = length // tm
    copy = pltpu.make_async_copy

    loads = {"x": copy(x_hbm, xv, in_sem.at[0]), "cot": copy(cot_hbm, cot, in_sem.at[1])}
    pairs = ((w_out_hbm, w_out), (w_inner_hbm, w_inner), (w_outer_hbm, w_outer))
    if remote:
        vslots, send, recv, vsend, vrecv, whole_sem = refs
        vslots[0] = jnp.zeros(vslots.shape[1:], BF16)
        vslots[0, : vec_ref.shape[0], : vec_ref.shape[1]] = vec_ref[...]
        p = Place()
        n_shard = lax.axis_size("shard")
        owns = [
            copy(w_in_hbm.at[:, :, pl.ds(q * width + g * gw, gw)], w_in.at[g, p.shard, :, :, pl.ds(q * gw, gw)], in_sem.at[5 + 3 * g + q])
            for g in range(groups)
            for q in range(3)
        ]
        owns += [copy(source, whole.at[p.shard], in_sem.at[2 + n]) for n, (source, whole) in enumerate(pairs)]
        for own in owns:
            own.start()
        for name in ("x", "cot"):
            loads[name].start()
        barrier = pltpu.get_barrier_semaphore()
        for d in range(1, n_shard):
            pl.semaphore_signal(barrier, inc=1, device_id={"shard": (p.shard + d) % n_shard}, device_id_type=pl.DeviceIdType.MESH)
        for other in (p.sibling, p.across):
            pl.semaphore_signal(barrier, inc=1, device_id={"rep": other}, device_id_type=pl.DeviceIdType.MESH)
        wholes = {"in0": w_in.at[0], "in1": w_in.at[1], "in2": w_in.at[2], "out": w_out, "inner": w_inner, "outer": w_outer}
        units = [
            Gather(p, wholes[name], slice(row, row + 48), start, size, kind, send.at[u], recv.at[u])
            for u, (name, row, start, size, kind) in enumerate(GATHERED)
        ]
        shorts = [
            rcopy(vslots.at[0], vslots.at[n_shard - d], vsend.at[n_shard - d], vrecv.at[n_shard - d], "shard", (p.shard + d) % n_shard)
            for d in range(1, n_shard)
        ]

        def pump(steps):
            for stage, u in steps:
                getattr(units[u], STAGES[stage])()

        for own in owns:
            own.wait()
        pl.semaphore_wait(barrier, n_shard + 1)
        pump(AT_START)
        for short in shorts:
            short.start()
    else:
        owns = [copy(w_in_hbm, w_in, in_sem.at[5])] + [copy(source, whole, in_sem.at[2 + n]) for n, (source, whole) in enumerate(pairs)]
        for own in owns:
            own.start()
        for name in ("x", "cot"):
            loads[name].start()

        def pump(steps):
            pass

    code_rows = lax.broadcasted_iota(jnp.int32, (16, length), 0)
    seg = seg_ref[...]
    ok = ok_ref[...] > 0
    qcode[...] = jnp.where(code_rows == jnp.where(ok, seg, 4), 1.0, 0.0).astype(BF16)
    kcode[...] = jnp.where((code_rows < 5) & (code_rows != jnp.where(ok, seg, 5)), -BIG, 0.0).astype(BF16)
    vgrad_ref[...] = jnp.zeros_like(vgrad_ref)
    loads["x"].wait()
    xt[...] = xv[...].T
    xt_copy = copy(xt, xt_hbm, once_sem.at[0])
    xt_copy.start()
    if remote:
        pump(AHEAD_A)
        vec = placed(p, vslots, shorts, width, ff)
        pump(AHEAD_B)
    else:
        vec = vec_ref[...].astype(F32)
        for own in owns:
            own.wait()
    vcol[...] = vec.T

    def head_copy(h, slot):
        return copy(head.at[slot], head_hbm.at[h], head_sem.at[slot])

    def project(g):
        for q in range(3):
            weight = rows2(w_in[g, :, :, :, q * gw : (q + 1) * gw])
            acc = mm(weight, xt[...], TN)
            bias = vcol[pl.ds(pl.multiple_of(g * gw, gw), gw), :]
            if q == 0:
                acc = (acc + bias[:, 0:1]).astype(BF16) * 0.125
            elif q == 2:
                acc = acc + bias[:, 1:2]
            qkv[q * gw : (q + 1) * gw, :] = acc.astype(BF16)

    def attend(h):
        slot = lax.rem(h, 2)
        r0 = pl.multiple_of(lax.rem(h, HG) * hd, hd)
        rows = pl.ds(pl.multiple_of(h * hd, hd), hd)
        one_hot(qperm_ref, h, ptq)
        one_hot(kperm_ref, h, ptk)
        q_side = jnp.concatenate([qkv[pl.ds(r0, hd), :], qcode[...]], axis=0)
        k_side = jnp.concatenate(
            [qkv[pl.ds(pl.multiple_of(gw + r0, hd), hd), :], kcode[...], qkv[pl.ds(pl.multiple_of(2 * gw + r0, hd), hd), :]], axis=0
        )
        q_arr = mm(q_side, ptq[...], NN).astype(BF16)
        k_arr = mm(k_side, ptk[...], NN).astype(BF16)
        v_arr = k_arr[hd + 16 :, :]

        @pl.when(h >= 2)
        def _():
            head_copy(h - 2, slot).wait()

        head[slot, :hd, :] = q_arr[:hd, :]
        head[slot, hd : 2 * hd, :] = k_arr[:hd, :]
        head[slot, 2 * hd : 3 * hd, :] = v_arr
        cols = [slice(c * CL, (c + 1) * CL) for c in range(length // CL)]
        scores = jnp.concatenate([mm(k_arr[: hd + 16, c], q_arr[:, c], TN) for c in cols], axis=1)
        top = jnp.maximum(jnp.max(scores, axis=0, keepdims=True), -1e29)
        raised = jnp.exp(scores - top)
        total = jnp.maximum(jnp.sum(raised, axis=0, keepdims=True), 1.0)
        probs = (raised * (1.0 / total)).astype(BF16)
        head[slot, 3 * hd :, :] = probs
        head_copy(h, slot).start()
        combined = jnp.concatenate([mm(v_arr[:, c], probs[:, c], NN) for c in cols], axis=1)
        att[rows, :] = mm(combined.astype(BF16), ptq[...], NT).astype(BF16)

    @pl.loop(0, heads)
    def _(h):
        for at in AT_HEAD if remote else ():
            @pl.when(h == at)
            def _():
                pump(AT_HEAD[at])

        @pl.when(lax.rem(h, HG) == 0)
        def _():
            project(h // HG)

        attend(h)

    att_copy = copy(att, att_hbm, once_sem.at[1])
    att_copy.start()
    if remote:
        pump(AT_FFN)
        whole_copies = [copy(w_in, w_in_whole, whole_sem.at[0]), copy(w_out, w_out_whole, whole_sem.at[1])]
        for one in whole_copies:
            one.start()
    b_out, g_first, s_first = vec[2:3, :], vec[3:4, :], vec[4:5, :]
    b_outer, g_second, s_second = vec[5:6, :], vec[6:7, :], vec[7:8, :]

    def add_row(row, value):
        vgrad_ref[row : row + 1, :] += jnp.sum(value, axis=0, keepdims=True)

    def row_copies(i, which):
        rows = pl.ds(pl.multiple_of(i * tm, tm), tm)
        if which == 0:
            return [copy(act.at[i], act_hbm.at[rows, :], act_sem.at[i, 0]), copy(flow.at[i], flow_hbm.at[rows, :], act_sem.at[i, 1])]
        if which == 1:
            return [copy(gp.at[i], din_hbm.at[rows, :], act_sem.at[i, 2])]
        slot = lax.rem(i, 2)
        return [
            copy(s.at[slot], d.at[rows, :], out_sem.at[slot, n])
            for n, (s, d) in enumerate(((dou, dou_hbm), (dfi, dfi_hbm), (dbr, dbr_hbm), (hid, hid_hbm)))
        ]

    @pl.loop(0, n_tiles)
    def _(i):
        for at in AT_TILE if remote else ():
            @pl.when(i == at)
            def _():
                pump(AT_TILE[at])

        rows = pl.ds(pl.multiple_of(i * tm, tm), tm)
        branch = mm(att[:, rows], rows2(w_out[...]), TN)
        normed, inv_first = norm_parts(xv[rows, :].astype(F32) + branch + b_out)
        nf[i] = normed
        inv[i] = inv_first
        first_out = normed * g_first + s_first
        fo[i] = first_out
        flow[i] = first_out.astype(BF16)
        for j in range(ff // fc):
            cols = slice(j * fc, (j + 1) * fc)
            inner = mm(flow[i], rows2(w_inner[:, :, :, cols]), NN) + vec[8 + j : 9 + j, :]
            high, slope = gelu_both(inner)
            act[i, :, cols] = high.astype(BF16)
            gp[i, :, cols] = slope.astype(BF16)
        for one in row_copies(i, 0):
            one.start()

    if remote:
        pump(AT_BACK)
    loads["cot"].wait()
    per = w_outer.shape[0] * fc // ff

    @pl.loop(0, n_tiles)
    def _(i):
        slot = lax.rem(i, 2)
        rows = pl.ds(pl.multiple_of(i * tm, tm), tm)

        @pl.when(i >= 2)
        def _():
            for one in row_copies(i - 2, 2):
                one.wait()

        outer = None
        for j in range(ff // fc):
            term = mm(act[i, :, j * fc : (j + 1) * fc], rows2(w_outer[j * per : (j + 1) * per]), NN)
            outer = term if outer is None else outer + term
        normed_second, inv_second = norm_parts(fo[i] + outer + b_outer)
        hid[slot] = (normed_second * g_second + s_second).astype(BF16)
        grad = cot[rows, :].astype(F32)
        d_second = norm_back(grad, normed_second, inv_second, g_second)
        add_row(6, grad * normed_second)
        add_row(7, grad)
        ds[...] = d_second
        low = d_second.astype(BF16)
        dou[slot] = low
        add_row(5, low.astype(F32))
        back = None
        for j in range(ff // fc):
            cols = slice(j * fc, (j + 1) * fc)
            d_act = mm(dou[slot], rows2(w_outer[j * per : (j + 1) * per]), NT)
            d_inner = (d_act * gp[i, :, cols].astype(F32)).astype(BF16)
            gp[i, :, cols] = d_inner
            add_row(8 + j, d_inner.astype(F32))
            term = mm(d_inner, rows2(w_inner[:, :, :, cols]), NT)
            back = term if back is None else back + term
        for one in row_copies(i, 1):
            one.start()
        d_first_out = ds[...] + back
        normed = nf[i]
        add_row(3, d_first_out * normed)
        add_row(4, d_first_out)
        d_first = norm_back(d_first_out, normed, inv[i], g_first)
        dfi[slot] = d_first
        low = d_first.astype(BF16)
        dbr[slot] = low
        add_row(2, low.astype(F32))
        for one in row_copies(i, 2):
            one.start()

    if remote:
        for unit in units:
            unit.drain()
        for short in shorts:
            short.wait_send()
        for one in whole_copies:
            one.wait()
    for i in range(n_tiles):
        for which in (0, 1, 2) if i >= n_tiles - 2 else (0, 1):
            for one in row_copies(i, which):
                one.wait()
    for h in range(max(0, heads - 2), heads):
        head_copy(h, h % 2).wait()
    xt_copy.wait()
    att_copy.wait()


def fwd_call(remote, x, w_in, w_out, w_inner, w_outer, vec, seg, ok, qperm, kperm, cot):
    length, width = x.shape
    heads = qperm.shape[0]
    hd = width // heads
    ff = w_inner.shape[-1]
    groups = heads // HG
    wholes = [(groups, 8, 2, width // 16, 3 * HG * hd)] + [(8, 2, w.shape[-2], w.shape[-1]) for w in (w_out, w_inner, w_outer)]
    tm = 256
    n_tiles = length // tm
    hbm = pl.BlockSpec(memory_space=pl.ANY)
    vmem = pl.BlockSpec(memory_space=pltpu.VMEM)
    outs = [
        ((length, width), BF16), ((length, ff), BF16), ((length, ff), BF16), ((length, width), BF16), ((length, width), BF16),
        ((length, width), F32), ((length, width), BF16), ((width, length), BF16), ((heads, 3 * hd + CL, length), BF16),
        ((width, length), BF16), ((16, width), F32),
    ]
    if remote:
        outs += [(wholes[0], BF16), (wholes[1], BF16)]
    scratch = [
        ((length, width), BF16), ((length, width), BF16), *[(whole, BF16) for whole in wholes],
        ((3 * HG * hd, length), BF16), ((width, 16), F32), ((16, length), BF16), ((16, length), BF16), ((length, length), BF16), ((length, length), BF16),
        ((width, length), BF16), ((2, 3 * hd + CL, length), BF16), ((width, length), BF16),
        ((n_tiles, tm, ff), BF16), ((n_tiles, tm, ff), BF16), ((n_tiles, tm, width), BF16), ((n_tiles, tm, width), F32), ((n_tiles, tm, width), F32),
        ((n_tiles, tm, 1), F32), ((2, tm, width), BF16), ((2, tm, width), F32), ((2, tm, width), BF16), ((2, tm, width), BF16), ((tm, width), F32),
    ]
    sems = [(5 + 3 * groups,), (n_tiles, 3), (2, 4), (2,), (2,)]
    extra = []
    if remote:
        n_shard, units = lax.axis_size("shard"), len(GATHERED)
        extra = [pltpu.VMEM((n_shard, 16, 128), BF16)]
        extra += [pltpu.SemaphoreType.DMA(n) for n in ((units, GATHER_SEMS), (units, GATHER_SEMS), (n_shard,), (n_shard,), (2,))]
    return pl.pallas_call(
        partial(fwd_kernel, heads, remote),
        out_shape=[jax.ShapeDtypeStruct(s, d) for s, d in outs],
        in_specs=[hbm] * 5 + [vmem] * 5 + [hbm],
        out_specs=[hbm] * 10 + [vmem] + [hbm] * (len(outs) - 11),
        scratch_shapes=[pltpu.VMEM(s, d) for s, d in scratch] + [pltpu.SemaphoreType.DMA(n) for n in sems] + extra,
        compiler_params=pltpu.CompilerParams(vmem_limit_bytes=63_400_000, collective_id=0 if remote else None, has_side_effects=remote),
        name="layer_forward",
    )(x, w_in, w_out, w_inner, w_outer, vec, seg, ok, qperm, kperm, cot)


SUMMED = [("outer", n * 48, 0, 384, "xy"[n % 2]) for n in range(4)]
SUMMED += [("inner", 0, n * 384, 384, "xy"[n % 2]) for n in range(4)]
SUMMED += [("out", 0, 0, 384, "x"), ("in0", 0, 0, 384, "y"), ("in1", 0, 0, 384, "x"), ("in2", 0, 0, 256, "x"), ("in2", 0, 256, 128, "y")]
SUM_STAGES = ("core", "first", "second", "third", "fourth", "fifth", "last")
AT_INNER = {0: [(0, 0), (0, 1), (0, 2), (0, 3)], 4: [(1, 0), (1, 1)], 5: [(1, 2), (1, 3)]}
AT_ATTENDED = [(0, 4), (0, 5), (0, 6), (0, 7)]
AT_BACK_HEAD = {0: [(0, 8)], 1: [(2, 0), (2, 1), (1, 4), (1, 5)], 2: [(1, 6), (1, 7), (2, 2), (2, 3)], 3: [(3, 0), (3, 1)], 4: [(1, 8), (0, 9)], 5: [(4, 0), (2, 4), (2, 5)], 6: [(4, 1), (1, 9)], 7: [(2, 6), (2, 7)], 8: [(3, 2), (3, 3), (3, 4), (0, 10)], 9: [(5, 0), (2, 8)], 10: [(5, 1), (4, 2), (3, 5), (2, 9), (1, 10)], 11: [(5, 2), (4, 3), (3, 6), (3, 7), (3, 8)]}
AT_GRAD = {0: [(4, 4), (4, 5), (3, 9), (0, 11), (0, 12)], 1: [(4, 6)], 2: [(5, 3), (2, 10), (5, 4), (4, 7), (1, 11), (1, 12)], 3: [(5, 5), (5, 6)]}
AT_END_A = [(5, 7), (4, 8), (3, 10), (4, 9), (2, 11), (2, 12), (5, 8), (5, 9), (4, 10), (3, 12), (3, 11)]
AT_END_B = [(5, 10), (4, 12), (4, 11), (5, 12), (5, 11)]


def bwd_kernel(heads, remote, *refs):
    (act_hbm, din_hbm, flow_hbm, dou_hbm, dfi_hbm, dbr_hbm, att_hbm, head_hbm, xt_hbm, w_in_hbm, w_out_hbm, qperm_ref, kperm_ref, vg_ref), refs = (
        refs[:14], refs[14:]
    )
    (ig_hbm, vgrad_ref, *grad_outs), refs = refs[:6], refs[6:]
    (act, din, flow, dou, dfi, att, head, xt, w_in, w_out, ptq, ptk, mixed, dproj), refs = refs[:14], refs[14:]
    (g_outer, g_inner, g_out, g_in), refs = refs[:4], refs[4:]
    (ig, in_sem, act_sem, din_sem, head_sem, dfi_sem, ig_sem, out_sem), refs = refs[:8], refs[8:]
    dbr = flow
    length, width = flow.shape
    hd = width // heads
    groups = heads // HG
    gw = HG * hd
    tm = ig.shape[1]
    fc = act.shape[2]
    ic = din.shape[2]
    copy = pltpu.make_async_copy
    n_act = act_hbm.shape[1] // fc
    n_din = din_hbm.shape[1] // ic
    n_tiles = length // tm
    acts = [copy(act_hbm.at[:, j * fc : (j + 1) * fc], act.at[j % 2], act_sem.at[j % 2]) for j in range(n_act)]
    dins = [copy(din_hbm.at[:, j * ic : (j + 1) * ic], din.at[j % 2], din_sem.at[j % 2]) for j in range(n_din)]
    dfis = [copy(dfi_hbm.at[i * tm : (i + 1) * tm, :], dfi.at[i % 2], dfi_sem.at[i % 2]) for i in range(n_tiles)]
    loads = {
        name: copy(s, d, in_sem.at[i])
        for i, (name, s, d) in enumerate(
            (
                ("dou", dou_hbm, dou), ("flow", flow_hbm, flow), ("dbr", dbr_hbm, dbr), ("w_out", w_out_hbm, w_out),
                ("att", att_hbm, att), ("xt", xt_hbm, xt.at[:width, :]), ("w_in", w_in_hbm, w_in),
            )
        )
    }

    def head_copy(h, slot):
        return copy(head_hbm.at[h], head.at[slot], head_sem.at[slot])

    loads["dou"].start()
    acts[0].start()
    acts[1].start()
    loads["flow"].start()
    dins[0].start()
    dins[1].start()
    for name in ("w_out", "att", "xt", "w_in"):
        loads[name].start()
    head_copy(0, 0).start()
    dfis[0].start()
    dfis[1].start()

    if remote:
        sum_outs, (vslots, vsum, vsend, vrecv, send, recv, *buffers) = refs[:4], refs[4:]
        p = Place()
        barrier = pltpu.get_barrier_semaphore()
        for other in (p.sibling, p.across):
            pl.semaphore_signal(barrier, inc=1, device_id={"rep": other}, device_id_type=pl.DeviceIdType.MESH)
        for other in [p.beside] + [p.plane(dz) * 2 + p.y for dz in (1, 2, 3)]:
            pl.semaphore_signal(barrier, inc=1, device_id={"shard": other}, device_id_type=pl.DeviceIdType.MESH)
        parts = {"outer": (g_outer, sum_outs[0]), "inner": (g_inner, sum_outs[1]), "out": (g_out, sum_outs[2])}
        parts.update({"in%d" % g: (g_in.at[g], sum_outs[3].at[g]) for g in range(groups)})
        units = [
            Scatter(p, *parts[name], slice(row, row + 48), start, size, kind, buffers[4 * u : 4 * u + 4], send.at[u], recv.at[u])
            for u, (name, row, start, size, kind) in enumerate(SUMMED)
        ]

        def pump(steps):
            for stage, u in steps:
                getattr(units[u], SUM_STAGES[stage])()
    else:
        def pump(steps):
            pass

    loads["dou"].wait()
    for j in range(n_act):
        acts[j].wait()
        part = mm(act[j % 2], dou[...], TN)
        g_outer[j] = part.astype(BF16).reshape(g_outer.shape[1:])
        if j + 2 < n_act:
            acts[j + 2].start()
    if remote:
        pl.semaphore_wait(barrier, 6)

    loads["flow"].wait()
    mixed[...] = flow[...].T
    loads["dbr"].start()
    for j in range(n_din):
        pump(AT_INNER.get(j, ()))
        dins[j].wait()
        part = mm(mixed[...], din[j % 2], NN)
        g_inner[:, :, :, j * ic : (j + 1) * ic] = part.astype(BF16).reshape(g_inner.shape[:3] + (ic,))
        if j + 2 < n_din:
            dins[j + 2].start()
    pump(AT_ATTENDED)

    for name in ("dbr", "w_out", "att"):
        loads[name].wait()
    mixed[...] = mm(rows2(w_out[...]), dbr[...], NT).astype(BF16)
    g_out[...] = mm(att[...], dbr[...], NN).astype(BF16).reshape(g_out.shape)

    cols = [slice(c * CL, (c + 1) * CL) for c in range(length // CL)]

    def attend(h):
        slot = lax.rem(h, 2)
        one_hot(qperm_ref, h, ptq)
        one_hot(kperm_ref, h, ptk)
        d_arr = mm(mixed[pl.ds(pl.multiple_of(h * hd, hd), hd), :], ptq[...], NN).astype(BF16)
        head_copy(h, slot).wait()

        @pl.when(h + 1 < heads)
        def _():
            head_copy(h + 1, 1 - slot).start()

        q_arr = head[slot, :hd, :]
        k_arr = head[slot, hd : 2 * hd, :]
        v_arr = head[slot, 2 * hd : 3 * hd, :]
        probs = head[slot, 3 * hd :, :]
        d_probs = jnp.concatenate([mm(v_arr[:, c], d_arr[:, c], TN) for c in cols], axis=1)
        wide = probs.astype(F32)
        terms = jnp.sum(wide * d_probs, axis=0, keepdims=True)
        d_scores = (wide * (d_probs - terms)).astype(BF16)
        dq = jnp.concatenate([mm(k_arr[:, c], d_scores[:, c], NN) for c in cols], axis=1) * 0.125
        dk = jnp.concatenate([mm(q_arr[:, c], d_scores[:, c], NT) for c in cols], axis=1)
        dv = jnp.concatenate([mm(d_arr[:, c], probs[:, c], NT) for c in cols], axis=1)
        base = (h // HG) * 3 * gw + lax.rem(h, HG) * hd
        dproj[pl.ds(pl.multiple_of(base, hd), hd), :] = mm(dq.astype(BF16), ptq[...], NT).astype(BF16)
        dkv = mm(jnp.concatenate([dk, dv], axis=0).astype(BF16), ptk[...], NT).astype(BF16)
        dproj[pl.ds(pl.multiple_of(base + gw, hd), hd), :] = dkv[:hd, :]
        dproj[pl.ds(pl.multiple_of(base + 2 * gw, hd), hd), :] = dkv[hd:, :]

    loads["xt"].wait()
    xt[width:, :] = jnp.where(lax.broadcasted_iota(jnp.int32, (16, length), 0) == 0, 1.0, 0.0).astype(BF16)
    vgrad_ref[...] = vg_ref[...]

    @pl.loop(0, heads)
    def _(h):
        for at in AT_BACK_HEAD if remote else ():
            @pl.when(h == at)
            def _():
                pump(AT_BACK_HEAD[at])

        attend(h)

        @pl.when(lax.rem(h, HG) == HG - 1)
        def _():
            g = h // HG
            prod = mm(xt[...], dproj[pl.ds(pl.multiple_of(g * 3 * gw, gw), 3 * gw), :], NT)
            g_in[g] = prod[:width].astype(BF16).reshape(g_in.shape[1:])
            where = pl.ds(pl.multiple_of(g * gw, gw), gw)
            vgrad_ref[0:1, where] = prod[width : width + 1, :gw]
            vgrad_ref[1:2, where] = prod[width : width + 1, 2 * gw :]

    def vector_stage(n, axis, others):
        copies = [rcopy(vsum, vslots.at[n + i], vsend.at[n + i], vrecv.at[n + i], axis, other) for i, other in enumerate(others)]
        for one in copies:
            one.start()

        def wait():
            for one in copies:
                one.wait()
            total = vsum[...]
            for i in range(len(others)):
                total = total + vslots[n + i]
            vsum[...] = total

        return wait

    if not remote:
        outs = [copy(s, d, out_sem.at[i]) for i, (s, d) in enumerate(zip((g_outer, g_inner, g_out, g_in), grad_outs))]
        for out in outs:
            out.start()
    loads["w_in"].wait()
    stores = [copy(ig.at[i % 2], ig_hbm.at[i * tm : (i + 1) * tm, :], ig_sem.at[i % 2]) for i in range(n_tiles)]
    if remote:
        planes = [p.plane(dz) * 2 + p.y for dz in (3, 2, 1)]
        vector_steps = [(0, "rep", [p.sibling]), (1, "rep", [p.across]), (2, "shard", [p.beside]), (3, "shard", planes)]
        vsum[...] = vgrad_ref[...]
    for i in range(n_tiles):
        if remote:
            pump(AT_GRAD.get(i, ()))
            if i != 2:
                if i:
                    vector_wait()
                vector_wait = vector_stage(*vector_steps[min(i, 2)])
        prod = mm(rows2(w_in[0]), dproj[: 3 * gw, i * tm : (i + 1) * tm], NN)
        for g in range(1, groups):
            prod = prod + mm(rows2(w_in[g]), dproj[g * 3 * gw : (g + 1) * 3 * gw, i * tm : (i + 1) * tm], NN)
        dfis[i].wait()
        if i >= 2:
            stores[i - 2].wait()
        ig[i % 2] = (dfi[i % 2] + prod.T).astype(BF16)
        stores[i].start()
        if i + 2 < n_tiles:
            dfis[i + 2].start()
    if remote:
        pump(AT_END_A)
        vector_wait()
        vector_wait = vector_stage(*vector_steps[3])
        pump(AT_END_B)
        vector_wait()
        vgrad_ref[...] = vsum[...]
        for unit in units:
            unit.last()
        outs = [copy(s, d, out_sem.at[i]) for i, (s, d) in enumerate(zip(sum_outs[:3], grad_outs))]
        outs += [
            copy(
                sum_outs[3].at[g, :, :, pl.ds(q * gw, gw)], grad_outs[3].at[:, :, pl.ds(q * width + g * gw, gw)], out_sem.at[3 + 3 * g + q]
            )
            for g in range(groups)
            for q in range(3)
        ]
        for out in outs:
            out.start()
        for unit in units:
            unit.drain()
    for i in range(max(0, n_tiles - 2), n_tiles):
        stores[i].wait()
    for out in outs:
        out.wait()


def bwd_call(remote, act, din, flow, dou, dfi, dbr, att, head, xt, w_in, w_out, qperm, kperm, vgrad):
    length, width = flow.shape
    heads = qperm.shape[0]
    hd = width // heads
    ff = act.shape[1]
    groups = heads // HG
    tm = 256
    hbm = pl.BlockSpec(memory_space=pl.ANY)
    vmem = pl.BlockSpec(memory_space=pltpu.VMEM)
    gshapes = [(8, 2, ff // 16, width), (8, 2, width // 16, ff), (8, 2, width // 16, width), (groups, 8, 2, width // 16, 3 * HG * hd)]
    fc = ff // 8
    if remote:
        finals = [shape[1:] for shape in gshapes[:3]] + [(2, width // 16, 3 * width)]
    else:
        finals = gshapes
    outs = [((length, width), BF16), ((16, width), F32)] + [(shape, BF16) for shape in finals]
    scratch = [
        ((2, length, fc), BF16), ((2, length, fc), BF16), ((length, width), BF16), ((length, width), BF16), ((2, tm, width), F32),
        ((width, length), BF16), ((2,) + head.shape[1:], BF16), ((width + 16, length), BF16), (w_in.shape, BF16), (w_out.shape, BF16),
        ((length, length), BF16), ((length, length), BF16), ((width, length), BF16), ((3 * width, length), BF16),
    ] + [(s, BF16) for s in gshapes] + [((2, tm, width), BF16)]
    sems = [(7,), (2,), (2,), (2,), (2,), (2,), (3 + 3 * groups,)]
    extra = []
    if remote:
        extra += [pltpu.VMEM(s, BF16) for s in [s[1:] for s in gshapes[:3]] + [(groups,) + gshapes[3][2:]]]
        extra += [pltpu.VMEM((6, 16, width), F32), pltpu.VMEM((16, width), F32)]
        extra += [pltpu.SemaphoreType.DMA(n) for n in ((6,), (6,), (len(SUMMED), SCATTER_SEMS), (len(SUMMED), SCATTER_SEMS))]
        for _, _, _, size, _ in SUMMED:
            extra += [pltpu.VMEM(s, BF16) for s in scatter_buffers(width // 16, size)]
    return pl.pallas_call(
        partial(bwd_kernel, heads, remote),
        out_shape=[jax.ShapeDtypeStruct(s, d) for s, d in outs],
        in_specs=[hbm] * 11 + [vmem] * 3,
        out_specs=[hbm, vmem] + [hbm] * 4,
        scratch_shapes=[pltpu.VMEM(s, d) for s, d in scratch] + [pltpu.SemaphoreType.DMA(n) for n in sems] + extra,
        compiler_params=pltpu.CompilerParams(vmem_limit_bytes=63_400_000, collective_id=1 if remote else None, has_side_effects=remote),
        name="layer_backward",
    )(act, din, flow, dou, dfi, dbr, att, head, xt, w_in, w_out, qperm, kperm, vgrad)


def shards(
    layer_input, in_weight, query_bias, value_bias, out_weight, out_bias, first_gain, first_shift, inner_weight, inner_bias,
    outer_weight, outer_bias, second_gain, second_shift, segment_ids, token_valid, query_perm, key_perm, out_cotangent,
):
    _, length, width = layer_input.shape
    heads = query_perm.shape[1]
    ff = inner_weight.shape[1]
    n_shard = lax.axis_size("shard")
    shard = lax.axis_index("shard")

    piece = width // n_shard
    groups = heads // HG
    remote = n_shard == 8 and lax.axis_size("rep") == 4

    q_order, k_order = [jnp.transpose(order, (1, 0, 2)) for order in (query_perm, key_perm)]

    def whole(rows):
        return lax.all_gather(rows, "shard", axis=0, tiled=True)

    def blocked(rows):
        return rows.reshape(8, 2, rows.shape[0] // 16, rows.shape[1])

    def halved(rows):
        return rows.reshape(2, rows.shape[0] // 2, rows.shape[1])

    weights = (in_weight, out_weight, inner_weight, outer_weight)
    short = jnp.stack([query_bias, value_bias, out_bias, first_gain, first_shift, outer_bias, second_gain, second_shift])
    if remote:
        w_in, w_out, w_inner, w_outer = [halved(w) for w in weights]
        vec = jnp.concatenate([short, inner_bias.reshape(-1, piece)])
    else:
        w_in, w_out, w_inner, w_outer = [whole(w) for w in weights]
        w_in = jnp.transpose(w_in.reshape(width, 3, groups, -1), (2, 0, 1, 3)).reshape(groups, 8, 2, width // 16, -1)
        w_out, w_inner, w_outer = [blocked(w) for w in (w_out, w_inner, w_outer)]
        vectors = lax.all_gather(jnp.concatenate([short.reshape(-1), inner_bias]), "shard", axis=0)
        vec = jnp.concatenate(
            [
                jnp.transpose(vectors[:, : 8 * piece].reshape(n_shard, 8, piece), (1, 0, 2)).reshape(8, width),
                vectors[:, 8 * piece :].reshape(ff // width, width),
                jnp.zeros((8 - ff // width, width), BF16),
            ]
        )
    hidden, act, din, flow, dou, dfi, dbr, att, head, xt, vg, *wholes = fwd_call(
        remote, layer_input[0], w_in, w_out, w_inner, w_outer, vec, segment_ids, token_valid, q_order, k_order, out_cotangent[0]
    )
    if remote:
        w_in, w_out = wholes
    grad_x, vg, g_outer, g_inner, g_out, g_in = bwd_call(
        remote, act, din, flow, dou, dfi, dbr, att, head, xt, w_in, w_out, q_order, k_order, vg
    )
    if not remote:
        g_in = jnp.transpose(g_in.reshape(groups, width, 3, -1), (1, 2, 0, 3))
    grads = [g_in.reshape(-1, 3 * width), g_out.reshape(-1, width), g_inner.reshape(-1, ff), g_outer.reshape(-1, width)]

    def summed(grad):
        rows = lax.psum_scatter(grad.astype(F32), "shard", scatter_dimension=0, tiled=True)
        return lax.psum(rows.astype(BF16), "rep").astype(F32)

    if remote:
        d_in, d_out, d_inner, d_outer = [g.astype(F32) for g in grads]
    else:
        d_in, d_out, d_inner, d_outer = [summed(g) for g in grads]
        vg = lax.psum(vg, ("rep", "shard"))
    mine = lax.dynamic_slice(vg, (0, shard * piece), (8, piece))
    inner_piece = ff // n_shard
    inner_mine = lax.dynamic_slice(vg[8 : 8 + ff // width].reshape(ff), (shard * inner_piece,), (inner_piece,))
    return (
        hidden[None], grad_x[None], d_in, mine[0], mine[1], d_out, mine[2], mine[3], mine[4], d_inner, inner_mine, d_outer,
        mine[5], mine[6], mine[7],
    )


def solution(mesh):
    rows, vector = P("shard", None), P("shard")
    seq2, seq3 = P(("rep", "shard"), None), P(("rep", "shard"), None, None)
    return jax.shard_map(
        shards,
        mesh=mesh,
        in_specs=(
            seq3, rows, vector, vector, rows, vector, vector, vector, rows, vector, rows, vector, vector, vector, seq2, seq2, seq3, seq3, seq3,
        ),
        out_specs=(seq3, seq3, rows, vector, vector, rows, vector, vector, vector, rows, vector, rows, vector, vector, vector),
        check_vma=False,
    )
```

```python
from functools import partial

import jax
import jax.numpy as jnp
from jax import lax
from jax.experimental import pallas as pl
from jax.experimental.pallas import tpu as pltpu
from jax.sharding import PartitionSpec as P

CL = 128
EPS = 1e-06
BIG = 2.0**100
F32 = jnp.float32
BF16 = jnp.bfloat16
NN = (((1,), (0,)), ((), ()))
NT = (((1,), (1,)), ((), ()))
TN = (((0,), (0,)), ((), ()))
TT = (((0,), (1,)), ((), ()))


def mm(a, b, dims):
    return lax.dot_general(a, b, dims, preferred_element_type=F32)


def rows2(value):
    return value.reshape(value.shape[0] * value.shape[1] * value.shape[2], value.shape[3])


def norm_parts(resid):
    average = jnp.mean(resid, axis=-1, keepdims=True)
    centred = resid - average
    variance = jnp.mean(centred * centred, axis=-1, keepdims=True)
    inv_std = lax.rsqrt(variance + EPS)
    return centred * inv_std, inv_std


def norm_back(grad_out, normed, inv_std, gain):
    scaled = grad_out * gain
    first_term = jnp.mean(scaled, axis=-1, keepdims=True)
    second_term = jnp.mean(scaled * normed, axis=-1, keepdims=True)
    return inv_std * (scaled - first_term - normed * second_term)


def gelu_both(z):
    gauss = jnp.exp(-0.5 * (z * z))
    t = 1.0 / (1.0 + (0.3275911 * 0.7071067811865476) * jnp.abs(z))
    poly = t * (0.127414796 + t * (-0.142248368 + t * (0.7107068705 + t * (-0.7265760135 + t * 0.5307027145))))
    tail = poly * gauss
    phi = jnp.where(z >= 0.0, 1.0 - tail, tail)
    return z * phi, phi + z * gauss * 0.3989422804014327


def rcopy(src, dst, send, recv, axis, index):
    return pltpu.make_async_remote_copy(
        src_ref=src, dst_ref=dst, send_sem=send, recv_sem=recv, device_id={axis: index}, device_id_type=pl.DeviceIdType.MESH
    )


class Place:
    def __init__(self):
        rep, shard = lax.axis_index("rep"), lax.axis_index("shard")
        self.x, self.c = rep // 2, rep % 2
        self.z, self.y = shard // 2, shard % 2
        self.rep, self.shard = rep, shard
        self.sibling = self.x * 2 + (1 - self.c)
        self.across = (1 - self.x) * 2 + self.c
        self.beside = self.z * 2 + (1 - self.y)

    def plane(self, dz):
        return (self.z + dz) % 4

    def block(self, dz, dy):
        return self.plane(dz) * 2 + (self.y + dy) % 2


GZ, GX, GA, GB, GC, GD, GATHER_SEMS = 0, 3, 6, 7, 8, 11, 12


class Gather:
    def __init__(self, place, whole, rows, start, size, kind, send, recv):
        half = whole.shape[-1] // 2
        self.p, self.rows, self.size, self.kind, self.send, self.recv = place, rows, size, kind, send, recv
        self.whole = whole.reshape(4, 2, 2, *whole.shape[2:])
        self.mine = pl.ds(pl.multiple_of(place.c * half + start, 128), size)
        self.theirs = pl.ds(pl.multiple_of((1 - place.c) * half + start, 128), size)

    def spot(self, z, y, x, columns=None):
        return self.whole.at[z, y, x, self.rows, self.mine if columns is None else columns]

    def go(self, spot, sem, axis, index):
        rcopy(spot, spot, self.send.at[sem], self.recv.at[sem], axis, index).start()

    def came(self, spot, sem):
        rcopy(spot, spot, self.send.at[sem], self.recv.at[sem], "rep", self.p.sibling).wait_recv()

    def first(self):
        p = self.p
        for dz in (1, 2, 3):
            self.go(self.spot(p.z, p.y, p.x), GZ + 3 - dz, "shard", p.plane(dz) * 2 + p.y)

    def second(self):
        p = self.p
        for dz in (1, 2, 3):
            spot = self.spot(p.plane(dz), p.y, p.x)
            self.came(spot, GZ + dz - 1)
            self.go(spot, GX + dz - 1, "rep", p.across)
        if self.kind == "x":
            self.go(self.spot(slice(None), p.y, p.x), GA, "shard", p.beside)

    def third(self):
        p = self.p
        if self.kind == "x":
            spot = self.spot(slice(None), 1 - p.y, p.x)
            self.came(spot, GA)
            self.go(spot, GB, "rep", p.across)
        for dz in (1, 2, 3):
            self.came(self.spot(p.plane(dz), p.y, 1 - p.x), GX + dz - 1)
        if self.kind == "y":
            self.go(self.spot(slice(None), p.y, slice(None)), GA, "shard", p.beside)
        for dz in (1, 2, 3):
            self.go(self.spot(p.plane(dz), p.y, slice(None)), GC + dz - 1, "rep", p.sibling)

    def fourth(self):
        p = self.p
        if self.kind == "x":
            self.came(self.spot(slice(None), 1 - p.y, 1 - p.x), GB)
        else:
            self.came(self.spot(slice(None), 1 - p.y, slice(None)), GA)
        self.go(self.spot(slice(None), 1 - p.y, slice(None)), GD, "rep", p.sibling)

    def last(self):
        p = self.p
        for dz in (1, 2, 3):
            self.came(self.spot(p.plane(dz), p.y, slice(None), self.theirs), GC + dz - 1)
        self.came(self.spot(slice(None), 1 - p.y, slice(None), self.theirs), GD)

    def drain(self):
        every = slice(None)
        columns = slice(0, self.size)
        one, four, pair, eight = (0, 0, 0), (every, 0, 0), (0, 0, every), (every, 0, every)
        sizes = {GA: four if self.kind == "x" else eight, GB: four, GD: eight}
        for dz in range(3):
            sizes.update({GZ + dz: one, GX + dz: one, GC + dz: pair})
        if self.kind == "y":
            del sizes[GB]
        for sem, (z, y, x) in sizes.items():
            spot = self.spot(z, y, x, columns)
            rcopy(spot, spot, self.send.at[sem], self.recv.at[sem], "rep", self.p.sibling).wait_send()


SC, S1, S2, SZ, SX, SL, SCATTER_SEMS = 0, 1, 2, 3, 6, 7, 8


def scatter_buffers(rows, size):
    return [(4, 2, 2, rows, size), (4, 2, rows, size), (4, rows, size), (3, rows, size)]


class Scatter:
    def __init__(self, place, part, out, rows, start, size, kind, buffers, send, recv):
        half = part.shape[-1] // 2
        self.p, self.kind, self.send, self.recv, self.out, self.rows, self.size = place, kind, send, recv, out, rows, size
        self.part = part.reshape(4, 2, 2, *part.shape[2:])
        self.one, self.two, self.three, self.four = buffers
        self.mine = pl.ds(pl.multiple_of(place.c * half + start, 128), size)
        self.theirs = pl.ds(pl.multiple_of((1 - place.c) * half + start, 128), size)

    def go(self, src, dst, sem, axis, index):
        rcopy(src, dst, self.send.at[sem], self.recv.at[sem], axis, index).start()

    def came(self, dst, sem):
        rcopy(dst, dst, self.send.at[sem], self.recv.at[sem], "rep", self.p.sibling).wait_recv()

    def core(self):
        self.go(self.part.at[:, :, :, self.rows, self.theirs], self.one, SC, "rep", self.p.sibling)

    def first(self):
        p = self.p
        self.came(self.one, SC)

        @pl.loop(0, 4)
        def _(z):
            self.one[z] = self.one[z] + self.part[z, :, :, self.rows, self.mine]

        if self.kind == "x":
            self.go(self.one.at[:, :, 1 - p.x], self.two, S1, "rep", p.across)
        else:
            self.go(self.one.at[:, 1 - p.y], self.two, S1, "shard", p.beside)

    def second(self):
        p = self.p
        self.came(self.two, S1)
        if self.kind == "x":
            self.two[...] = self.two[...] + self.one[:, :, p.x]
            self.go(self.two.at[:, 1 - p.y], self.three, S2, "shard", p.beside)
        else:
            self.two[...] = self.two[...] + self.one[:, p.y]
            self.go(self.two.at[:, 1 - p.x], self.three, S2, "rep", p.across)

    def third(self):
        p = self.p
        self.came(self.three, S2)
        self.three[...] = self.three[...] + self.two[:, p.y if self.kind == "x" else p.x]
        for dz in (1, 2, 3):
            self.go(self.three.at[p.plane(dz)], self.four.at[3 - dz], SZ + 3 - dz, "shard", p.plane(dz) * 2 + p.y)

    def fourth(self):
        p = self.p
        total = self.three[p.z].astype(F32)
        for dz in range(3):
            self.came(self.four.at[dz], SZ + dz)
            total = total + self.four[dz].astype(F32)
        self.out[p.x, self.rows, self.mine] = total.astype(BF16)
        spot = self.out.at[p.x, self.rows, self.mine]
        self.go(spot, spot, SX, "rep", p.across)

    def fifth(self):
        p = self.p
        self.came(self.out.at[1 - p.x, self.rows, self.mine], SX)
        spot = self.out.at[:, self.rows, self.mine]
        self.go(spot, spot, SL, "rep", p.sibling)

    def last(self):
        self.came(self.out.at[:, self.rows, self.theirs], SL)

    def drain(self):
        columns = slice(0, self.size)
        spots = [(self.one, SC), (self.two, S1), (self.three, S2)] + [(self.four.at[dz], SZ + dz) for dz in range(3)]
        spots += [(self.out.at[0, self.rows, columns], SX), (self.out.at[:, self.rows, columns], SL)]
        for spot, sem in spots:
            rcopy(spot, spot, self.send.at[sem], self.recv.at[sem], "rep", self.p.sibling).wait_send()


def one_hot(perm_ref, h, pt_ref):
    length = pt_ref.shape[0]
    row = perm_ref[h].astype(jnp.int16)
    places = lax.broadcasted_iota(jnp.int16, (length, length), 0)
    pt_ref[...] = jnp.where(places == row, jnp.ones((), BF16), jnp.zeros((), BF16))


HG = 4

GATHERED = [("in0", 0, 0, 256, "x"), ("in0", 0, 256, 128, "y"), ("in1", 0, 0, 384, "x"), ("in2", 0, 0, 384, "y"), ("out", 0, 0, 384, "x")]
GATHERED += [("inner", 0, n * 384, 384, "yx"[n % 2]) for n in range(4)]
GATHERED += [("outer", n * 48, 0, 384, "xxyx"[n]) for n in range(4)]
IN0, IN1, IN2, OUT, INNER, OUTER = [0, 1], [2], [3], [4], [5, 6, 7, 8], [9, 10, 11, 12]
AT_START = [(1, 0), (1, 1), (1, 2)]
AHEAD_A = [(2, 0), (1, 3), (2, 1), (1, 4), (2, 2), (1, 5), (3, 0), (3, 1), (2, 3), (1, 6), (3, 2), (2, 4), (1, 7)]
AHEAD_B = [(4, 0), (4, 1), (5, 0), (5, 1)]
AT_HEAD = {0: [(3, 3), (2, 5), (1, 8)], 1: [(4, 2), (2, 6), (1, 9), (3, 4)], 2: [(2, 7), (3, 5), (1, 10)], 3: [(4, 3), (2, 8), (1, 11)], 4: [(3, 6), (2, 9), (4, 4), (1, 12), (5, 2)], 5: [(3, 7), (2, 10)], 6: [(4, 5), (2, 11)], 7: [(4, 6), (3, 8), (2, 12)], 8: [(5, 3)], 9: [(3, 9)], 11: [(4, 7), (4, 8)]}
AT_FFN = [(5, 4), (5, 5), (5, 6), (5, 7), (5, 8)]
AT_TILE = {0: [(3, 10), (3, 11)], 1: [(4, 9), (3, 12)], 2: [(4, 10)], 3: [(4, 11), (4, 12)]}
AT_BACK = [(5, 9), (5, 10), (5, 11), (5, 12)]
STAGES = ("", "first", "second", "third", "fourth", "last")


def placed(p, vslots, shorts, width, ff):
    n_shard = len(shorts) + 1
    piece = width // n_shard
    lanes = vslots.shape[2]
    per_row = width // piece
    for short in shorts:
        short.wait_recv()
    slots = [vslots[m] for m in range(n_shard)]
    joined = jnp.concatenate(slots, axis=1)
    shape = (n_shard * lanes, width)
    source = lax.broadcasted_iota(jnp.int32, shape, 0)
    offset = lax.broadcasted_iota(jnp.int32, shape, 1) - source % lanes
    owner = (source // lanes + p.shard) % n_shard
    offset = jnp.where(source % lanes < piece, offset, -1)
    spread = jnp.where(offset == owner * piece, 1.0, 0.0).astype(BF16)
    vec = mm(joined, spread, NN)
    rows = lax.broadcasted_iota(jnp.int32, (16, joined.shape[1]), 0)
    owners = (lax.broadcasted_iota(jnp.int32, (16, joined.shape[1]), 1) // lanes + p.shard) % n_shard
    repeats = ff // width
    result = jnp.where(lax.broadcasted_iota(jnp.int32, vec.shape, 0) < 8, vec, 0.0)
    for r in range(repeats):
        chunk = owners * repeats + r
        left = jnp.where(rows == 8 + chunk // per_row, joined[8 + r : 9 + r, :].astype(F32), 0.0).astype(BF16)
        spread = jnp.where(offset == (owner * repeats + r) % per_row * piece, 1.0, 0.0).astype(BF16)
        result = result + mm(left, spread, NN)
    return result


def fwd_kernel(heads, remote, *refs):
    (x_hbm, w_in_hbm, w_out_hbm, w_inner_hbm, w_outer_hbm, vec_ref, seg_ref, ok_ref, qperm_ref, kperm_ref, cot_hbm), refs = refs[:11], refs[11:]
    (hid_hbm, act_hbm, din_hbm, flow_hbm, dou_hbm, dfi_hbm, dbr_hbm, att_hbm, head_hbm, xt_hbm, vgrad_ref), refs = refs[:11], refs[11:]
    if remote:
        (w_in_whole, w_out_whole), refs = refs[:2], refs[2:]
    (xv, cot, w_in, w_out, w_inner, w_outer, qkv, vcol, qcode, kcode, ptq, ptk, att, head, xt), refs = refs[:15], refs[15:]
    (act, gp, flow, fo, nf, inv, dou, dfi, dbr, hid, ds, in_sem, act_sem, out_sem, head_sem, once_sem), refs = refs[:16], refs[16:]
    length, width = xv.shape
    hd = width // heads
    tm, ff = act.shape[1:]
    fc = width
    groups = heads // HG
    gw = HG * hd
    n_tiles = length // tm
    copy = pltpu.make_async_copy

    loads = {"x": copy(x_hbm, xv, in_sem.at[0]), "cot": copy(cot_hbm, cot, in_sem.at[1])}
    pairs = ((w_out_hbm, w_out), (w_inner_hbm, w_inner), (w_outer_hbm, w_outer))
    if remote:
        vslots, send, recv, vsend, vrecv, whole_sem = refs
        vslots[0] = jnp.zeros(vslots.shape[1:], BF16)
        vslots[0, : vec_ref.shape[0], : vec_ref.shape[1]] = vec_ref[...]
        p = Place()
        n_shard = lax.axis_size("shard")
        owns = [
            copy(w_in_hbm.at[:, :, pl.ds(q * width + g * gw, gw)], w_in.at[g, p.shard, :, :, pl.ds(q * gw, gw)], in_sem.at[5 + 3 * g + q])
            for g in range(groups)
            for q in range(3)
        ]
        owns += [copy(source, whole.at[p.shard], in_sem.at[2 + n]) for n, (source, whole) in enumerate(pairs)]
        for own in owns:
            own.start()
        for name in ("x", "cot"):
            loads[name].start()
        barrier = pltpu.get_barrier_semaphore()
        for d in range(1, n_shard):
            pl.semaphore_signal(barrier, inc=1, device_id={"shard": (p.shard + d) % n_shard}, device_id_type=pl.DeviceIdType.MESH)
        for other in (p.sibling, p.across):
            pl.semaphore_signal(barrier, inc=1, device_id={"rep": other}, device_id_type=pl.DeviceIdType.MESH)
        wholes = {"in0": w_in.at[0], "in1": w_in.at[1], "in2": w_in.at[2], "out": w_out, "inner": w_inner, "outer": w_outer}
        units = [
            Gather(p, wholes[name], slice(row, row + 48), start, size, kind, send.at[u], recv.at[u])
            for u, (name, row, start, size, kind) in enumerate(GATHERED)
        ]
        shorts = [
            rcopy(vslots.at[0], vslots.at[n_shard - d], vsend.at[n_shard - d], vrecv.at[n_shard - d], "shard", (p.shard + d) % n_shard)
            for d in range(1, n_shard)
        ]

        def pump(steps):
            for stage, u in steps:
                getattr(units[u], STAGES[stage])()

        for own in owns:
            own.wait()
        pl.semaphore_wait(barrier, n_shard + 1)
        pump(AT_START)
        for short in shorts:
            short.start()
    else:
        owns = [copy(w_in_hbm, w_in, in_sem.at[5])] + [copy(source, whole, in_sem.at[2 + n]) for n, (source, whole) in enumerate(pairs)]
        for own in owns:
            own.start()
        for name in ("x", "cot"):
            loads[name].start()

        def pump(steps):
            pass

    code_rows = lax.broadcasted_iota(jnp.int32, (16, length), 0)
    seg = seg_ref[...]
    ok = ok_ref[...] > 0
    qcode[...] = jnp.where(code_rows == jnp.where(ok, seg, 4), 1.0, 0.0).astype(BF16)
    kcode[...] = jnp.where((code_rows < 5) & (code_rows != jnp.where(ok, seg, 5)), -BIG, 0.0).astype(BF16)
    vgrad_ref[...] = jnp.zeros_like(vgrad_ref)
    loads["x"].wait()
    xt[...] = xv[...].T
    xt_copy = copy(xt, xt_hbm, once_sem.at[0])
    xt_copy.start()
    if remote:
        pump(AHEAD_A)
        vec = placed(p, vslots, shorts, width, ff)
        pump(AHEAD_B)
    else:
        vec = vec_ref[...].astype(F32)
        for own in owns:
            own.wait()
    vcol[...] = vec.T

    def head_copy(h, slot):
        return copy(head.at[slot], head_hbm.at[h], head_sem.at[slot])

    def project(g):
        for q in range(3):
            weight = rows2(w_in[g, :, :, :, q * gw : (q + 1) * gw])
            acc = mm(weight, xt[...], TN)
            bias = vcol[pl.ds(pl.multiple_of(g * gw, gw), gw), :]
            if q == 0:
                acc = (acc + bias[:, 0:1]).astype(BF16) * 0.125
            elif q == 2:
                acc = acc + bias[:, 1:2]
            qkv[q * gw : (q + 1) * gw, :] = acc.astype(BF16)

    def attend(h):
        slot = lax.rem(h, 2)
        r0 = pl.multiple_of(lax.rem(h, HG) * hd, hd)
        rows = pl.ds(pl.multiple_of(h * hd, hd), hd)
        one_hot(qperm_ref, h, ptq)
        one_hot(kperm_ref, h, ptk)
        q_side = jnp.concatenate([qkv[pl.ds(r0, hd), :], qcode[...]], axis=0)
        k_side = jnp.concatenate(
            [qkv[pl.ds(pl.multiple_of(gw + r0, hd), hd), :], kcode[...], qkv[pl.ds(pl.multiple_of(2 * gw + r0, hd), hd), :]], axis=0
        )
        q_arr = mm(q_side, ptq[...], NN).astype(BF16)
        k_arr = mm(k_side, ptk[...], NN).astype(BF16)
        v_arr = k_arr[hd + 16 :, :]

        @pl.when(h >= 2)
        def _():
            head_copy(h - 2, slot).wait()

        head[slot, :hd, :] = q_arr[:hd, :]
        head[slot, hd : 2 * hd, :] = k_arr[:hd, :]
        head[slot, 2 * hd : 3 * hd, :] = v_arr
        cols = [slice(c * CL, (c + 1) * CL) for c in range(length // CL)]
        scores = jnp.concatenate([mm(k_arr[: hd + 16, c], q_arr[:, c], TN) for c in cols], axis=1)
        top = jnp.maximum(jnp.max(scores, axis=0, keepdims=True), -1e29)
        raised = jnp.exp(scores - top)
        total = jnp.maximum(jnp.sum(raised, axis=0, keepdims=True), 1.0)
        probs = (raised * (1.0 / total)).astype(BF16)
        head[slot, 3 * hd :, :] = probs
        head_copy(h, slot).start()
        combined = jnp.concatenate([mm(v_arr[:, c], probs[:, c], NN) for c in cols], axis=1)
        att[rows, :] = mm(combined.astype(BF16), ptq[...], NT).astype(BF16)

    @pl.loop(0, heads)
    def _(h):
        for at in AT_HEAD if remote else ():
            @pl.when(h == at)
            def _():
                pump(AT_HEAD[at])

        @pl.when(lax.rem(h, HG) == 0)
        def _():
            project(h // HG)

        attend(h)

    att_copy = copy(att, att_hbm, once_sem.at[1])
    att_copy.start()
    if remote:
        pump(AT_FFN)
        whole_copies = [copy(w_in, w_in_whole, whole_sem.at[0]), copy(w_out, w_out_whole, whole_sem.at[1])]
        for one in whole_copies:
            one.start()
    b_out, g_first, s_first = vec[2:3, :], vec[3:4, :], vec[4:5, :]
    b_outer, g_second, s_second = vec[5:6, :], vec[6:7, :], vec[7:8, :]

    def add_row(row, value):
        vgrad_ref[row : row + 1, :] += jnp.sum(value, axis=0, keepdims=True)

    def row_copies(i, which):
        rows = pl.ds(pl.multiple_of(i * tm, tm), tm)
        if which == 0:
            return [copy(act.at[i], act_hbm.at[rows, :], act_sem.at[i, 0]), copy(flow.at[i], flow_hbm.at[rows, :], act_sem.at[i, 1])]
        if which == 1:
            return [copy(gp.at[i], din_hbm.at[rows, :], act_sem.at[i, 2])]
        slot = lax.rem(i, 2)
        return [
            copy(s.at[slot], d.at[rows, :], out_sem.at[slot, n])
            for n, (s, d) in enumerate(((dou, dou_hbm), (dfi, dfi_hbm), (dbr, dbr_hbm), (hid, hid_hbm)))
        ]

    @pl.loop(0, n_tiles)
    def _(i):
        for at in AT_TILE if remote else ():
            @pl.when(i == at)
            def _():
                pump(AT_TILE[at])

        rows = pl.ds(pl.multiple_of(i * tm, tm), tm)
        branch = mm(att[:, rows], rows2(w_out[...]), TN)
        normed, inv_first = norm_parts(xv[rows, :].astype(F32) + branch + b_out)
        nf[i] = normed
        inv[i] = inv_first
        first_out = normed * g_first + s_first
        fo[i] = first_out
        flow[i] = first_out.astype(BF16)
        for j in range(ff // fc):
            cols = slice(j * fc, (j + 1) * fc)
            inner = mm(flow[i], rows2(w_inner[:, :, :, cols]), NN) + vec[8 + j : 9 + j, :]
            high, slope = gelu_both(inner)
            act[i, :, cols] = high.astype(BF16)
            gp[i, :, cols] = slope.astype(BF16)
        for one in row_copies(i, 0):
            one.start()

    if remote:
        pump(AT_BACK)
    loads["cot"].wait()
    per = w_outer.shape[0] * fc // ff

    @pl.loop(0, n_tiles)
    def _(i):
        slot = lax.rem(i, 2)
        rows = pl.ds(pl.multiple_of(i * tm, tm), tm)

        @pl.when(i >= 2)
        def _():
            for one in row_copies(i - 2, 2):
                one.wait()

        outer = None
        for j in range(ff // fc):
            term = mm(act[i, :, j * fc : (j + 1) * fc], rows2(w_outer[j * per : (j + 1) * per]), NN)
            outer = term if outer is None else outer + term
        normed_second, inv_second = norm_parts(fo[i] + outer + b_outer)
        hid[slot] = (normed_second * g_second + s_second).astype(BF16)
        grad = cot[rows, :].astype(F32)
        d_second = norm_back(grad, normed_second, inv_second, g_second)
        add_row(6, grad * normed_second)
        add_row(7, grad)
        ds[...] = d_second
        low = d_second.astype(BF16)
        dou[slot] = low
        add_row(5, low.astype(F32))
        back = None
        for j in range(ff // fc):
            cols = slice(j * fc, (j + 1) * fc)
            d_act = mm(dou[slot], rows2(w_outer[j * per : (j + 1) * per]), NT)
            d_inner = (d_act * gp[i, :, cols].astype(F32)).astype(BF16)
            gp[i, :, cols] = d_inner
            add_row(8 + j, d_inner.astype(F32))
            term = mm(d_inner, rows2(w_inner[:, :, :, cols]), NT)
            back = term if back is None else back + term
        for one in row_copies(i, 1):
            one.start()
        d_first_out = ds[...] + back
        normed = nf[i]
        add_row(3, d_first_out * normed)
        add_row(4, d_first_out)
        d_first = norm_back(d_first_out, normed, inv[i], g_first)
        dfi[slot] = d_first
        low = d_first.astype(BF16)
        dbr[slot] = low
        add_row(2, low.astype(F32))
        for one in row_copies(i, 2):
            one.start()

    if remote:
        for unit in units:
            unit.drain()
        for short in shorts:
            short.wait_send()
        for one in whole_copies:
            one.wait()
    for i in range(n_tiles):
        for which in (0, 1, 2) if i >= n_tiles - 2 else (0, 1):
            for one in row_copies(i, which):
                one.wait()
    for h in range(max(0, heads - 2), heads):
        head_copy(h, h % 2).wait()
    xt_copy.wait()
    att_copy.wait()


def fwd_call(remote, x, w_in, w_out, w_inner, w_outer, vec, seg, ok, qperm, kperm, cot):
    length, width = x.shape
    heads = qperm.shape[0]
    hd = width // heads
    ff = w_inner.shape[-1]
    groups = heads // HG
    wholes = [(groups, 8, 2, width // 16, 3 * HG * hd)] + [(8, 2, w.shape[-2], w.shape[-1]) for w in (w_out, w_inner, w_outer)]
    tm = 256
    n_tiles = length // tm
    hbm = pl.BlockSpec(memory_space=pl.ANY)
    vmem = pl.BlockSpec(memory_space=pltpu.VMEM)
    outs = [
        ((length, width), BF16), ((length, ff), BF16), ((length, ff), BF16), ((length, width), BF16), ((length, width), BF16),
        ((length, width), F32), ((length, width), BF16), ((width, length), BF16), ((heads, 3 * hd + CL, length), BF16),
        ((width, length), BF16), ((16, width), F32),
    ]
    if remote:
        outs += [(wholes[0], BF16), (wholes[1], BF16)]
    scratch = [
        ((length, width), BF16), ((length, width), BF16), *[(whole, BF16) for whole in wholes],
        ((3 * HG * hd, length), BF16), ((width, 16), F32), ((16, length), BF16), ((16, length), BF16), ((length, length), BF16), ((length, length), BF16),
        ((width, length), BF16), ((2, 3 * hd + CL, length), BF16), ((width, length), BF16),
        ((n_tiles, tm, ff), BF16), ((n_tiles, tm, ff), BF16), ((n_tiles, tm, width), BF16), ((n_tiles, tm, width), F32), ((n_tiles, tm, width), F32),
        ((n_tiles, tm, 1), F32), ((2, tm, width), BF16), ((2, tm, width), F32), ((2, tm, width), BF16), ((2, tm, width), BF16), ((tm, width), F32),
    ]
    sems = [(5 + 3 * groups,), (n_tiles, 3), (2, 4), (2,), (2,)]
    extra = []
    if remote:
        n_shard, units = lax.axis_size("shard"), len(GATHERED)
        extra = [pltpu.VMEM((n_shard, 16, 128), BF16)]
        extra += [pltpu.SemaphoreType.DMA(n) for n in ((units, GATHER_SEMS), (units, GATHER_SEMS), (n_shard,), (n_shard,), (2,))]
    return pl.pallas_call(
        partial(fwd_kernel, heads, remote),
        out_shape=[jax.ShapeDtypeStruct(s, d) for s, d in outs],
        in_specs=[hbm] * 5 + [vmem] * 5 + [hbm],
        out_specs=[hbm] * 10 + [vmem] + [hbm] * (len(outs) - 11),
        scratch_shapes=[pltpu.VMEM(s, d) for s, d in scratch] + [pltpu.SemaphoreType.DMA(n) for n in sems] + extra,
        compiler_params=pltpu.CompilerParams(vmem_limit_bytes=63_400_000, collective_id=0 if remote else None, has_side_effects=remote),
        name="layer_forward",
    )(x, w_in, w_out, w_inner, w_outer, vec, seg, ok, qperm, kperm, cot)


SUMMED = [("outer", n * 48, 0, 384, "xy"[n % 2]) for n in range(4)]
SUMMED += [("inner", 0, n * 384, 384, "xy"[n % 2]) for n in range(4)]
SUMMED += [("out", 0, 0, 384, "x"), ("in0", 0, 0, 384, "y"), ("in1", 0, 0, 384, "x"), ("in2", 0, 0, 256, "x"), ("in2", 0, 256, 128, "y")]
SUM_STAGES = ("core", "first", "second", "third", "fourth", "fifth", "last")
AT_INNER = {0: [(0, 0), (0, 1), (0, 2), (0, 3)], 4: [(1, 0), (1, 1)], 5: [(1, 2), (1, 3)]}
AT_ATTENDED = [(0, 4), (0, 5), (0, 6), (0, 7)]
AT_BACK_HEAD = {0: [(0, 8)], 1: [(2, 0), (2, 1), (1, 4), (1, 5)], 2: [(1, 6), (1, 7), (2, 2), (2, 3)], 3: [(3, 0), (3, 1)], 4: [(1, 8), (0, 9)], 5: [(4, 0), (2, 4), (2, 5)], 6: [(4, 1), (1, 9)], 7: [(2, 6), (2, 7)], 8: [(3, 2), (3, 3), (3, 4), (0, 10)], 9: [(5, 0), (2, 8)], 10: [(5, 1), (4, 2), (3, 5), (2, 9), (1, 10)], 11: [(5, 2), (4, 3), (3, 6), (3, 7), (3, 8)]}
AT_GRAD = {0: [(4, 4), (4, 5), (3, 9), (0, 11), (0, 12)], 1: [(4, 6)], 2: [(5, 3), (2, 10), (5, 4), (4, 7), (1, 11), (1, 12)], 3: [(5, 5), (5, 6)]}
AT_END_A = [(5, 7), (4, 8), (3, 10), (4, 9), (2, 11), (2, 12), (5, 8), (5, 9), (4, 10), (3, 12), (3, 11)]
AT_END_B = [(5, 10), (4, 12), (4, 11), (5, 12), (5, 11)]


def bwd_kernel(heads, remote, *refs):
    (act_hbm, din_hbm, flow_hbm, dou_hbm, dfi_hbm, dbr_hbm, att_hbm, head_hbm, xt_hbm, w_in_hbm, w_out_hbm, qperm_ref, kperm_ref, vg_ref), refs = (
        refs[:14], refs[14:]
    )
    (ig_hbm, vgrad_ref, *grad_outs), refs = refs[:6], refs[6:]
    (act, din, flow, dou, dfi, att, head, xt, w_in, w_out, ptq, ptk, mixed, dproj), refs = refs[:14], refs[14:]
    (g_outer, g_inner, g_out, g_in), refs = refs[:4], refs[4:]
    (ig, in_sem, act_sem, din_sem, head_sem, dfi_sem, ig_sem, out_sem), refs = refs[:8], refs[8:]
    dbr = flow
    length, width = flow.shape
    hd = width // heads
    groups = heads // HG
    gw = HG * hd
    tm = ig.shape[1]
    fc = act.shape[2]
    ic = din.shape[2]
    copy = pltpu.make_async_copy
    n_act = act_hbm.shape[1] // fc
    n_din = din_hbm.shape[1] // ic
    n_tiles = length // tm
    acts = [copy(act_hbm.at[:, j * fc : (j + 1) * fc], act.at[j % 2], act_sem.at[j % 2]) for j in range(n_act)]
    dins = [copy(din_hbm.at[:, j * ic : (j + 1) * ic], din.at[j % 2], din_sem.at[j % 2]) for j in range(n_din)]
    dfis = [copy(dfi_hbm.at[i * tm : (i + 1) * tm, :], dfi.at[i % 2], dfi_sem.at[i % 2]) for i in range(n_tiles)]
    loads = {
        name: copy(s, d, in_sem.at[i])
        for i, (name, s, d) in enumerate(
            (
                ("dou", dou_hbm, dou), ("flow", flow_hbm, flow), ("dbr", dbr_hbm, dbr), ("w_out", w_out_hbm, w_out),
                ("att", att_hbm, att), ("xt", xt_hbm, xt.at[:width, :]), ("w_in", w_in_hbm, w_in),
            )
        )
    }

    def head_copy(h, slot):
        return copy(head_hbm.at[h], head.at[slot], head_sem.at[slot])

    loads["dou"].start()
    acts[0].start()
    acts[1].start()
    loads["flow"].start()
    dins[0].start()
    dins[1].start()
    for name in ("w_out", "att", "xt", "w_in"):
        loads[name].start()
    head_copy(0, 0).start()
    dfis[0].start()
    dfis[1].start()

    if remote:
        sum_outs, (vslots, vsum, vsend, vrecv, send, recv, *buffers) = refs[:4], refs[4:]
        p = Place()
        barrier = pltpu.get_barrier_semaphore()
        for other in (p.sibling, p.across):
            pl.semaphore_signal(barrier, inc=1, device_id={"rep": other}, device_id_type=pl.DeviceIdType.MESH)
        for other in [p.beside] + [p.plane(dz) * 2 + p.y for dz in (1, 2, 3)]:
            pl.semaphore_signal(barrier, inc=1, device_id={"shard": other}, device_id_type=pl.DeviceIdType.MESH)
        parts = {"outer": (g_outer, sum_outs[0]), "inner": (g_inner, sum_outs[1]), "out": (g_out, sum_outs[2])}
        parts.update({"in%d" % g: (g_in.at[g], sum_outs[3].at[g]) for g in range(groups)})
        units = [
            Scatter(p, *parts[name], slice(row, row + 48), start, size, kind, buffers[4 * u : 4 * u + 4], send.at[u], recv.at[u])
            for u, (name, row, start, size, kind) in enumerate(SUMMED)
        ]

        def pump(steps):
            for stage, u in steps:
                getattr(units[u], SUM_STAGES[stage])()
    else:
        def pump(steps):
            pass

    loads["dou"].wait()
    for j in range(n_act):
        acts[j].wait()
        part = mm(act[j % 2], dou[...], TN)
        g_outer[j] = part.astype(BF16).reshape(g_outer.shape[1:])
        if j + 2 < n_act:
            acts[j + 2].start()
    if remote:
        pl.semaphore_wait(barrier, 6)

    loads["flow"].wait()
    mixed[...] = flow[...].T
    loads["dbr"].start()
    for j in range(n_din):
        pump(AT_INNER.get(j, ()))
        dins[j].wait()
        part = mm(mixed[...], din[j % 2], NN)
        g_inner[:, :, :, j * ic : (j + 1) * ic] = part.astype(BF16).reshape(g_inner.shape[:3] + (ic,))
        if j + 2 < n_din:
            dins[j + 2].start()
    pump(AT_ATTENDED)

    for name in ("dbr", "w_out", "att"):
        loads[name].wait()
    mixed[...] = mm(rows2(w_out[...]), dbr[...], NT).astype(BF16)
    g_out[...] = mm(att[...], dbr[...], NN).astype(BF16).reshape(g_out.shape)

    cols = [slice(c * CL, (c + 1) * CL) for c in range(length // CL)]

    def attend(h):
        slot = lax.rem(h, 2)
        one_hot(qperm_ref, h, ptq)
        one_hot(kperm_ref, h, ptk)
        d_arr = mm(mixed[pl.ds(pl.multiple_of(h * hd, hd), hd), :], ptq[...], NN).astype(BF16)
        head_copy(h, slot).wait()

        @pl.when(h + 1 < heads)
        def _():
            head_copy(h + 1, 1 - slot).start()

        q_arr = head[slot, :hd, :]
        k_arr = head[slot, hd : 2 * hd, :]
        v_arr = head[slot, 2 * hd : 3 * hd, :]
        probs = head[slot, 3 * hd :, :]
        d_probs = jnp.concatenate([mm(v_arr[:, c], d_arr[:, c], TN) for c in cols], axis=1)
        wide = probs.astype(F32)
        terms = jnp.sum(wide * d_probs, axis=0, keepdims=True)
        d_scores = (wide * (d_probs - terms)).astype(BF16)
        dq = jnp.concatenate([mm(k_arr[:, c], d_scores[:, c], NN) for c in cols], axis=1) * 0.125
        dk = jnp.concatenate([mm(q_arr[:, c], d_scores[:, c], NT) for c in cols], axis=1)
        dv = jnp.concatenate([mm(d_arr[:, c], probs[:, c], NT) for c in cols], axis=1)
        base = (h // HG) * 3 * gw + lax.rem(h, HG) * hd
        dproj[pl.ds(pl.multiple_of(base, hd), hd), :] = mm(dq.astype(BF16), ptq[...], NT).astype(BF16)
        dkv = mm(jnp.concatenate([dk, dv], axis=0).astype(BF16), ptk[...], NT).astype(BF16)
        dproj[pl.ds(pl.multiple_of(base + gw, hd), hd), :] = dkv[:hd, :]
        dproj[pl.ds(pl.multiple_of(base + 2 * gw, hd), hd), :] = dkv[hd:, :]

    loads["xt"].wait()
    xt[width:, :] = jnp.where(lax.broadcasted_iota(jnp.int32, (16, length), 0) == 0, 1.0, 0.0).astype(BF16)
    vgrad_ref[...] = vg_ref[...]

    @pl.loop(0, heads)
    def _(h):
        for at in AT_BACK_HEAD if remote else ():
            @pl.when(h == at)
            def _():
                pump(AT_BACK_HEAD[at])

        attend(h)

        @pl.when(lax.rem(h, HG) == HG - 1)
        def _():
            g = h // HG
            prod = mm(xt[...], dproj[pl.ds(pl.multiple_of(g * 3 * gw, gw), 3 * gw), :], NT)
            g_in[g] = prod[:width].astype(BF16).reshape(g_in.shape[1:])
            where = pl.ds(pl.multiple_of(g * gw, gw), gw)
            vgrad_ref[0:1, where] = prod[width : width + 1, :gw]
            vgrad_ref[1:2, where] = prod[width : width + 1, 2 * gw :]

    def vector_stage(n, axis, others):
        copies = [rcopy(vsum, vslots.at[n + i], vsend.at[n + i], vrecv.at[n + i], axis, other) for i, other in enumerate(others)]
        for one in copies:
            one.start()

        def wait():
            for one in copies:
                one.wait()
            total = vsum[...]
            for i in range(len(others)):
                total = total + vslots[n + i]
            vsum[...] = total

        return wait

    if not remote:
        outs = [copy(s, d, out_sem.at[i]) for i, (s, d) in enumerate(zip((g_outer, g_inner, g_out, g_in), grad_outs))]
        for out in outs:
            out.start()
    loads["w_in"].wait()
    stores = [copy(ig.at[i % 2], ig_hbm.at[i * tm : (i + 1) * tm, :], ig_sem.at[i % 2]) for i in range(n_tiles)]
    if remote:
        planes = [p.plane(dz) * 2 + p.y for dz in (3, 2, 1)]
        vector_steps = [(0, "rep", [p.sibling]), (1, "rep", [p.across]), (2, "shard", [p.beside]), (3, "shard", planes)]
        vsum[...] = vgrad_ref[...]
    for i in range(n_tiles):
        if remote:
            pump(AT_GRAD.get(i, ()))
            if i != 2:
                if i:
                    vector_wait()
                vector_wait = vector_stage(*vector_steps[min(i, 2)])
        prod = mm(rows2(w_in[0]), dproj[: 3 * gw, i * tm : (i + 1) * tm], NN)
        for g in range(1, groups):
            prod = prod + mm(rows2(w_in[g]), dproj[g * 3 * gw : (g + 1) * 3 * gw, i * tm : (i + 1) * tm], NN)
        dfis[i].wait()
        if i >= 2:
            stores[i - 2].wait()
        ig[i % 2] = (dfi[i % 2] + prod.T).astype(BF16)
        stores[i].start()
        if i + 2 < n_tiles:
            dfis[i + 2].start()
    if remote:
        pump(AT_END_A)
        vector_wait()
        vector_wait = vector_stage(*vector_steps[3])
        pump(AT_END_B)
        vector_wait()
        vgrad_ref[...] = vsum[...]
        for unit in units:
            unit.last()
        outs = [copy(s, d, out_sem.at[i]) for i, (s, d) in enumerate(zip(sum_outs[:3], grad_outs))]
        outs += [
            copy(
                sum_outs[3].at[g, :, :, pl.ds(q * gw, gw)], grad_outs[3].at[:, :, pl.ds(q * width + g * gw, gw)], out_sem.at[3 + 3 * g + q]
            )
            for g in range(groups)
            for q in range(3)
        ]
        for out in outs:
            out.start()
        for unit in units:
            unit.drain()
    for i in range(max(0, n_tiles - 2), n_tiles):
        stores[i].wait()
    for out in outs:
        out.wait()


def bwd_call(remote, act, din, flow, dou, dfi, dbr, att, head, xt, w_in, w_out, qperm, kperm, vgrad):
    length, width = flow.shape
    heads = qperm.shape[0]
    hd = width // heads
    ff = act.shape[1]
    groups = heads // HG
    tm = 256
    hbm = pl.BlockSpec(memory_space=pl.ANY)
    vmem = pl.BlockSpec(memory_space=pltpu.VMEM)
    gshapes = [(8, 2, ff // 16, width), (8, 2, width // 16, ff), (8, 2, width // 16, width), (groups, 8, 2, width // 16, 3 * HG * hd)]
    fc = ff // 8
    if remote:
        finals = [shape[1:] for shape in gshapes[:3]] + [(2, width // 16, 3 * width)]
    else:
        finals = gshapes
    outs = [((length, width), BF16), ((16, width), F32)] + [(shape, BF16) for shape in finals]
    scratch = [
        ((2, length, fc), BF16), ((2, length, fc), BF16), ((length, width), BF16), ((length, width), BF16), ((2, tm, width), F32),
        ((width, length), BF16), ((2,) + head.shape[1:], BF16), ((width + 16, length), BF16), (w_in.shape, BF16), (w_out.shape, BF16),
        ((length, length), BF16), ((length, length), BF16), ((width, length), BF16), ((3 * width, length), BF16),
    ] + [(s, BF16) for s in gshapes] + [((2, tm, width), BF16)]
    sems = [(7,), (2,), (2,), (2,), (2,), (2,), (3 + 3 * groups,)]
    extra = []
    if remote:
        extra += [pltpu.VMEM(s, BF16) for s in [s[1:] for s in gshapes[:3]] + [(groups,) + gshapes[3][2:]]]
        extra += [pltpu.VMEM((6, 16, width), F32), pltpu.VMEM((16, width), F32)]
        extra += [pltpu.SemaphoreType.DMA(n) for n in ((6,), (6,), (len(SUMMED), SCATTER_SEMS), (len(SUMMED), SCATTER_SEMS))]
        for _, _, _, size, _ in SUMMED:
            extra += [pltpu.VMEM(s, BF16) for s in scatter_buffers(width // 16, size)]
    return pl.pallas_call(
        partial(bwd_kernel, heads, remote),
        out_shape=[jax.ShapeDtypeStruct(s, d) for s, d in outs],
        in_specs=[hbm] * 11 + [vmem] * 3,
        out_specs=[hbm, vmem] + [hbm] * 4,
        scratch_shapes=[pltpu.VMEM(s, d) for s, d in scratch] + [pltpu.SemaphoreType.DMA(n) for n in sems] + extra,
        compiler_params=pltpu.CompilerParams(vmem_limit_bytes=63_400_000, collective_id=1 if remote else None, has_side_effects=remote),
        name="layer_backward",
    )(act, din, flow, dou, dfi, dbr, att, head, xt, w_in, w_out, qperm, kperm, vgrad)


def shards(
    layer_input, in_weight, query_bias, value_bias, out_weight, out_bias, first_gain, first_shift, inner_weight, inner_bias,
    outer_weight, outer_bias, second_gain, second_shift, segment_ids, token_valid, query_perm, key_perm, out_cotangent,
):
    _, length, width = layer_input.shape
    heads = query_perm.shape[1]
    ff = inner_weight.shape[1]
    n_shard = lax.axis_size("shard")
    shard = lax.axis_index("shard")

    piece = width // n_shard
    groups = heads // HG
    remote = n_shard == 8 and lax.axis_size("rep") == 4

    q_order, k_order = [jnp.transpose(order, (1, 0, 2)) for order in (query_perm, key_perm)]

    def whole(rows):
        return lax.all_gather(rows, "shard", axis=0, tiled=True)

    def blocked(rows):
        return rows.reshape(8, 2, rows.shape[0] // 16, rows.shape[1])

    def halved(rows):
        return rows.reshape(2, rows.shape[0] // 2, rows.shape[1])

    weights = (in_weight, out_weight, inner_weight, outer_weight)
    short = jnp.stack([query_bias, value_bias, out_bias, first_gain, first_shift, outer_bias, second_gain, second_shift])
    if remote:
        w_in, w_out, w_inner, w_outer = [halved(w) for w in weights]
        vec = jnp.concatenate([short, inner_bias.reshape(-1, piece)])
    else:
        w_in, w_out, w_inner, w_outer = [whole(w) for w in weights]
        w_in = jnp.transpose(w_in.reshape(width, 3, groups, -1), (2, 0, 1, 3)).reshape(groups, 8, 2, width // 16, -1)
        w_out, w_inner, w_outer = [blocked(w) for w in (w_out, w_inner, w_outer)]
        vectors = lax.all_gather(jnp.concatenate([short.reshape(-1), inner_bias]), "shard", axis=0)
        vec = jnp.concatenate(
            [
                jnp.transpose(vectors[:, : 8 * piece].reshape(n_shard, 8, piece), (1, 0, 2)).reshape(8, width),
                vectors[:, 8 * piece :].reshape(ff // width, width),
                jnp.zeros((8 - ff // width, width), BF16),
            ]
        )
    hidden, act, din, flow, dou, dfi, dbr, att, head, xt, vg, *wholes = fwd_call(
        remote, layer_input[0], w_in, w_out, w_inner, w_outer, vec, segment_ids, token_valid, q_order, k_order, out_cotangent[0]
    )
    if remote:
        w_in, w_out = wholes
    grad_x, vg, g_outer, g_inner, g_out, g_in = bwd_call(
        remote, act, din, flow, dou, dfi, dbr, att, head, xt, w_in, w_out, q_order, k_order, vg
    )
    if not remote:
        g_in = jnp.transpose(g_in.reshape(groups, width, 3, -1), (1, 2, 0, 3))
    grads = [g_in.reshape(-1, 3 * width), g_out.reshape(-1, width), g_inner.reshape(-1, ff), g_outer.reshape(-1, width)]

    def summed(grad):
        rows = lax.psum_scatter(grad.astype(F32), "shard", scatter_dimension=0, tiled=True)
        return lax.psum(rows.astype(BF16), "rep").astype(F32)

    if remote:
        d_in, d_out, d_inner, d_outer = [g.astype(F32) for g in grads]
    else:
        d_in, d_out, d_inner, d_outer = [summed(g) for g in grads]
        vg = lax.psum(vg, ("rep", "shard"))
    mine = lax.dynamic_slice(vg, (0, shard * piece), (8, piece))
    inner_piece = ff // n_shard
    inner_mine = lax.dynamic_slice(vg[8 : 8 + ff // width].reshape(ff), (shard * inner_piece,), (inner_piece,))
    return (
        hidden[None], grad_x[None], d_in, mine[0], mine[1], d_out, mine[2], mine[3], mine[4], d_inner, inner_mine, d_outer,
        mine[5], mine[6], mine[7],
    )


def solution(mesh):
    rows, vector = P("shard", None), P("shard")
    seq2, seq3 = P(("rep", "shard"), None), P(("rep", "shard"), None, None)
    return jax.shard_map(
        shards,
        mesh=mesh,
        in_specs=(
            seq3, rows, vector, vector, rows, vector, vector, vector, rows, vector, rows, vector, vector, vector, seq2, seq2, seq3, seq3, seq3,
        ),
        out_specs=(seq3, seq3, rows, vector, vector, rows, vector, vector, vector, rows, vector, rows, vector, vector, vector),
        check_vma=False,
    )
```
